32 devices in a mesh: dp: 2 (over y), mp: 16 (over z, x, core).
Axes of the slice: x: 2, y: 2, z: 4, core: 2. Of those that a mesh axis runs over, the one named last changes fastest.
Arguments:
- tokens: bfloat16 [32, 1024, 1024], P(('dp', 'mp')), may hold values from -6 to 6
- segment_ids: int32 [32, 1024], P(('dp', 'mp')), may hold values from 0 to 15, never falling along the last dimension, each value on 1 to 128 neighbouring positions
- qkv_weight: bfloat16 [1024, 3072], replicated, may hold values from -0.1875 to 0.1875
- prefix_keys: bfloat16 [64, 1024], replicated, may hold values from -6 to 6
- prefix_values: bfloat16 [64, 1024], replicated, may hold values from -6 to 6
- out_weight: bfloat16 [1024, 1024], replicated, may hold values from -1.5 to 1.5
- out_bias: float32 [1024], replicated, may hold values from -3 to 3
- norm1_gain: float32 [1024], replicated, may hold values from 0.5 to 1.5
- norm1_shift: float32 [1024], replicated, may hold values from -3 to 3
- up_weight: bfloat16 [1024, 4096], P(None, 'mp'), may hold values from -0.1875 to 0.1875
- up_bias: bfloat16 [4096], P('mp'), may hold values from -3 to 3
- down_weight: bfloat16 [4096, 1024], P('mp'), may hold values from -0.09375 to 0.09375
- down_bias: float32 [1024], replicated, may hold values from -3 to 3
- norm2_gain: float32 [1024], replicated, may hold values from 0.5 to 1.5
- norm2_shift: float32 [1024], replicated, may hold values from -3 to 3
- out_grad: bfloat16 [32, 1024, 1024], P(('dp', 'mp')), may hold values from -6 to 6
Outputs:
- layer_out: bfloat16 [32, 1024, 1024], P(('dp', 'mp'))
- tokens_grad: bfloat16 [32, 1024, 1024], P(('dp', 'mp'))
- prefix_keys_grad: float32 [64, 1024], replicated
- prefix_values_grad: float32 [64, 1024], replicated
The draws below stay inside these ranges and needn't reach their ends.
Inputs may be any that keep to these rules, and one draw needn't show every extreme that they name: `segment_ids`: in every row the ids run from 0 to 15 without falling, each sentence 1 to 128 tokens, one of them exactly 128.
All inputs are finite; a program needn't handle non-finite values.
Results may differ from the reference program's by a relative error of at most 0.012.
Values may be sent and summed in bfloat16 or wider, within the bound.
A program may use at most 256 MiB of HBM per device.

```python
import math
import jax
import jax.numpy as jnp
import numpy as np
from jax import lax

D = 1024
HEADS = 16
FF = 4096
HEAD_DIM = 64
SEQ = 1024
PRE = 64
SEGS = 16
SEG_MOST = 128
ROWS = 32


def steps_of(rng, shape, pieces, smallest, largest):
    factor_of = 1.0
    for position, shards_of in pieces:
        steps = jax.random.uniform(jax.random.fold_in(jax.random.fold_in(rng, 6), position), (shards_of,), jnp.float32, smallest / len(pieces), largest / len(pieces))
        factor_of = factor_of * jnp.repeat(jnp.exp(steps), shape[position] // shards_of).reshape((-1,) + (1,) * (len(shape) - 1 - position))
    return factor_of


def profile(amount, total, limit, slope):
    portions = [(1 << 20) // math.isqrt(rank ** slope) + 1 for rank in range(2, amount + 1)]
    surplus, counts = total - limit - (amount - 1), [1] * (amount - 1)
    while surplus > 0:
        free = [i for i in range(amount - 1) if counts[i] < limit]
        mass, left = sum([portions[i] for i in free]), surplus
        for i in free:
            more = min(limit - counts[i], max(1, left * portions[i] // mass), surplus)
            counts[i] = counts[i] + more
            surplus = surplus - more
    return np.array([limit] + counts)


def uneven(rng, count, total, limit, skew):
    if count == 2:
        one = jax.random.randint(rng, (), max(1, total - limit), min(limit, total - 1) + 1)
        return jnp.stack([one, total - one])
    lengths = jnp.asarray(profile(count, total, limit, skew), jnp.int32)
    pairs = (count - 1) // 2
    giver, taker = lengths[1:1 + 2 * pairs:2], lengths[2:2 + 2 * pairs:2]
    margin = jnp.minimum(giver - 1, limit - taker)
    shifted = jax.random.randint(jax.random.fold_in(rng, 1), (pairs,), 0, 1 << 20) % (margin + 1)
    lengths = lengths.at[1:1 + 2 * pairs:2].set(giver - shifted).at[2:2 + 2 * pairs:2].set(taker + shifted)
    return lengths[jax.random.permutation(jax.random.fold_in(rng, 2), count)]


def normal_values(own_key, shape, spread, most, shards=(), held_as=jnp.bfloat16):
    array = jax.random.normal(own_key, shape, jnp.float32) * spread
    if len(shards) > 0:
        array = steps_of(own_key, shape, shards, -0.22, 0.18) * array
    return jnp.clip(array, min=-most, max=most).astype(held_as)


def setup_inputs(seed: int = 0) -> dict:
    key_list = jax.random.split(jax.random.key(seed), 17)
    return {
        "tokens": normal_values(key_list[0], (ROWS, SEQ, D), 1.0, 6.0, ((0, 32),)),
        "segment_ids": jax.vmap(lambda own: jnp.searchsorted(jnp.cumsum(uneven(own, SEGS, SEQ, SEG_MOST, 2)), jnp.arange(SEQ), side="right"))(jax.random.split(key_list[1], ROWS)).reshape((ROWS, SEQ)).astype(jnp.int32),
        "qkv_weight": normal_values(key_list[2], (D, 3 * D), D ** -0.5, 0.1875),
        "prefix_keys": normal_values(key_list[3], (PRE, D), 1.0, 6.0),
        "prefix_values": normal_values(key_list[4], (PRE, D), 1.0, 6.0),
        "out_weight": normal_values(key_list[5], (D, D), (D // 64) ** -0.5, 1.5),
        "out_bias": normal_values(key_list[6], (D,), 0.5, 3.0, (), jnp.float32),
        "norm1_gain": jnp.clip(1.0 + 0.1 * jax.random.normal(key_list[7], (D,), jnp.float32), 0.5, 1.5),
        "norm1_shift": normal_values(key_list[8], (D,), 0.5, 3.0, (), jnp.float32),
        "up_weight": normal_values(key_list[9], (D, FF), D ** -0.5, 0.1875, ((1, 16),)),
        "up_bias": normal_values(key_list[10], (FF,), 0.5, 3.0, ((0, 16),)),
        "down_weight": normal_values(key_list[11], (FF, D), FF ** -0.5, 0.09375, ((0, 16),)),
        "down_bias": normal_values(key_list[12], (D,), 0.5, 3.0, (), jnp.float32),
        "norm2_gain": jnp.clip(1.0 + 0.1 * jax.random.normal(key_list[13], (D,), jnp.float32), 0.5, 1.5),
        "norm2_shift": normal_values(key_list[14], (D,), 0.5, 3.0, (), jnp.float32),
        "out_grad": normal_values(key_list[15], (ROWS, SEQ, D), 1.0, 6.0, ((0, 32),)),
    }


@jax.custom_vjp
def low(v):
    return lax.optimization_barrier(v.astype(jnp.bfloat16)).astype(jnp.float32)

@jax.custom_vjp
def low_back(v):
    return v

def low_keep(v):
    return (low(v), None)

def low_pass(kept, grad):
    return (grad,)

def back_keep(v):
    return (v, None)

def back_low(kept, grad):
    return (low(grad),)
low.defvjp(low_keep, low_pass)
low_back.defvjp(back_keep, back_low)
EPSILON = 1e-05
ROOT_HALF = 0.7071067811865476
MASK_FILL = -1e+30
HIGHEST = lax.Precision.HIGHEST

def gelu_act(values):
    return 0.5 * values * (1.0 + lax.erf(values * ROOT_HALF))

def layer_norm(values, norm_gain, norm_shift):
    average = lax.optimization_barrier(jnp.mean(values, -1, keepdims=True))
    centred = values - average
    variance = lax.optimization_barrier(jnp.mean(centred * centred, -1, keepdims=True))
    return centred * lax.rsqrt(variance + EPSILON) * norm_gain + norm_shift

def row_forward(row_x, row_seg, pre_keys, pre_vals, weights):
    qkv_w, out_w, out_b, gain_one, shift_one, up_w, up_b, down_w, down_b, gain_two, shift_two = weights
    width = row_x.shape[-1]
    scale = 1.0 / math.sqrt(HEAD_DIM)
    joined = low_back(low(jnp.dot(row_x, qkv_w, precision=HIGHEST)))
    queries = joined[:, :width].reshape(SEQ, HEADS, HEAD_DIM)
    keys_all = jnp.concatenate([pre_keys, joined[:, width:2 * width]], axis=0).reshape(PRE + SEQ, HEADS, HEAD_DIM)
    vals_all = jnp.concatenate([pre_vals, joined[:, 2 * width:]], axis=0).reshape(PRE + SEQ, HEADS, HEAD_DIM)
    scores = jnp.einsum('qhd,khd->hqk', queries, keys_all, precision=HIGHEST) * scale
    scores = low_back(scores)
    visible = jnp.concatenate([jnp.ones((SEQ, PRE), bool), row_seg[:, None] == row_seg[None, :]], axis=1)
    scores = jnp.where(visible[None], scores, MASK_FILL)
    highest = lax.optimization_barrier(jnp.max(scores, -1, keepdims=True))
    expo = jnp.exp(scores - highest)
    probs = low(expo / lax.optimization_barrier(jnp.sum(expo, -1, keepdims=True)))
    mixed = jnp.einsum('hqk,khd->qhd', probs, vals_all, precision=HIGHEST).reshape(SEQ, width)
    mixed = low_back(low(mixed))
    attn_branch = low_back(jnp.dot(mixed, out_w, precision=HIGHEST) + out_b)
    first = layer_norm(row_x + attn_branch, gain_one, shift_one)
    first_low = low(first)
    pre_act = low_back(jnp.dot(first_low, up_w, precision=HIGHEST) + up_b)
    hidden = low(gelu_act(pre_act))
    branch = low_back(jnp.dot(hidden, down_w, precision=HIGHEST) + down_b)
    return layer_norm(first + branch, gain_two, shift_two)

def reference(tokens, segment_ids, qkv_weight, prefix_keys, prefix_values, out_weight, out_bias, norm1_gain, norm1_shift, up_weight, up_bias, down_weight, down_bias, norm2_gain, norm2_shift, out_grad):
    weights = tuple((item.astype(jnp.float32) for item in (qkv_weight, out_weight, out_bias, norm1_gain, norm1_shift, up_weight, up_bias, down_weight, down_bias, norm2_gain, norm2_shift)))
    width = tokens.shape[-1]
    pre_keys = prefix_keys.astype(jnp.float32)
    pre_vals = prefix_values.astype(jnp.float32)

    def one_row(carry, items):
        row_x, row_seg, row_dy = items

        def forward(xin, keys_in, vals_in):
            return row_forward(xin, row_seg, keys_in, vals_in, weights)
        result, pullback = jax.vjp(forward, row_x.astype(jnp.float32), pre_keys, pre_vals)
        grad_x, grad_k, grad_v = pullback(row_dy.astype(jnp.float32))
        return ((carry[0] + grad_k, carry[1] + grad_v), (result.astype(jnp.bfloat16), grad_x.astype(jnp.bfloat16)))
    start = (jnp.zeros((PRE, width), jnp.float32), jnp.zeros((PRE, width), jnp.float32))
    (sum_k, sum_v), (outputs, grads) = lax.scan(one_row, start, (tokens, segment_ids, out_grad))
    return (outputs, grads, sum_k, sum_v)
```

```python
import functools

import jax
import jax.numpy as jnp
from jax import lax
from jax.experimental import pallas as pl
from jax.experimental.pallas import tpu as pltpu
from jax.sharding import PartitionSpec as P

EPSILON = 1e-05
ROOT_HALF = 0.7071067811865476
INV_ROOT_TWOPI = 0.3989422804014327
MASK_FILL = -1e30
HEAD_DIM = 64
PAIR = 2 * HEAD_DIM
QB = 128
F32 = jnp.float32
BF16 = jnp.bfloat16
VMEM_LIMIT = 62 * 1024 * 1024


def dot(a, b):
    return lax.dot_general(a, b, (((1,), (0,)), ((), ())), preferred_element_type=F32)


def dot_t(a, b):
    return lax.dot_general(a, b, (((1,), (1,)), ((), ())), preferred_element_type=F32)


def eye(n):
    r = lax.broadcasted_iota(jnp.int32, (n, n), 0)
    c = lax.broadcasted_iota(jnp.int32, (n, n), 1)
    return jnp.where(r == c, 1.0, 0.0).astype(BF16)


def split_heads(x):
    lane = lax.broadcasted_iota(jnp.int32, x.shape, 1)
    zero = jnp.zeros_like(x)
    return jnp.concatenate([jnp.where(lane < HEAD_DIM, x, zero), jnp.where(lane < HEAD_DIM, zero, x)], axis=0)


def own_blocks(x):
    return jnp.concatenate([x[:HEAD_DIM, :QB], x[HEAD_DIM:, QB:]], axis=0)


def normalize(x):
    scale = 1.0 / x.shape[-1]
    cen = x - jnp.sum(x, -1, keepdims=True) * scale
    inv = lax.rsqrt(jnp.sum(cen * cen, -1, keepdims=True) * scale + EPSILON)
    return cen * inv, inv


def norm_back(grad, hat, inv, gain):
    scale = 1.0 / grad.shape[-1]
    sc = grad * gain
    mean1 = jnp.sum(sc, -1, keepdims=True) * scale
    mean2 = jnp.sum(sc * hat, -1, keepdims=True) * scale
    return (sc - mean1 - hat * mean2) * inv


def whole(a):
    return pl.BlockSpec(a.shape, lambda i: (0,) * a.ndim, pipeline_mode=pl.Buffered(1))


def kept(shape, dtype):
    spec = pl.BlockSpec(shape, lambda i: (0,) * len(shape), pipeline_mode=pl.Buffered(1))
    return spec, jax.ShapeDtypeStruct(shape, dtype)


def forward_kernel(tok_ref, wqkv_ref, seg_ref, pk_ref, pv_ref, wo_ref, bo_ref,
                   q_out, k_out, v_out, mix_out, p_out, res_out,
                   vt, pvt, segc, bias, sbuf, mixt):
    qb = pl.program_id(0)
    length, width = tok_ref.shape
    window = bias.shape[0]
    pairs = width // PAIR

    @pl.when(qb == 0)
    def _():
        tile = 256
        for part, ref in enumerate((q_out, k_out, v_out)):
            for j in range(width // tile):
                x = dot(tok_ref[...], wqkv_ref[:, part * width + j * tile:part * width + (j + 1) * tile]).astype(BF16)
                if part == 0:
                    x = x * jnp.asarray(HEAD_DIM ** -0.5, BF16)
                ref[:, j * tile:(j + 1) * tile] = x
        big = eye(256)
        for j in range(width // 256):
            cols = slice(j * 256, (j + 1) * 256)
            vt[cols, :] = dot_t(big, v_out[:, cols]).astype(BF16)
            pvt[cols, :] = dot_t(big, pv_ref[:, cols]).astype(BF16)
        ident = eye(QB)
        seg = jnp.broadcast_to(seg_ref[...].astype(F32), (QB, length)).astype(BF16)
        for j in range(length // QB):
            segc[j * QB:(j + 1) * QB, :] = dot_t(ident, seg[:, j * QB:(j + 1) * QB])

    start = pl.multiple_of(jnp.clip(qb * QB - QB, 0, length - window), QB)
    win = pl.ds(start, window)
    rows = pl.ds(pl.multiple_of(qb * QB, QB), QB)
    segq = seg_ref[:, rows].astype(F32)
    bias[...] = jnp.where(segc[win, :] == segq, 0.0, MASK_FILL)

    def score(pair):
        cols = slice(pair * PAIR, (pair + 1) * PAIR)
        keys = jnp.concatenate([k_out[win, cols], pk_ref[:, cols]], axis=0)
        sbuf[pair % 2] = dot_t(keys, split_heads(q_out[rows, cols]))

    def soft(pair):
        both = jnp.concatenate([bias[...], bias[...]], axis=1)
        sw = sbuf[pair % 2, :window] + both
        sp = sbuf[pair % 2, window:]
        top = jnp.maximum(jnp.max(sw, 0, keepdims=True), jnp.max(sp, 0, keepdims=True))
        ew = jnp.exp(sw - top)
        ep = jnp.exp(sp - top)
        inv = 1.0 / (jnp.sum(ew, 0, keepdims=True) + jnp.sum(ep, 0, keepdims=True))
        p_out[0, pair, :window] = (ew * inv).astype(BF16)
        p_out[0, pair, window:] = (ep * inv).astype(BF16)

    def mixing(pair):
        cols = slice(pair * PAIR, (pair + 1) * PAIR)
        vals = jnp.concatenate([vt[cols, win], pvt[cols, :]], axis=1)
        mixt[cols, rows] = own_blocks(dot(vals, p_out[0, pair])).astype(BF16)

    for i in range(pairs + 2):
        if i < pairs:
            score(i)
        if 0 <= i - 1 < pairs:
            soft(i - 1)
        if 0 <= i - 2 < pairs:
            mixing(i - 2)

    @pl.when(qb == pl.num_programs(0) - 1)
    def _():
        big = eye(256)
        for r in range(length // 256):
            rr = slice(r * 256, (r + 1) * 256)
            mix_out[rr] = dot_t(big, mixt[:, rr]).astype(BF16)
        for r in range(length // 256):
            rr = slice(r * 256, (r + 1) * 256)
            res_out[rr] = tok_ref[rr].astype(F32) + dot(mix_out[rr], wo_ref[...]) + bo_ref[...]


def attend_forward(tok, wqkv, seg, pk, pv, wo, bo):
    length, width = tok.shape
    pre = pk.shape[0]
    window = 3 * QB
    pairs, blocks = width // PAIR, length // QB
    outs = [kept((length, width), BF16)] * 4 + [
        (pl.BlockSpec((1, pairs, window + pre, 2 * QB), lambda i: (i, 0, 0, 0)),
         jax.ShapeDtypeStruct((blocks, pairs, window + pre, 2 * QB), BF16)),
        kept((length, width), F32)]
    return pl.pallas_call(
        forward_kernel,
        grid=(blocks,),
        in_specs=[whole(a) for a in (tok, wqkv, seg, pk, pv, wo, bo)],
        out_specs=[o[0] for o in outs],
        out_shape=[o[1] for o in outs],
        scratch_shapes=[
            pltpu.VMEM((width, length), BF16),
            pltpu.VMEM((width, pre), BF16),
            pltpu.VMEM((length, QB), F32),
            pltpu.VMEM((window, QB), F32),
            pltpu.VMEM((2, window + pre, 2 * QB), F32),
            pltpu.VMEM((width, length), BF16),
        ],
        compiler_params=pltpu.CompilerParams(vmem_limit_bytes=VMEM_LIMIT),
        name="attend_forward",
    )(tok, wqkv, seg, pk, pv, wo, bo)


def ffn_kernel(chunk, res_ref, dy_ref, up_hbm, down_hbm, ub_ref, wo_ref, db_ref, g1_ref, s1_ref, g2_ref, s2_ref,
               out_ref, gone_ref, gmix_ref, up, down, pre, hid, slope, low, acc, hat_s, sems):
    step = pl.program_id(0)
    count = up.shape[1] // chunk

    def fetch(j):
        cols = pl.ds(j * chunk, chunk)
        return (
            pltpu.make_async_copy(up_hbm.at[:, cols], up.at[:, cols], sems.at[0, j]),
            pltpu.make_async_copy(down_hbm.at[cols], down.at[cols], sems.at[1, j]),
        )

    @pl.when(step == 0)
    def _():
        for j in range(count):
            for copy in fetch(j):
                copy.start()
        for j in range(count):
            for copy in fetch(j):
                copy.wait()

    hat, inv1 = normalize(res_ref[...])
    hat_s[...] = hat
    low[...] = (hat * g1_ref[...] + s1_ref[...]).astype(BF16)

    def cols_of(j):
        return slice(j * chunk, (j + 1) * chunk)

    def rows_up(j):
        pre[j % 2] = dot(low[...], up[:, cols_of(j)])

    def act(j):
        u = pre[j % 2] + ub_ref[:, cols_of(j)].astype(F32)
        half = 0.5 * lax.erf(u * ROOT_HALF) + 0.5
        hid[j % 2] = (u * half).astype(BF16)
        slope[:, cols_of(j)] = (half + u * (jnp.exp(-0.5 * u * u) * INV_ROOT_TWOPI)).astype(BF16)

    def rows_down(j):
        acc[...] += dot(hid[j % 2], down[cols_of(j)])

    acc[...] = jnp.zeros_like(acc)
    for j in range(count + 2):
        if j < count:
            rows_up(j)
        if 0 <= j - 2 < count:
            rows_down(j - 2)
        if 0 <= j - 1 < count:
            act(j - 1)

    hat2, inv2 = normalize(hat_s[...] * g1_ref[...] + s1_ref[...] + acc[...] + db_ref[...])
    out_ref[...] = (hat2 * g2_ref[...] + s2_ref[...]).astype(BF16)
    grad_two = norm_back(dy_ref[...].astype(F32), hat2, inv2, g2_ref[...])
    acc[...] = grad_two
    low[...] = grad_two.astype(BF16)

    def back_down(j):
        gh = dot_t(low[...], down[cols_of(j)])
        hid[j % 2] = (gh * slope[:, cols_of(j)].astype(F32)).astype(BF16)

    def back_up(j):
        acc[...] += dot_t(hid[j % 2], up[:, cols_of(j)])

    for j in range(count + 1):
        if j < count:
            back_down(j)
        if j >= 1:
            back_up(j - 1)

    grad_one = norm_back(acc[...], hat_s[...], inv1, g1_ref[...])
    gone_ref[...] = grad_one
    gmix_ref[...] = dot_t(grad_one.astype(BF16), wo_ref[...]).astype(BF16)


def feed_forward(res, dy, up, down, ub, wo, db, g1, s1, g2, s2, tb=256, chunk=512):
    rows, width = res.shape
    ff = up.shape[1]
    block = pl.BlockSpec((tb, width), lambda i: (i, 0))
    hbm = pl.BlockSpec(memory_space=pl.ANY)
    return pl.pallas_call(
        functools.partial(ffn_kernel, chunk),
        grid=(rows // tb,),
        in_specs=[block, block, hbm, hbm] + [whole(a) for a in (ub, wo, db, g1, s1, g2, s2)],
        out_specs=[block] * 3,
        out_shape=[jax.ShapeDtypeStruct((rows, width), t) for t in (BF16, F32, BF16)],
        scratch_shapes=[
            pltpu.VMEM((width, ff), BF16),
            pltpu.VMEM((ff, width), BF16),
            pltpu.VMEM((2, tb, chunk), F32),
            pltpu.VMEM((2, tb, chunk), BF16),
            pltpu.VMEM((tb, ff), BF16),
            pltpu.VMEM((tb, width), BF16),
            pltpu.VMEM((tb, width), F32),
            pltpu.VMEM((tb, width), F32),
            pltpu.SemaphoreType.DMA((2, ff // chunk)),
        ],
        compiler_params=pltpu.CompilerParams(vmem_limit_bytes=VMEM_LIMIT),
        name="feed_forward",
    )(res, dy, up, down, ub, wo, db, g1, s1, g2, s2)


def backward_kernel(group, p_ref, q_ref, k_ref, v_ref, mix_ref, do_ref, pk_ref, pv_ref, w_ref, gone_ref,
                    out_ref, gk_ref, gv_ref, kt, dk, dv, gj, delta, gbuf, dsbuf, dqt):
    step = pl.program_id(0)
    length = q_ref.shape[0]
    pre = pk_ref.shape[0]
    width = out_ref.shape[1]
    blocks = length // QB
    window = p_ref.shape[2] - pre
    ident = eye(QB)
    sub = lax.broadcasted_iota(jnp.int32, (8, PAIR), 0)
    lane = lax.broadcasted_iota(jnp.int32, (8, PAIR), 1)
    pick = jnp.where((sub == 0) == (lane < HEAD_DIM), 1.0, 0.0).astype(BF16)
    dk[...] = jnp.zeros_like(dk)
    dv[...] = jnp.zeros_like(dv)
    for g in range(group):
        cols = slice(g * PAIR, (g + 1) * PAIR)
        kt[cols, :length] = dot_t(ident, k_ref[:, cols]).astype(BF16)
        kt[cols, length:] = dot_t(ident, pk_ref[:, cols]).astype(BF16)
        prod = do_ref[:, cols].astype(F32) * mix_ref[:, cols].astype(F32)
        high = prod.astype(BF16)
        low = (prod - high.astype(F32)).astype(BF16)
        delta[g] = dot_t(pick, high) + dot_t(pick, low)

    def where_of(i):
        g, qb = divmod(i, blocks)
        start = min(max(qb * QB - QB, 0), length - window)
        return g, qb, slice(start, start + window), slice(qb * QB, (qb + 1) * QB), slice(g * PAIR, (g + 1) * PAIR)

    def grad_probs(i):
        g, qb, win, rows, cols = where_of(i)
        vals = jnp.concatenate([v_ref[win, cols], pv_ref[:, cols]], axis=0)
        gbuf[i % 2] = dot_t(vals, split_heads(do_ref[rows, cols]))

    def grad_scores(i):
        g, qb, win, rows, cols = where_of(i)
        d = jnp.concatenate([delta[g, 0:1, rows], delta[g, 1:2, rows]], axis=1)
        dsbuf[i % 2] = (p_ref[qb, g].astype(F32) * (gbuf[i % 2] - d)).astype(BF16)

    def grads(i):
        g, qb, win, rows, cols = where_of(i)
        ds = dsbuf[i % 2]
        dva = dot(p_ref[qb, g], split_heads(do_ref[rows, cols]))
        dv[win, cols] += dva[:window]
        dv[length:, cols] += dva[window:]
        dka = dot(ds, split_heads(q_ref[rows, cols]))
        dk[win, cols] += dka[:window]
        dk[length:, cols] += dka[window:]
        keys = jnp.concatenate([kt[cols, win], kt[cols, length:]], axis=1)
        dqt[cols, rows] = own_blocks(dot(keys, ds) * HEAD_DIM ** -0.5).astype(BF16)

    total = group * blocks
    for i in range(total + 2):
        if i < total:
            grad_probs(i)
        if 0 <= i - 1 < total:
            grad_scores(i - 1)
        if 0 <= i - 2 < total:
            grads(i - 2)
    gw = group * PAIR
    big = eye(256)
    for r in range(length // 256):
        rr = slice(r * 256, (r + 1) * 256)
        gj[step, rr, 0:gw] = dot_t(big, dqt[:, rr]).astype(BF16)
    gj[step, :, gw:2 * gw] = dk[:length].astype(BF16)
    gj[step, :, 2 * gw:] = dv[:length].astype(BF16)
    gk_ref[...] = dk[length:]
    gv_ref[...] = dv[length:]

    @pl.when(step == pl.num_programs(0) - 1)
    def _():
        steps = width // gw
        for r in range(length // 256):
            rr = slice(r * 256, (r + 1) * 256)
            acc = gone_ref[rr]
            for part in range(3):
                x = jnp.concatenate([gj[i, rr, part * gw:(part + 1) * gw] for i in range(steps)], axis=1)
                acc = acc + dot_t(x, w_ref[:, part * width:(part + 1) * width])
            out_ref[rr] = acc.astype(BF16)


def attend_backward(p, q, k, v, mix, do, pk, pv, wqkv, gone, group=2):
    length, width = q.shape
    pre = pk.shape[0]
    blocks, pairs, depth, _ = p.shape
    gw = group * PAIR

    def col(a):
        return pl.BlockSpec((a.shape[0], gw), lambda i: (0, i))

    out_spec, out_shape = kept((length, width), BF16)
    return pl.pallas_call(
        functools.partial(backward_kernel, group),
        grid=(pairs // group,),
        in_specs=[pl.BlockSpec((blocks, group, depth, 2 * QB), lambda i: (0, i, 0, 0))]
        + [col(a) for a in (q, k, v, mix, do, pk, pv)] + [whole(wqkv), whole(gone)],
        out_specs=[out_spec, col(pk), col(pv)],
        out_shape=[out_shape] + [jax.ShapeDtypeStruct((pre, width), F32)] * 2,
        scratch_shapes=[
            pltpu.VMEM((gw, length + pre), BF16),
            pltpu.VMEM((length + pre, gw), F32),
            pltpu.VMEM((length + pre, gw), F32),
            pltpu.VMEM((pairs // group, length, 3 * gw), BF16),
            pltpu.VMEM((group, 8, length), F32),
            pltpu.VMEM((2, depth, 2 * QB), F32),
            pltpu.VMEM((2, depth, 2 * QB), BF16),
            pltpu.VMEM((gw, length), BF16),
        ],
        compiler_params=pltpu.CompilerParams(vmem_limit_bytes=VMEM_LIMIT),
        name="attend_backward",
    )(p, q, k, v, mix, do, pk, pv, wqkv, gone)


def on_device(tokens, segment_ids, qkv_weight, prefix_keys, prefix_values, out_weight, out_bias, norm1_gain, norm1_shift,
              up_weight, up_bias, down_weight, down_bias, norm2_gain, norm2_shift, out_grad):
    row = lambda a: a.reshape(1, -1)
    up_all = lax.all_gather(up_weight, "mp", axis=1, tiled=True)
    down_all = lax.all_gather(down_weight, "mp", axis=0, tiled=True)
    bias_all = lax.all_gather(up_bias, "mp", axis=0, tiled=True)
    q, k, v, mix, probs, res = attend_forward(
        tokens[0], qkv_weight, segment_ids, prefix_keys, prefix_values, out_weight, row(out_bias))
    out, grad_one, grad_mixed = feed_forward(
        res, out_grad[0], up_all, down_all, row(bias_all), out_weight, row(down_bias), row(norm1_gain), row(norm1_shift),
        row(norm2_gain), row(norm2_shift))
    grad_tokens, gk, gv = attend_backward(
        probs, q, k, v, mix, grad_mixed, prefix_keys, prefix_values, qkv_weight, grad_one)
    total_k, total_v = lax.psum((gk, gv), ("dp", "mp"))
    return out[None], grad_tokens[None], total_k, total_v


def solution(mesh):
    rows = P(("dp", "mp"), None, None)
    return jax.shard_map(
        on_device,
        mesh=mesh,
        in_specs=(rows, P(("dp", "mp"), None), P(), P(), P(), P(), P(), P(), P(), P(None, "mp"), P("mp"), P("mp", None),
                  P(), P(), P(), rows),
        out_specs=(rows, rows, P(), P()),
        check_vma=False,
    )
```

```python
import functools

import jax
import jax.numpy as jnp
from jax import lax
from jax.experimental import pallas as pl
from jax.experimental.pallas import tpu as pltpu
from jax.sharding import PartitionSpec as P

EPSILON = 1e-05
ROOT_HALF = 0.7071067811865476
INV_ROOT_TWOPI = 0.3989422804014327
MASK_FILL = -1e30
HEAD_DIM = 64
PAIR = 2 * HEAD_DIM
QB = 128
F32 = jnp.float32
BF16 = jnp.bfloat16
VMEM_LIMIT = 62 * 1024 * 1024
BIAS_ROWS = 32
GATHER_SLOTS = ((0, 0, 0), (1, 1, 0), (2, 0, 1), (4, 1, 1), (5, 0, 2), (7, 1, 2), (8, 0, 3), (9, 1, 3), (9, 0, 4), (9, 1, 4))


def dot(a, b):
    return lax.dot_general(a, b, (((1,), (0,)), ((), ())), preferred_element_type=F32)


def dot_t(a, b):
    return lax.dot_general(a, b, (((1,), (1,)), ((), ())), preferred_element_type=F32)


def eye(n):
    r = lax.broadcasted_iota(jnp.int32, (n, n), 0)
    c = lax.broadcasted_iota(jnp.int32, (n, n), 1)
    return jnp.where(r == c, 1.0, 0.0).astype(BF16)


def split_heads(x):
    lane = lax.broadcasted_iota(jnp.int32, x.shape, 1)
    zero = jnp.zeros_like(x)
    return jnp.concatenate([jnp.where(lane < HEAD_DIM, x, zero), jnp.where(lane < HEAD_DIM, zero, x)], axis=0)


def own_blocks(x):
    return jnp.concatenate([x[:HEAD_DIM, :QB], x[HEAD_DIM:, QB:]], axis=0)


def normalize(x):
    scale = 1.0 / x.shape[-1]
    cen = x - jnp.sum(x, -1, keepdims=True) * scale
    inv = lax.rsqrt(jnp.sum(cen * cen, -1, keepdims=True) * scale + EPSILON)
    return cen * inv, inv


def norm_back(grad, hat, inv, gain):
    scale = 1.0 / grad.shape[-1]
    sc = grad * gain
    mean1 = jnp.sum(sc, -1, keepdims=True) * scale
    mean2 = jnp.sum(sc * hat, -1, keepdims=True) * scale
    return (sc - mean1 - hat * mean2) * inv


def whole(a):
    return pl.BlockSpec(a.shape, lambda i: (0,) * a.ndim, pipeline_mode=pl.Buffered(1))


def kept(shape, dtype):
    spec = pl.BlockSpec(shape, lambda i: (0,) * len(shape), pipeline_mode=pl.Buffered(1))
    return spec, jax.ShapeDtypeStruct(shape, dtype)


LINE = 4


def flip(x, bits):
    bit = 1
    while bit <= bits:
        if bits & bit:
            x = x + bit - 2 * bit * ((x // bit) % 2)
        bit *= 2
    return x


def guarded(condition, body):
    if condition is None:
        body()
    else:
        pl.when(condition)(body)


def gather_keys(count_b):
    others = range(1, count_b)
    keys = [("z", side, d, 0) for side in (1, -1) for d in (1, 2, 3)]
    keys += [("z", side, d, 1) for side in (1, -1) for d in (1, 2)]
    for s in others:
        keys += [("x", s, d, 0) for d in (0, 1, -1, 2, 3)] + [("x", s, 3, 1)]
        keys += [("y", s, d, 0) for d in (0, 1, -1, 2)]
    keys.append(("y", 0, 3, 0))
    keys.append(("core", 0, 0, None))
    for s in range(count_b):
        keys += [("core", s, d, part) for d in (0, 1, -1, 2, 3) for part in (0, 1) if (s, d) != (0, 0)]
    return {key: i for i, key in enumerate(keys)}


def gather_events(count_b):
    others = range(1, count_b)
    sides = (1, -1)
    return [
        [("x", s, 0, 0) for s in others] + [("z", side, 1, 0) for side in sides],
        [("z", side, 2, 0) for side in sides] + [("x", s, d, 0) for s in others for d in sides] + [("y", s, 0, 0) for s in others],
        [("z", side, 3, 0) for side in sides] + [("x", s, 2, 0) for s in others] + [("z", side, 1, 1) for side in sides]
        + [("y", s, d, 0) for s in others for d in sides],
        [("y", 0, 3, 0)] + [("x", s, 3, 0) for s in others] + [("z", side, 2, 1) for side in sides],
        [("y", s, 2, 0) for s in others] + [("x", s, 3, 1) for s in others],
    ]


class Gather:
    def __init__(self, count_b, inputs, alls, sems):
        self.count_b = count_b
        self.inputs, self.alls = inputs, alls
        self.send, self.recv = sems
        self.dp = lax.axis_index("dp")
        self.mp = lax.axis_index("mp")
        self.core = self.mp % 2
        self.b = (self.mp // 2) % self.count_b
        self.a = self.mp // (2 * self.count_b)
        self.half = self.dp % 2
        self.keys = gather_keys(count_b)

    def index(self, a, s, other=False):
        core = 1 - self.core if other else self.core
        return (a * self.count_b + flip(self.b, s)) * 2 + core

    def at(self, d):
        if d in (2, 3):
            return self.a + d - 2 * d * ((self.a + d) // LINE)
        return self.a + d

    def inside(self, d):
        if d == 1:
            return self.a < LINE - 1
        if d == -1:
            return self.a > 0
        if d == 3:
            return self.a % 3 == 0
        return None

    def gets(self, key):
        kind, s, d, part = key
        if kind != "z":
            return self.inside(d)
        return self.a + d < LINE if s == 1 else self.a >= d

    def sends(self, key):
        kind, s, d, part = key
        if kind != "z":
            return self.inside(d)
        low, high = (1, LINE - d) if s == 1 else (d - 1, LINE - 2)
        return (self.a >= low) & (self.a <= high)

    def copy(self, t, key, arriving):
        kind, s, d, part = key
        own = d == 0 and not arriving
        if kind == "z":
            own = d == 1 and not arriving
            target = (self.dp, self.index(self.a - s, 0))
            chunk = self.index(self.a + s * d, 0) if arriving else self.index(self.a + s * (d - 1), 0)
        elif kind == "x":
            target = (self.dp, self.index(self.a, s))
            chunk = self.index(self.at(d), s if arriving else 0)
        elif kind == "y":
            target = (flip(self.dp, 1), self.mp)
            chunk = self.index(self.at(d), s)
            own = False
        else:
            target = (self.dp, self.index(self.a, 0, True))
            chunk = self.index(self.at(d), s, arriving)
            own = own and s == 0
        ref = self.alls[t]
        rows = ref.shape[1]
        if part is None:
            span = pl.ds(0, rows)
        else:
            which = 1 - part if kind == "y" and arriving else part
            which = self.half if which == 0 else 1 - self.half
            span = pl.ds(pl.multiple_of(which * (rows // 2), 16), rows // 2)
        src = self.inputs[t].at[span] if own else ref.at[chunk, span]
        number = self.keys[key]
        return pltpu.make_async_remote_copy(
            src_ref=src, dst_ref=ref.at[chunk, span], send_sem=self.send.at[t, number], recv_sem=self.recv.at[t, number],
            device_id=target, device_id_type=pl.DeviceIdType.MESH)

    def start(self, t, *key):
        guarded(self.sends(key), lambda: self.copy(t, key, False).start())

    def arrive(self, t, key):
        self.copy(t, key, True).wait_recv()

    def greet(self):
        barrier = pltpu.get_barrier_semaphore()
        partners = [(self.inside(d), (self.dp, self.index(self.a + d, 0))) for d in (1, -1)]
        partners += [(None, (self.dp, self.index(self.a, s))) for s in range(1, self.count_b)]
        partners += [(None, (self.dp, self.index(self.a, 0, True))), (None, (flip(self.dp, 1), self.mp))]
        for condition, device in partners:
            guarded(condition, lambda: pl.semaphore_signal(
                barrier, inc=1, device_id=device, device_id_type=pl.DeviceIdType.MESH))
        ends = 1 - (self.a % 3 + 1) // 2
        pl.semaphore_wait(barrier, len(partners) - ends)

    def open(self, t):
        for side in (1, -1):
            self.start(t, "z", side, 1, 0)
        for s in range(1, self.count_b):
            self.start(t, "x", s, 0, 0)
        self.start(t, "core", 0, 0, None)

    def pass_on(self, t, key):
        kind, s, d, part = key

        def body():
            self.arrive(t, key)
            if kind == "z":
                if d < (3 if part == 0 else 2):
                    self.start(t, "z", s, d + 1, part)
                at = s if d == 1 else d
                if part == 0:
                    for other in range(1, self.count_b):
                        self.start(t, "x", other, at, 0)
                    if d == 3:
                        self.start(t, "y", 0, 3, 0)
                self.start(t, "core", 0, at, part)
            elif kind == "x":
                if d != 3:
                    self.start(t, "y", s, d, 0)
                self.start(t, "core", s, d, part)
            else:
                if d == 3:
                    for other in range(1, self.count_b):
                        self.start(t, "x", other, 3, 1)
                self.start(t, "core", s, d, 1)

        guarded(self.gets(key), body)

    def level(self, t, n):
        for key in gather_events(self.count_b)[n]:
            self.pass_on(t, key)
        if n == 0:
            for side in (1, -1):
                self.start(t, "z", side, 1, 1)

    def finish(self, t):
        for key in self.keys:
            if key[0] == "core":
                guarded(self.gets(key), lambda: self.arrive(t, key))

    def close(self, t):
        for key in self.keys:
            guarded(self.sends(key), lambda: self.copy(t, key, False).wait_send())


def forward_kernel(count_b, tok_ref, wqkv_ref, seg_ref, pk_ref, pv_ref, wo_ref, bo_ref, up_in, down_in,
                   q_out, k_out, v_out, mix_out, p_out, res_out, up_all, down_all,
                   vt, pvt, segc, bias, sbuf, mixt, send, recv):
    qb = pl.program_id(0)
    gather = Gather(count_b, (up_in, down_in), (up_all, down_all), (send, recv))

    def pass_on(now):
        for slot, t, n in GATHER_SLOTS:
            if slot == now:
                gather.level(t, n)

    length, width = tok_ref.shape
    window = bias.shape[0]
    pairs = width // PAIR

    @pl.when(qb == 0)
    def _():
        gather.greet()
        gather.open(0)
        gather.open(1)
        tile = 256
        for part, ref in enumerate((q_out, k_out, v_out)):
            for j in range(width // tile):
                x = dot(tok_ref[...], wqkv_ref[:, part * width + j * tile:part * width + (j + 1) * tile]).astype(BF16)
                if part == 0:
                    x = x * jnp.asarray(HEAD_DIM ** -0.5, BF16)
                ref[:, j * tile:(j + 1) * tile] = x
                if part == 2 and j == 2:
                    pass_on(0)
        big = eye(256)
        for j in range(width // 256):
            cols = slice(j * 256, (j + 1) * 256)
            vt[cols, :] = dot_t(big, v_out[:, cols]).astype(BF16)
            pvt[cols, :] = dot_t(big, pv_ref[:, cols]).astype(BF16)
        ident = eye(QB)
        seg = jnp.broadcast_to(seg_ref[...].astype(F32), (QB, length)).astype(BF16)
        for j in range(length // QB):
            segc[j * QB:(j + 1) * QB, :] = dot_t(ident, seg[:, j * QB:(j + 1) * QB])

    for slot in range(1, length // QB):

        @pl.when(qb == slot)
        def _():
            pass_on(slot)

    start = pl.multiple_of(jnp.clip(qb * QB - QB, 0, length - window), QB)
    win = pl.ds(start, window)
    rows = pl.ds(pl.multiple_of(qb * QB, QB), QB)
    segq = seg_ref[:, rows].astype(F32)
    bias[...] = jnp.where(segc[win, :] == segq, 0.0, MASK_FILL)

    def score(pair):
        cols = slice(pair * PAIR, (pair + 1) * PAIR)
        keys = jnp.concatenate([k_out[win, cols], pk_ref[:, cols]], axis=0)
        sbuf[pair % 2] = dot_t(keys, split_heads(q_out[rows, cols]))

    def soft(pair):
        both = jnp.concatenate([bias[...], bias[...]], axis=1)
        sw = sbuf[pair % 2, :window] + both
        sp = sbuf[pair % 2, window:]
        top = jnp.maximum(jnp.max(sw, 0, keepdims=True), jnp.max(sp, 0, keepdims=True))
        ew = jnp.exp(sw - top)
        ep = jnp.exp(sp - top)
        inv = 1.0 / (jnp.sum(ew, 0, keepdims=True) + jnp.sum(ep, 0, keepdims=True))
        p_out[0, pair, :window] = (ew * inv).astype(BF16)
        p_out[0, pair, window:] = (ep * inv).astype(BF16)

    def mixing(pair):
        cols = slice(pair * PAIR, (pair + 1) * PAIR)
        vals = jnp.concatenate([vt[cols, win], pvt[cols, :]], axis=1)
        mixt[cols, rows] = own_blocks(dot(vals, p_out[0, pair])).astype(BF16)

    for i in range(pairs + 2):
        if i < pairs:
            score(i)
        if 0 <= i - 1 < pairs:
            soft(i - 1)
        if 0 <= i - 2 < pairs:
            mixing(i - 2)

    @pl.when(qb == pl.num_programs(0) - 1)
    def _():
        pass_on(8)
        big = eye(256)
        for r in range(length // 256):
            rr = slice(r * 256, (r + 1) * 256)
            mix_out[rr] = dot_t(big, mixt[:, rr]).astype(BF16)
        for r in range(length // 256):
            rr = slice(r * 256, (r + 1) * 256)
            res_out[rr] = tok_ref[rr].astype(F32) + dot(mix_out[rr], wo_ref[...]) + bo_ref[...]
        pass_on(9)
        for t in range(2):
            gather.finish(t)
        for t in range(2):
            gather.close(t)


def attend_forward(tok, wqkv, seg, pk, pv, wo, bo, up, down, group):
    length, width = tok.shape
    pre = pk.shape[0]
    window = 3 * QB
    pairs, blocks = width // PAIR, length // QB
    outs = [kept((length, width), BF16)] * 4 + [
        (pl.BlockSpec((1, pairs, window + pre, 2 * QB), lambda i: (i, 0, 0, 0)),
         jax.ShapeDtypeStruct((blocks, pairs, window + pre, 2 * QB), BF16)),
        kept((length, width), F32)]
    hbm = pl.BlockSpec(memory_space=pl.ANY)
    outs += [(hbm, jax.ShapeDtypeStruct((group,) + a.shape, BF16)) for a in (up, down)]
    count_b = group // (2 * LINE)
    pieces = len(gather_keys(count_b))
    return pl.pallas_call(
        functools.partial(forward_kernel, count_b),
        grid=(blocks,),
        in_specs=[whole(a) for a in (tok, wqkv, seg, pk, pv, wo, bo)] + [hbm, hbm],
        out_specs=[o[0] for o in outs],
        out_shape=[o[1] for o in outs],
        scratch_shapes=[
            pltpu.VMEM((width, length), BF16),
            pltpu.VMEM((width, pre), BF16),
            pltpu.VMEM((length, QB), F32),
            pltpu.VMEM((window, QB), F32),
            pltpu.VMEM((2, window + pre, 2 * QB), F32),
            pltpu.VMEM((width, length), BF16),
            pltpu.SemaphoreType.DMA((2, pieces)),
            pltpu.SemaphoreType.DMA((2, pieces)),
        ],
        compiler_params=pltpu.CompilerParams(vmem_limit_bytes=VMEM_LIMIT, collective_id=0, has_side_effects=True),
        name="attend_forward",
    )(tok, wqkv, seg, pk, pv, wo, bo, up, down)


def ffn_kernel(chunk, res_ref, dy_ref, up_hbm, down_hbm, up_own, down_own, wo_ref, db_ref, g1_ref, s1_ref, g2_ref, s2_ref,
               out_ref, gone_ref, gmix_ref, up, down, ub, pre, hid, slope, low, acc, hat_s, sems):
    step = pl.program_id(0)
    count = up.shape[1] // chunk
    width = up.shape[0]
    parts, _, part = up_hbm.shape

    me = lax.axis_index("mp")

    def fetch(d, t):
        cols = pl.ds(d * part, part)
        up_src, down_src = (up_own, down_own) if d == 0 else (up_hbm.at[(me + d) % parts], down_hbm.at[(me + d) % parts])
        src = (up_src.at[pl.ds(0, width)], up_src.at[pl.ds(width, BIAS_ROWS)], down_src)[t]
        dst = (up.at[:, cols], ub.at[:, cols], down.at[cols])[t]
        return pltpu.make_async_copy(src, dst, sems.at[t, d])

    @pl.when(step == 0)
    def _():
        for t in range(3):
            for d in range(parts):
                fetch(d, t).start()

    hat, inv1 = normalize(res_ref[...])
    hat_s[...] = hat
    low[...] = (hat * g1_ref[...] + s1_ref[...]).astype(BF16)

    @pl.when(step == 0)
    def _():
        for t in range(2):
            for d in range(parts):
                fetch(d, t).wait()

    def cols_of(j):
        return slice(j * chunk, (j + 1) * chunk)

    def rows_up(j):
        pre[j % 2] = dot(low[...], up[:, cols_of(j)])

    def act(j):
        u = pre[j % 2] + ub[0:1, cols_of(j)].astype(F32)
        half = 0.5 * lax.erf(u * ROOT_HALF) + 0.5
        hid[j % 2] = (u * half).astype(BF16)
        slope[:, cols_of(j)] = (half + u * (jnp.exp(-0.5 * u * u) * INV_ROOT_TWOPI)).astype(BF16)

    def rows_down(j):
        acc[...] += dot(hid[j % 2], down[cols_of(j)])

    acc[...] = jnp.zeros_like(acc)
    for j in range(count + 2):
        if j == 2:

            @pl.when(step == 0)
            def _():
                for d in range(parts):
                    fetch(d, 2).wait()

        if j < count:
            rows_up(j)
        if 0 <= j - 2 < count:
            rows_down(j - 2)
        if 0 <= j - 1 < count:
            act(j - 1)

    hat2, inv2 = normalize(hat_s[...] * g1_ref[...] + s1_ref[...] + acc[...] + db_ref[...])
    out_ref[...] = (hat2 * g2_ref[...] + s2_ref[...]).astype(BF16)
    grad_two = norm_back(dy_ref[...].astype(F32), hat2, inv2, g2_ref[...])
    acc[...] = grad_two
    low[...] = grad_two.astype(BF16)

    def back_down(j):
        gh = dot_t(low[...], down[cols_of(j)])
        hid[j % 2] = (gh * slope[:, cols_of(j)].astype(F32)).astype(BF16)

    def back_up(j):
        acc[...] += dot_t(hid[j % 2], up[:, cols_of(j)])

    for j in range(count + 1):
        if j < count:
            back_down(j)
        if j >= 1:
            back_up(j - 1)

    grad_one = norm_back(acc[...], hat_s[...], inv1, g1_ref[...])
    gone_ref[...] = grad_one
    gmix_ref[...] = dot_t(grad_one.astype(BF16), wo_ref[...]).astype(BF16)


def feed_forward(res, dy, up, down, up_own, down_own, wo, db, g1, s1, g2, s2, tb=256, chunk=512):
    rows, width = res.shape
    parts, ffl, _ = down.shape
    ff = parts * ffl
    block = pl.BlockSpec((tb, width), lambda i: (i, 0))
    hbm = pl.BlockSpec(memory_space=pl.ANY)
    return pl.pallas_call(
        functools.partial(ffn_kernel, chunk),
        grid=(rows // tb,),
        in_specs=[block, block] + [hbm] * 4 + [whole(a) for a in (wo, db, g1, s1, g2, s2)],
        out_specs=[block] * 3,
        out_shape=[jax.ShapeDtypeStruct((rows, width), t) for t in (BF16, F32, BF16)],
        scratch_shapes=[
            pltpu.VMEM((width, ff), BF16),
            pltpu.VMEM((ff, width), BF16),
            pltpu.VMEM((BIAS_ROWS, ff), BF16),
            pltpu.VMEM((2, tb, chunk), F32),
            pltpu.VMEM((2, tb, chunk), BF16),
            pltpu.VMEM((tb, ff), BF16),
            pltpu.VMEM((tb, width), BF16),
            pltpu.VMEM((tb, width), F32),
            pltpu.VMEM((tb, width), F32),
            pltpu.SemaphoreType.DMA((3, parts)),
        ],
        compiler_params=pltpu.CompilerParams(vmem_limit_bytes=VMEM_LIMIT),
        name="feed_forward",
    )(res, dy, up, down, up_own, down_own, wo, db, g1, s1, g2, s2)


def backward_kernel(group, p_ref, q_ref, k_ref, v_ref, mix_ref, do_ref, pk_ref, pv_ref, w_ref, gone_ref,
                    out_ref, gk_ref, gv_ref, kt, dk, dv, gj, delta, gbuf, dsbuf, dqt):
    step = pl.program_id(0)
    length = q_ref.shape[0]
    pre = pk_ref.shape[0]
    width = out_ref.shape[1]
    blocks = length // QB
    window = p_ref.shape[2] - pre
    ident = eye(QB)
    sub = lax.broadcasted_iota(jnp.int32, (8, PAIR), 0)
    lane = lax.broadcasted_iota(jnp.int32, (8, PAIR), 1)
    pick = jnp.where((sub == 0) == (lane < HEAD_DIM), 1.0, 0.0).astype(BF16)
    dk[...] = jnp.zeros_like(dk)
    dv[...] = jnp.zeros_like(dv)
    for g in range(group):
        cols = slice(g * PAIR, (g + 1) * PAIR)
        kt[cols, :length] = dot_t(ident, k_ref[:, cols]).astype(BF16)
        kt[cols, length:] = dot_t(ident, pk_ref[:, cols]).astype(BF16)
        prod = do_ref[:, cols].astype(F32) * mix_ref[:, cols].astype(F32)
        high = prod.astype(BF16)
        low = (prod - high.astype(F32)).astype(BF16)
        delta[g] = dot_t(pick, high) + dot_t(pick, low)

    def where_of(i):
        g, qb = divmod(i, blocks)
        start = min(max(qb * QB - QB, 0), length - window)
        return g, qb, slice(start, start + window), slice(qb * QB, (qb + 1) * QB), slice(g * PAIR, (g + 1) * PAIR)

    def grad_probs(i):
        g, qb, win, rows, cols = where_of(i)
        vals = jnp.concatenate([v_ref[win, cols], pv_ref[:, cols]], axis=0)
        gbuf[i % 2] = dot_t(vals, split_heads(do_ref[rows, cols]))

    def grad_scores(i):
        g, qb, win, rows, cols = where_of(i)
        d = jnp.concatenate([delta[g, 0:1, rows], delta[g, 1:2, rows]], axis=1)
        dsbuf[i % 2] = (p_ref[qb, g].astype(F32) * (gbuf[i % 2] - d)).astype(BF16)

    def grads(i):
        g, qb, win, rows, cols = where_of(i)
        ds = dsbuf[i % 2]
        dva = dot(p_ref[qb, g], split_heads(do_ref[rows, cols]))
        dv[win, cols] += dva[:window]
        dv[length:, cols] += dva[window:]
        dka = dot(ds, split_heads(q_ref[rows, cols]))
        dk[win, cols] += dka[:window]
        dk[length:, cols] += dka[window:]
        keys = jnp.concatenate([kt[cols, win], kt[cols, length:]], axis=1)
        dqt[cols, rows] = own_blocks(dot(keys, ds) * HEAD_DIM ** -0.5).astype(BF16)

    total = group * blocks
    for i in range(total + 2):
        if i < total:
            grad_probs(i)
        if 0 <= i - 1 < total:
            grad_scores(i - 1)
        if 0 <= i - 2 < total:
            grads(i - 2)
    gw = group * PAIR
    big = eye(256)
    for r in range(length // 256):
        rr = slice(r * 256, (r + 1) * 256)
        gj[step, rr, 0:gw] = dot_t(big, dqt[:, rr]).astype(BF16)
    gj[step, :, gw:2 * gw] = dk[:length].astype(BF16)
    gj[step, :, 2 * gw:] = dv[:length].astype(BF16)
    gk_ref[...] = dk[length:]
    gv_ref[...] = dv[length:]

    @pl.when(step == pl.num_programs(0) - 1)
    def _():
        steps = width // gw
        for r in range(length // 256):
            rr = slice(r * 256, (r + 1) * 256)
            acc = gone_ref[rr]
            for part in range(3):
                x = jnp.concatenate([gj[i, rr, part * gw:(part + 1) * gw] for i in range(steps)], axis=1)
                acc = acc + dot_t(x, w_ref[:, part * width:(part + 1) * width])
            out_ref[rr] = acc.astype(BF16)


def attend_backward(p, q, k, v, mix, do, pk, pv, wqkv, gone, group=2):
    length, width = q.shape
    pre = pk.shape[0]
    blocks, pairs, depth, _ = p.shape
    gw = group * PAIR

    def col(a):
        return pl.BlockSpec((a.shape[0], gw), lambda i: (0, i))

    out_spec, out_shape = kept((length, width), BF16)
    return pl.pallas_call(
        functools.partial(backward_kernel, group),
        grid=(pairs // group,),
        in_specs=[pl.BlockSpec((blocks, group, depth, 2 * QB), lambda i: (0, i, 0, 0))]
        + [col(a) for a in (q, k, v, mix, do, pk, pv)] + [whole(wqkv), whole(gone)],
        out_specs=[out_spec, col(pk), col(pv)],
        out_shape=[out_shape] + [jax.ShapeDtypeStruct((pre, width), F32)] * 2,
        scratch_shapes=[
            pltpu.VMEM((gw, length + pre), BF16),
            pltpu.VMEM((length + pre, gw), F32),
            pltpu.VMEM((length + pre, gw), F32),
            pltpu.VMEM((pairs // group, length, 3 * gw), BF16),
            pltpu.VMEM((group, 8, length), F32),
            pltpu.VMEM((2, depth, 2 * QB), F32),
            pltpu.VMEM((2, depth, 2 * QB), BF16),
            pltpu.VMEM((gw, length), BF16),
        ],
        compiler_params=pltpu.CompilerParams(vmem_limit_bytes=VMEM_LIMIT),
        name="attend_backward",
    )(p, q, k, v, mix, do, pk, pv, wqkv, gone)


def on_device(group, tokens, segment_ids, qkv_weight, prefix_keys, prefix_values, out_weight, out_bias, norm1_gain,
              norm1_shift, up_weight, up_bias, down_weight, down_bias, norm2_gain, norm2_shift, out_grad):
    row = lambda a: a.reshape(1, -1)
    up_part = jnp.concatenate([up_weight, jnp.broadcast_to(row(up_bias), (BIAS_ROWS, up_bias.shape[0]))], axis=0)
    q, k, v, mix, probs, res, up_all, down_all = attend_forward(
        tokens[0], qkv_weight, segment_ids, prefix_keys, prefix_values, out_weight, row(out_bias), up_part, down_weight, group)
    out, grad_one, grad_mixed = feed_forward(
        res, out_grad[0], up_all, down_all, up_part, down_weight, out_weight, row(down_bias), row(norm1_gain), row(norm1_shift),
        row(norm2_gain), row(norm2_shift))
    grad_tokens, gk, gv = attend_backward(
        probs, q, k, v, mix, grad_mixed, prefix_keys, prefix_values, qkv_weight, grad_one)
    total_k, total_v = lax.psum((gk, gv), ("dp", "mp"))
    return out[None], grad_tokens[None], total_k, total_v


def solution(mesh):
    rows = P(("dp", "mp"), None, None)
    return jax.shard_map(
        functools.partial(on_device, mesh.shape["mp"]),
        mesh=mesh,
        in_specs=(rows, P(("dp", "mp"), None), P(), P(), P(), P(), P(), P(), P(), P(None, "mp"), P("mp"), P("mp", None),
                  P(), P(), P(), rows),
        out_specs=(rows, rows, P(), P()),
        check_vma=False,
    )
```

```python
import functools

import jax
import jax.numpy as jnp
from jax import lax
from jax.experimental import pallas as pl
from jax.experimental.pallas import tpu as pltpu
from jax.sharding import PartitionSpec as P

EPSILON = 1e-05
ROOT_HALF = 0.7071067811865476
INV_ROOT_TWOPI = 0.3989422804014327
MASK_FILL = -1e30
HEAD_DIM = 64
PAIR = 2 * HEAD_DIM
QB = 128
F32 = jnp.float32
BF16 = jnp.bfloat16
VMEM_LIMIT = 62 * 1024 * 1024
BIAS_ROWS = 32
GATHER_SLOTS = ((0, 0, 0), (1, 1, 0), (2, 0, 1), (4, 1, 1), (5, 0, 2), (7, 1, 2), (8, 0, 3), (9, 1, 3), (9, 0, 4), (9, 1, 4))


def dot(a, b):
    return lax.dot_general(a, b, (((1,), (0,)), ((), ())), preferred_element_type=F32)


def dot_t(a, b):
    return lax.dot_general(a, b, (((1,), (1,)), ((), ())), preferred_element_type=F32)


def eye(n):
    r = lax.broadcasted_iota(jnp.int32, (n, n), 0)
    c = lax.broadcasted_iota(jnp.int32, (n, n), 1)
    return jnp.where(r == c, 1.0, 0.0).astype(BF16)


def split_heads(x):
    lane = lax.broadcasted_iota(jnp.int32, x.shape, 1)
    zero = jnp.zeros_like(x)
    return jnp.concatenate([jnp.where(lane < HEAD_DIM, x, zero), jnp.where(lane < HEAD_DIM, zero, x)], axis=0)


def own_blocks(x):
    return jnp.concatenate([x[:HEAD_DIM, :QB], x[HEAD_DIM:, QB:]], axis=0)


def normalize(x):
    scale = 1.0 / x.shape[-1]
    cen = x - jnp.sum(x, -1, keepdims=True) * scale
    inv = lax.rsqrt(jnp.sum(cen * cen, -1, keepdims=True) * scale + EPSILON)
    return cen * inv, inv


def norm_back(grad, hat, inv, gain):
    scale = 1.0 / grad.shape[-1]
    sc = grad * gain
    mean1 = jnp.sum(sc, -1, keepdims=True) * scale
    mean2 = jnp.sum(sc * hat, -1, keepdims=True) * scale
    return (sc - mean1 - hat * mean2) * inv


def whole(a):
    return pl.BlockSpec(a.shape, lambda i: (0,) * a.ndim, pipeline_mode=pl.Buffered(1))


def kept(shape, dtype):
    spec = pl.BlockSpec(shape, lambda i: (0,) * len(shape), pipeline_mode=pl.Buffered(1))
    return spec, jax.ShapeDtypeStruct(shape, dtype)


LINE = 4


def flip(x, bits):
    bit = 1
    while bit <= bits:
        if bits & bit:
            x = x + bit - 2 * bit * ((x // bit) % 2)
        bit *= 2
    return x


def guarded(condition, body):
    if condition is None:
        body()
    else:
        pl.when(condition)(body)


def gather_keys(count_b):
    others = range(1, count_b)
    keys = [("z", side, d, 0) for side in (1, -1) for d in (1, 2, 3)]
    keys += [("z", side, d, 1) for side in (1, -1) for d in (1, 2)]
    for s in others:
        keys += [("x", s, d, 0) for d in (0, 1, -1, 2, 3)] + [("x", s, 3, 1)]
        keys += [("y", s, d, 0) for d in (0, 1, -1, 2)]
    keys.append(("y", 0, 3, 0))
    keys.append(("core", 0, 0, None))
    for s in range(count_b):
        keys += [("core", s, d, part) for d in (0, 1, -1, 2, 3) for part in (0, 1) if (s, d) != (0, 0)]
    return {key: i for i, key in enumerate(keys)}


def gather_events(count_b):
    others = range(1, count_b)
    sides = (1, -1)
    return [
        [("x", s, 0, 0) for s in others] + [("z", side, 1, 0) for side in sides],
        [("z", side, 2, 0) for side in sides] + [("x", s, d, 0) for s in others for d in sides] + [("y", s, 0, 0) for s in others],
        [("z", side, 3, 0) for side in sides] + [("x", s, 2, 0) for s in others] + [("z", side, 1, 1) for side in sides]
        + [("y", s, d, 0) for s in others for d in sides],
        [("y", 0, 3, 0)] + [("x", s, 3, 0) for s in others] + [("z", side, 2, 1) for side in sides],
        [("y", s, 2, 0) for s in others] + [("x", s, 3, 1) for s in others],
    ]


class Gather:
    def __init__(self, count_b, inputs, alls, sems):
        self.count_b = count_b
        self.inputs, self.alls = inputs, alls
        self.send, self.recv = sems
        self.dp = lax.axis_index("dp")
        self.mp = lax.axis_index("mp")
        self.core = self.mp % 2
        self.b = (self.mp // 2) % self.count_b
        self.a = self.mp // (2 * self.count_b)
        self.half = self.dp % 2
        self.keys = gather_keys(count_b)

    def index(self, a, s, other=False):
        core = 1 - self.core if other else self.core
        return (a * self.count_b + flip(self.b, s)) * 2 + core

    def at(self, d):
        if d in (2, 3):
            return self.a + d - 2 * d * ((self.a + d) // LINE)
        return self.a + d

    def inside(self, d):
        if d == 1:
            return self.a < LINE - 1
        if d == -1:
            return self.a > 0
        if d == 3:
            return self.a % 3 == 0
        return None

    def gets(self, key):
        kind, s, d, part = key
        if kind != "z":
            return self.inside(d)
        return self.a + d < LINE if s == 1 else self.a >= d

    def sends(self, key):
        kind, s, d, part = key
        if kind != "z":
            return self.inside(d)
        low, high = (1, LINE - d) if s == 1 else (d - 1, LINE - 2)
        return (self.a >= low) & (self.a <= high)

    def copy(self, t, key, arriving):
        kind, s, d, part = key
        own = d == 0 and not arriving
        if kind == "z":
            own = d == 1 and not arriving
            target = (self.dp, self.index(self.a - s, 0))
            chunk = self.index(self.a + s * d, 0) if arriving else self.index(self.a + s * (d - 1), 0)
        elif kind == "x":
            target = (self.dp, self.index(self.a, s))
            chunk = self.index(self.at(d), s if arriving else 0)
        elif kind == "y":
            target = (flip(self.dp, 1), self.mp)
            chunk = self.index(self.at(d), s)
            own = False
        else:
            target = (self.dp, self.index(self.a, 0, True))
            chunk = self.index(self.at(d), s, arriving)
            own = own and s == 0
        ref = self.alls[t]
        rows = ref.shape[1]
        if part is None:
            span = pl.ds(0, rows)
        else:
            which = 1 - part if kind == "y" and arriving else part
            which = self.half if which == 0 else 1 - self.half
            span = pl.ds(pl.multiple_of(which * (rows // 2), 16), rows // 2)
        src = self.inputs[t].at[span] if own else ref.at[chunk, span]
        number = self.keys[key]
        return pltpu.make_async_remote_copy(
            src_ref=src, dst_ref=ref.at[chunk, span], send_sem=self.send.at[t, number], recv_sem=self.recv.at[t, number],
            device_id=target, device_id_type=pl.DeviceIdType.MESH)

    def start(self, t, *key):
        guarded(self.sends(key), lambda: self.copy(t, key, False).start())

    def arrive(self, t, key):
        self.copy(t, key, True).wait_recv()

    def greet(self):
        barrier = pltpu.get_barrier_semaphore()
        partners = [(self.inside(d), (self.dp, self.index(self.a + d, 0))) for d in (1, -1)]
        partners += [(None, (self.dp, self.index(self.a, s))) for s in range(1, self.count_b)]
        partners += [(None, (self.dp, self.index(self.a, 0, True))), (None, (flip(self.dp, 1), self.mp))]
        for condition, device in partners:
            guarded(condition, lambda: pl.semaphore_signal(
                barrier, inc=1, device_id=device, device_id_type=pl.DeviceIdType.MESH))
        ends = 1 - (self.a % 3 + 1) // 2
        pl.semaphore_wait(barrier, len(partners) - ends)

    def open(self, t):
        for side in (1, -1):
            self.start(t, "z", side, 1, 0)
        for s in range(1, self.count_b):
            self.start(t, "x", s, 0, 0)
        self.start(t, "core", 0, 0, None)

    def pass_on(self, t, key):
        kind, s, d, part = key

        def body():
            self.arrive(t, key)
            if kind == "z":
                if d < (3 if part == 0 else 2):
                    self.start(t, "z", s, d + 1, part)
                at = s if d == 1 else d
                if part == 0:
                    for other in range(1, self.count_b):
                        self.start(t, "x", other, at, 0)
                    if d == 3:
                        self.start(t, "y", 0, 3, 0)
                self.start(t, "core", 0, at, part)
            elif kind == "x":
                if d != 3:
                    self.start(t, "y", s, d, 0)
                self.start(t, "core", s, d, part)
            else:
                if d == 3:
                    for other in range(1, self.count_b):
                        self.start(t, "x", other, 3, 1)
                self.start(t, "core", s, d, 1)

        guarded(self.gets(key), body)

    def level(self, t, n):
        for key in gather_events(self.count_b)[n]:
            self.pass_on(t, key)
        if n == 0:
            for side in (1, -1):
                self.start(t, "z", side, 1, 1)

    def finish(self, t):
        for key in self.keys:
            if key[0] == "core":
                guarded(self.gets(key), lambda: self.arrive(t, key))

    def close(self, t):
        for key in self.keys:
            guarded(self.sends(key), lambda: self.copy(t, key, False).wait_send())


def forward_kernel(count_b, tok_ref, wqkv_ref, seg_ref, pk_ref, pv_ref, wo_ref, bo_ref, up_in, down_in,
                   q_out, k_out, v_out, mix_out, p_out, res_out, up_all, down_all,
                   vt, pvt, segc, bias, sbuf, mixt, send, recv):
    qb = pl.program_id(0)
    gather = Gather(count_b, (up_in, down_in), (up_all, down_all), (send, recv))

    def pass_on(now):
        for slot, t, n in GATHER_SLOTS:
            if slot == now:
                gather.level(t, n)

    length, width = tok_ref.shape
    window = bias.shape[0]
    pairs = width // PAIR

    @pl.when(qb == 0)
    def _():
        gather.greet()
        gather.open(0)
        gather.open(1)
        tile = 256
        for part, ref in enumerate((q_out, k_out, v_out)):
            for j in range(width // tile):
                x = dot(tok_ref[...], wqkv_ref[:, part * width + j * tile:part * width + (j + 1) * tile]).astype(BF16)
                if part == 0:
                    x = x * jnp.asarray(HEAD_DIM ** -0.5, BF16)
                ref[:, j * tile:(j + 1) * tile] = x
                if part == 2 and j == 2:
                    pass_on(0)
        big = eye(256)
        for j in range(width // 256):
            cols = slice(j * 256, (j + 1) * 256)
            vt[cols, :] = dot_t(big, v_out[:, cols]).astype(BF16)
            pvt[cols, :] = dot_t(big, pv_ref[:, cols]).astype(BF16)
        ident = eye(QB)
        seg = jnp.broadcast_to(seg_ref[...].astype(F32), (QB, length)).astype(BF16)
        for j in range(length // QB):
            segc[j * QB:(j + 1) * QB, :] = dot_t(ident, seg[:, j * QB:(j + 1) * QB])

    for slot in range(1, length // QB):

        @pl.when(qb == slot)
        def _():
            pass_on(slot)

    start = pl.multiple_of(jnp.clip(qb * QB - QB, 0, length - window), QB)
    win = pl.ds(start, window)
    rows = pl.ds(pl.multiple_of(qb * QB, QB), QB)
    segq = seg_ref[:, rows].astype(F32)
    bias[...] = jnp.where(segc[win, :] == segq, 0.0, MASK_FILL)

    def score(pair):
        cols = slice(pair * PAIR, (pair + 1) * PAIR)
        keys = jnp.concatenate([k_out[win, cols], pk_ref[:, cols]], axis=0)
        sbuf[pair % 2] = dot_t(keys, split_heads(q_out[rows, cols]))

    def soft(pair):
        both = jnp.concatenate([bias[...], bias[...]], axis=1)
        sw = sbuf[pair % 2, :window] + both
        sp = sbuf[pair % 2, window:]
        top = jnp.maximum(jnp.max(sw, 0, keepdims=True), jnp.max(sp, 0, keepdims=True))
        ew = jnp.exp(sw - top)
        ep = jnp.exp(sp - top)
        inv = 1.0 / (jnp.sum(ew, 0, keepdims=True) + jnp.sum(ep, 0, keepdims=True))
        p_out[0, pair, :window] = (ew * inv).astype(BF16)
        p_out[0, pair, window:] = (ep * inv).astype(BF16)

    def mixing(pair):
        cols = slice(pair * PAIR, (pair + 1) * PAIR)
        vals = jnp.concatenate([vt[cols, win], pvt[cols, :]], axis=1)
        mixt[cols, rows] = own_blocks(dot(vals, p_out[0, pair])).astype(BF16)

    for i in range(pairs + 2):
        if i < pairs:
            score(i)
        if 0 <= i - 1 < pairs:
            soft(i - 1)
        if 0 <= i - 2 < pairs:
            mixing(i - 2)

    @pl.when(qb == pl.num_programs(0) - 1)
    def _():
        pass_on(8)
        big = eye(256)
        for r in range(length // 256):
            rr = slice(r * 256, (r + 1) * 256)
            mix_out[rr] = dot_t(big, mixt[:, rr]).astype(BF16)
        for r in range(length // 256):
            rr = slice(r * 256, (r + 1) * 256)
            res_out[rr] = tok_ref[rr].astype(F32) + dot(mix_out[rr], wo_ref[...]) + bo_ref[...]
        pass_on(9)
        for t in range(2):
            gather.finish(t)
        for t in range(2):
            gather.close(t)


def attend_forward(tok, wqkv, seg, pk, pv, wo, bo, up, down, group):
    length, width = tok.shape
    pre = pk.shape[0]
    window = 3 * QB
    pairs, blocks = width // PAIR, length // QB
    outs = [kept((length, width), BF16)] * 4 + [
        (pl.BlockSpec((1, pairs, window + pre, 2 * QB), lambda i: (i, 0, 0, 0)),
         jax.ShapeDtypeStruct((blocks, pairs, window + pre, 2 * QB), BF16)),
        kept((length, width), F32)]
    hbm = pl.BlockSpec(memory_space=pl.ANY)
    outs += [(hbm, jax.ShapeDtypeStruct((group,) + a.shape, BF16)) for a in (up, down)]
    count_b = group // (2 * LINE)
    pieces = len(gather_keys(count_b))
    return pl.pallas_call(
        functools.partial(forward_kernel, count_b),
        grid=(blocks,),
        in_specs=[whole(a) for a in (tok, wqkv, seg, pk, pv, wo, bo)] + [hbm, hbm],
        out_specs=[o[0] for o in outs],
        out_shape=[o[1] for o in outs],
        scratch_shapes=[
            pltpu.VMEM((width, length), BF16),
            pltpu.VMEM((width, pre), BF16),
            pltpu.VMEM((length, QB), F32),
            pltpu.VMEM((window, QB), F32),
            pltpu.VMEM((2, window + pre, 2 * QB), F32),
            pltpu.VMEM((width, length), BF16),
            pltpu.SemaphoreType.DMA((2, pieces)),
            pltpu.SemaphoreType.DMA((2, pieces)),
        ],
        compiler_params=pltpu.CompilerParams(vmem_limit_bytes=VMEM_LIMIT, collective_id=0, has_side_effects=True),
        name="attend_forward",
    )(tok, wqkv, seg, pk, pv, wo, bo, up, down)


def ffn_kernel(chunk, res_ref, dy_ref, up_hbm, down_hbm, up_own, down_own, wo_ref, db_ref, g1_ref, s1_ref, g2_ref, s2_ref,
               out_ref, gone_ref, gmix_ref, up, down, ub, pre, hid, slope, low, acc, hat_s, sems):
    step = pl.program_id(0)
    count = up.shape[1] // chunk
    width = up.shape[0]
    parts, _, part = up_hbm.shape

    me = lax.axis_index("mp")

    def fetch(d, t):
        cols = pl.ds(d * part, part)
        up_src, down_src = (up_own, down_own) if d == 0 else (up_hbm.at[(me + d) % parts], down_hbm.at[(me + d) % parts])
        src = (up_src.at[pl.ds(0, width)], up_src.at[pl.ds(width, BIAS_ROWS)], down_src)[t]
        dst = (up.at[:, cols], ub.at[:, cols], down.at[cols])[t]
        return pltpu.make_async_copy(src, dst, sems.at[t, d])

    @pl.when(step == 0)
    def _():
        for t in range(3):
            for d in range(parts):
                fetch(d, t).start()

    hat, inv1 = normalize(res_ref[...])
    hat_s[...] = hat
    low[...] = (hat * g1_ref[...] + s1_ref[...]).astype(BF16)

    @pl.when(step == 0)
    def _():
        for t in range(2):
            for d in range(parts):
                fetch(d, t).wait()

    def cols_of(j):
        return slice(j * chunk, (j + 1) * chunk)

    def rows_up(j):
        pre[j % 2] = dot(low[...], up[:, cols_of(j)])

    def act(j):
        u = pre[j % 2] + ub[0:1, cols_of(j)].astype(F32)
        half = 0.5 * lax.erf(u * ROOT_HALF) + 0.5
        hid[j % 2] = (u * half).astype(BF16)
        slope[:, cols_of(j)] = (half + u * (jnp.exp(-0.5 * u * u) * INV_ROOT_TWOPI)).astype(BF16)

    def rows_down(j):
        acc[...] += dot(hid[j % 2], down[cols_of(j)])

    acc[...] = jnp.zeros_like(acc)
    for j in range(count + 2):
        if j == 2:

            @pl.when(step == 0)
            def _():
                for d in range(parts):
                    fetch(d, 2).wait()

        if j < count:
            rows_up(j)
        if 0 <= j - 2 < count:
            rows_down(j - 2)
        if 0 <= j - 1 < count:
            act(j - 1)

    hat2, inv2 = normalize(hat_s[...] * g1_ref[...] + s1_ref[...] + acc[...] + db_ref[...])
    out_ref[...] = (hat2 * g2_ref[...] + s2_ref[...]).astype(BF16)
    grad_two = norm_back(dy_ref[...].astype(F32), hat2, inv2, g2_ref[...])
    acc[...] = grad_two
    low[...] = grad_two.astype(BF16)

    def back_down(j):
        gh = dot_t(low[...], down[cols_of(j)])
        hid[j % 2] = (gh * slope[:, cols_of(j)].astype(F32)).astype(BF16)

    def back_up(j):
        acc[...] += dot_t(hid[j % 2], up[:, cols_of(j)])

    for j in range(count + 1):
        if j < count:
            back_down(j)
        if j >= 1:
            back_up(j - 1)

    grad_one = norm_back(acc[...], hat_s[...], inv1, g1_ref[...])
    gone_ref[...] = grad_one
    gmix_ref[...] = dot_t(grad_one.astype(BF16), wo_ref[...]).astype(BF16)


def feed_forward(res, dy, up, down, up_own, down_own, wo, db, g1, s1, g2, s2, tb=256, chunk=512):
    rows, width = res.shape
    parts, ffl, _ = down.shape
    ff = parts * ffl
    block = pl.BlockSpec((tb, width), lambda i: (i, 0))
    hbm = pl.BlockSpec(memory_space=pl.ANY)
    return pl.pallas_call(
        functools.partial(ffn_kernel, chunk),
        grid=(rows // tb,),
        in_specs=[block, block] + [hbm] * 4 + [whole(a) for a in (wo, db, g1, s1, g2, s2)],
        out_specs=[block] * 3,
        out_shape=[jax.ShapeDtypeStruct((rows, width), t) for t in (BF16, F32, BF16)],
        scratch_shapes=[
            pltpu.VMEM((width, ff), BF16),
            pltpu.VMEM((ff, width), BF16),
            pltpu.VMEM((BIAS_ROWS, ff), BF16),
            pltpu.VMEM((2, tb, chunk), F32),
            pltpu.VMEM((2, tb, chunk), BF16),
            pltpu.VMEM((tb, ff), BF16),
            pltpu.VMEM((tb, width), BF16),
            pltpu.VMEM((tb, width), F32),
            pltpu.VMEM((tb, width), F32),
            pltpu.SemaphoreType.DMA((3, parts)),
        ],
        compiler_params=pltpu.CompilerParams(vmem_limit_bytes=VMEM_LIMIT),
        name="feed_forward",
    )(res, dy, up, down, up_own, down_own, wo, db, g1, s1, g2, s2)


class Total:
    def __init__(self, count_dp, count_mp, low, slots, parts, result, sems):
        self.low, self.slots, self.parts, self.result = low, slots, parts, result
        self.sems = sems
        self.count_b = count_mp // (2 * LINE)
        self.high_b, self.high_dp = self.count_b // 2, count_dp // 2
        self.count_q = LINE * self.high_b * self.high_dp
        dp, mp = lax.axis_index("dp"), lax.axis_index("mp")
        b = (mp // 2) % self.count_b
        a = mp // (2 * self.count_b)
        self.g = ((dp % 2) * 2 + b % 2) * 2 + mp % 2
        self.q = (a * self.high_b + b // 2) * self.high_dp + dp // 2

    def device(self, g, q):
        a, high = q // (self.high_b * self.high_dp), q % (self.high_b * self.high_dp)
        dp = (high % self.high_dp) * 2 + g // 4
        b = (high // self.high_dp) * 2 + (g // 2) % 2
        return dp, (a * self.count_b + b) * 2 + g % 2

    def near(self, j):
        return self.device((self.g + j) % 8, self.q)

    def far(self, i):
        return self.device(self.g, (self.q + i) % self.count_q)

    def copy(self, phase, j, arriving=False):
        if phase == 0:
            src, dst, to = self.low.at[(self.g + j) % 8], self.slots.at[j], self.near(j)
        elif phase == 1:
            at = (self.q + self.count_q - j) % self.count_q if arriving else self.q
            src, dst, to = self.parts.at[at], self.parts.at[at], self.far(j)
        else:
            at = (self.g + 8 - j) % 8 if arriving else self.g
            src, dst, to = self.result.at[at], self.result.at[at], self.near(j)
        send, recv = self.sems[phase]
        return pltpu.make_async_remote_copy(
            src_ref=src, dst_ref=dst, send_sem=send.at[j], recv_sem=recv.at[j], device_id=to,
            device_id_type=pl.DeviceIdType.MESH)

    def peers(self, phase):
        return range(1, self.count_q if phase == 1 else 8)

    def greet(self):
        barrier = pltpu.get_barrier_semaphore()
        partners = [self.near(j) for j in self.peers(0)] + [self.far(i) for i in self.peers(1)]
        for device in partners:
            pl.semaphore_signal(barrier, inc=1, device_id=device, device_id_type=pl.DeviceIdType.MESH)
        pl.semaphore_wait(barrier, len(partners))

    def start(self, phase):
        for j in self.peers(phase):
            self.copy(phase, j).start()

    def arrive(self, phase):
        for j in self.peers(phase):
            self.copy(phase, j, True).wait_recv()

    def first(self):
        self.greet()
        self.start(0)

    def second(self):
        self.arrive(0)
        total = self.low[self.g].astype(F32)
        for j in self.peers(0):
            total = total + self.slots[j].astype(F32)
        self.parts[self.q] = total.astype(BF16)
        self.start(1)

    def third(self):
        self.arrive(1)
        total = self.parts[0].astype(F32)
        for i in range(1, self.count_q):
            total = total + self.parts[i].astype(F32)
        self.result[self.g] = total.astype(BF16)
        self.start(2)

    def last(self):
        self.arrive(2)
        for phase in range(3):
            for j in self.peers(phase):
                self.copy(phase, j).wait_send()


def backward_kernel(counts, p_ref, q_ref, k_ref, v_ref, mix_ref, do_ref, pk_ref, pv_ref, w_ref, gone_ref,
                    out_ref, gk_ref, gv_ref, kt, dk, dv, gj, delta, gbuf, ds_all, dqt, low, slots, parts, result,
                    send0, recv0, send1, recv1, send2, recv2):
    pair = pl.program_id(0)
    length = q_ref.shape[0]
    pre = pk_ref.shape[0]
    pairs, width = ds_all.shape[0], out_ref.shape[1]
    blocks = length // QB
    depth = p_ref.shape[2]
    window = depth - pre
    ident = eye(QB)
    sub = lax.broadcasted_iota(jnp.int32, (8, PAIR), 0)
    lane = lax.broadcasted_iota(jnp.int32, (8, PAIR), 1)
    pick = jnp.where((sub == 0) == (lane < HEAD_DIM), 1.0, 0.0).astype(BF16)
    dk[...] = jnp.zeros_like(dk)
    dv[...] = jnp.zeros_like(dv)
    kt[pair, :, :length] = dot_t(ident, k_ref[...]).astype(BF16)
    kt[pair, :, length:] = dot_t(ident, pk_ref[...]).astype(BF16)
    prod = do_ref[...].astype(F32) * mix_ref[...].astype(F32)
    high = prod.astype(BF16)
    rest = (prod - high.astype(F32)).astype(BF16)
    delta[...] = dot_t(pick, high) + dot_t(pick, rest)

    def where_of(qb):
        start = min(max(qb * QB - QB, 0), length - window)
        return slice(start, start + window), slice(qb * QB, (qb + 1) * QB)

    def grad_probs(qb):
        win, rows = where_of(qb)
        vals = jnp.concatenate([v_ref[win], pv_ref[...]], axis=0)
        gbuf[qb % 2] = dot_t(vals, split_heads(do_ref[rows]))

    def grad_scores(qb):
        win, rows = where_of(qb)
        d = jnp.concatenate([delta[0:1, rows], delta[1:2, rows]], axis=1)
        ds_all[pair, qb] = (p_ref[qb, 0].astype(F32) * (gbuf[qb % 2] - d)).astype(BF16)

    def grads(qb):
        win, rows = where_of(qb)
        dva = dot(p_ref[qb, 0], split_heads(do_ref[rows]))
        dv[win] += dva[:window]
        dv[length:] += dva[window:]
        dka = dot(ds_all[pair, qb], split_heads(q_ref[rows]))
        dk[win] += dka[:window]
        dk[length:] += dka[window:]

    for i in range(blocks + 2):
        if i < blocks:
            grad_probs(i)
        if 0 <= i - 1 < blocks:
            grad_scores(i - 1)
        if 0 <= i - 2 < blocks:
            grads(i - 2)
    gj[pair, :, 0:PAIR] = dk[:length].astype(BF16)
    gj[pair, :, PAIR:] = dv[:length].astype(BF16)
    cols = pl.ds(pl.multiple_of(pair * PAIR, PAIR), PAIR)
    each = 2 * pre // 8
    for part, ref in enumerate((dk, dv)):
        for i in range(4):
            low[part * 4 + i, :, cols] = ref[length + i * each:length + (i + 1) * each].astype(BF16)

    @pl.when(pair == pl.num_programs(0) - 1)
    def _():
        total = Total(*counts, low, slots, parts, result, ((send0, recv0), (send1, recv1), (send2, recv2)))
        total.first()

        def query_grads(i, carry):
            rows_of = pl.ds(pl.multiple_of(i * PAIR, PAIR), PAIR)
            for qb in range(blocks):
                win, rows = where_of(qb)
                keys = jnp.concatenate([kt[i, :, win], kt[i, :, length:]], axis=1)
                dqt[rows_of, rows] = own_blocks(dot(keys, ds_all[i, qb]) * HEAD_DIM ** -0.5).astype(BF16)
            return carry

        lax.fori_loop(0, pairs // 2, query_grads, 0)
        total.second()
        lax.fori_loop(pairs // 2, pairs, query_grads, 0)
        total.third()
        big = eye(256)
        for r in range(length // 256):
            rr = slice(r * 256, (r + 1) * 256)
            acc = gone_ref[rr] + dot_t(dot_t(big, dqt[:, rr]).astype(BF16), w_ref[:, :width])
            for part in range(2):
                x = jnp.concatenate([gj[i, rr, part * PAIR:(part + 1) * PAIR] for i in range(pairs)], axis=1)
                acc = acc + dot_t(x, w_ref[:, (part + 1) * width:(part + 2) * width])
            out_ref[rr] = acc.astype(BF16)
        total.last()
        for i in range(4):
            gk_ref[i * each:(i + 1) * each] = result[i].astype(F32)
            gv_ref[i * each:(i + 1) * each] = result[4 + i].astype(F32)


def attend_backward(p, q, k, v, mix, do, pk, pv, wqkv, gone, counts):
    length, width = q.shape
    pre = pk.shape[0]
    blocks, pairs, depth, _ = p.shape

    def col(a):
        return pl.BlockSpec((a.shape[0], PAIR), lambda i: (0, i))

    outs = [kept((length, width), BF16)] + [kept((pre, width), F32)] * 2
    count_q = counts[0] * counts[1] // 8
    piece = (2 * pre // 8, width)
    return pl.pallas_call(
        functools.partial(backward_kernel, counts),
        grid=(pairs,),
        in_specs=[pl.BlockSpec((blocks, 1, depth, 2 * QB), lambda i: (0, i, 0, 0))]
        + [col(a) for a in (q, k, v, mix, do, pk, pv)] + [whole(wqkv), whole(gone)],
        out_specs=[o[0] for o in outs],
        out_shape=[o[1] for o in outs],
        scratch_shapes=[
            pltpu.VMEM((pairs, PAIR, length + pre), BF16),
            pltpu.VMEM((length + pre, PAIR), F32),
            pltpu.VMEM((length + pre, PAIR), F32),
            pltpu.VMEM((pairs, length, 2 * PAIR), BF16),
            pltpu.VMEM((8, length), F32),
            pltpu.VMEM((2, depth, 2 * QB), F32),
            pltpu.VMEM((pairs, blocks, depth, 2 * QB), BF16),
            pltpu.VMEM((width, length), BF16),
            pltpu.VMEM((8,) + piece, BF16),
            pltpu.VMEM((8,) + piece, BF16),
            pltpu.VMEM((count_q,) + piece, BF16),
            pltpu.VMEM((8,) + piece, BF16),
        ] + [pltpu.SemaphoreType.DMA((n,)) for n in (8, 8, count_q, count_q, 8, 8)],
        compiler_params=pltpu.CompilerParams(vmem_limit_bytes=VMEM_LIMIT, collective_id=1, has_side_effects=True),
        name="attend_backward",
    )(p, q, k, v, mix, do, pk, pv, wqkv, gone)


def on_device(counts, tokens, segment_ids, qkv_weight, prefix_keys, prefix_values, out_weight, out_bias, norm1_gain,
              norm1_shift, up_weight, up_bias, down_weight, down_bias, norm2_gain, norm2_shift, out_grad):
    row = lambda a: a.reshape(1, -1)
    up_part = jnp.concatenate([up_weight, jnp.broadcast_to(row(up_bias), (BIAS_ROWS, up_bias.shape[0]))], axis=0)
    q, k, v, mix, probs, res, up_all, down_all = attend_forward(
        tokens[0], qkv_weight, segment_ids, prefix_keys, prefix_values, out_weight, row(out_bias), up_part, down_weight, counts[1])
    out, grad_one, grad_mixed = feed_forward(
        res, out_grad[0], up_all, down_all, up_part, down_weight, out_weight, row(down_bias), row(norm1_gain), row(norm1_shift),
        row(norm2_gain), row(norm2_shift))
    grad_tokens, total_k, total_v = attend_backward(
        probs, q, k, v, mix, grad_mixed, prefix_keys, prefix_values, qkv_weight, grad_one, counts)
    return out[None], grad_tokens[None], total_k, total_v


def solution(mesh):
    rows = P(("dp", "mp"), None, None)
    return jax.shard_map(
        functools.partial(on_device, (mesh.shape["dp"], mesh.shape["mp"])),
        mesh=mesh,
        in_specs=(rows, P(("dp", "mp"), None), P(), P(), P(), P(), P(), P(), P(), P(None, "mp"), P("mp"), P("mp", None),
                  P(), P(), P(), rows),
        out_specs=(rows, rows, P(), P()),
        check_vma=False,
    )
```

```python
import functools

import jax
import jax.numpy as jnp
from jax import lax
from jax.experimental import pallas as pl
from jax.experimental.pallas import tpu as pltpu
from jax.sharding import PartitionSpec as P

EPSILON = 1e-05
ROOT_HALF = 0.7071067811865476
INV_ROOT_TWOPI = 0.3989422804014327
MASK_FILL = -1e30
HEAD_DIM = 64
PAIR = 2 * HEAD_DIM
QB = 128
F32 = jnp.float32
BF16 = jnp.bfloat16
VMEM_LIMIT = 62 * 1024 * 1024
BIAS_ROWS = 32
GATHER_SLOTS = (
    (0, 0, 0, True), (0, 0, 0, False),
    (2, 1, 0, True), (2, 1, 0, False),
    (4, 0, 1, True),
    (6, 1, 1, True), (6, 0, 1, False),
    (7, 0, 2, True),
    (8, 1, 1, False),
    (9, 1, 2, True), (9, 0, 2, False),
    (11, 0, 3, True), (11, 1, 2, False),
    (12, 1, 3, True), (12, 0, 3, False),
    (13, 1, 3, False),
    (14, 0, 4, True), (14, 1, 4, True),
    (15, 0, 4, False), (15, 1, 4, False),
)


def dot(a, b):
    return lax.dot_general(a, b, (((1,), (0,)), ((), ())), preferred_element_type=F32)


def dot_t(a, b):
    return lax.dot_general(a, b, (((1,), (1,)), ((), ())), preferred_element_type=F32)


def eye(n):
    r = lax.broadcasted_iota(jnp.int32, (n, n), 0)
    c = lax.broadcasted_iota(jnp.int32, (n, n), 1)
    return jnp.where(r == c, 1.0, 0.0).astype(BF16)


def split_heads(x):
    lane = lax.broadcasted_iota(jnp.int32, x.shape, 1)
    zero = jnp.zeros_like(x)
    return jnp.concatenate([jnp.where(lane < HEAD_DIM, x, zero), jnp.where(lane < HEAD_DIM, zero, x)], axis=0)


def own_blocks(x):
    return jnp.concatenate([x[:HEAD_DIM, :QB], x[HEAD_DIM:, QB:]], axis=0)


def normalize(x):
    scale = 1.0 / x.shape[-1]
    cen = x - jnp.sum(x, -1, keepdims=True) * scale
    inv = lax.rsqrt(jnp.sum(cen * cen, -1, keepdims=True) * scale + EPSILON)
    return cen * inv, inv


def norm_back(grad, hat, inv, gain):
    scale = 1.0 / grad.shape[-1]
    sc = grad * gain
    mean1 = jnp.sum(sc, -1, keepdims=True) * scale
    mean2 = jnp.sum(sc * hat, -1, keepdims=True) * scale
    return (sc - mean1 - hat * mean2) * inv


def whole(a):
    return pl.BlockSpec(a.shape, lambda i: (0,) * a.ndim, pipeline_mode=pl.Buffered(1))


def kept(shape, dtype):
    spec = pl.BlockSpec(shape, lambda i: (0,) * len(shape), pipeline_mode=pl.Buffered(1))
    return spec, jax.ShapeDtypeStruct(shape, dtype)


LINE = 4


def flip(x, bits):
    bit = 1
    while bit <= bits:
        if bits & bit:
            x = x + bit - 2 * bit * ((x // bit) % 2)
        bit *= 2
    return x


def guarded(condition, body):
    if condition is None:
        body()
    else:
        pl.when(condition)(body)


def gather_keys(count_b):
    others = range(1, count_b)
    keys = [("z", side, d, 0) for side in (1, -1) for d in (1, 2, 3)]
    keys += [("z", side, d, 1) for side in (1, -1) for d in (1, 2)]
    for s in others:
        keys += [("x", s, d, 0) for d in (0, 1, -1, 2, 3)] + [("x", s, 3, 1)]
        keys += [("y", s, d, 0) for d in (0, 1, -1, 2)]
    keys.append(("y", 0, 3, 0))
    keys.append(("core", 0, 0, None))
    for s in range(count_b):
        keys += [("core", s, d, part) for d in (0, 1, -1, 2, 3) for part in (0, 1) if (s, d) != (0, 0)]
    return {key: i for i, key in enumerate(keys)}


def gather_events(count_b):
    others = range(1, count_b)
    sides = (1, -1)
    return [
        [("x", s, 0, 0) for s in others] + [("z", side, 1, 0) for side in sides],
        [("z", side, 2, 0) for side in sides] + [("x", s, d, 0) for s in others for d in sides] + [("y", s, 0, 0) for s in others],
        [("z", side, 3, 0) for side in sides] + [("x", s, 2, 0) for s in others] + [("y", s, d, 0) for s in others for d in sides],
        [("z", side, 1, 1) for side in sides] + [("y", 0, 3, 0)] + [("x", s, 3, 0) for s in others],
        [("z", side, 2, 1) for side in sides] + [("y", s, 2, 0) for s in others] + [("x", s, 3, 1) for s in others],
    ]


class Gather:
    def __init__(self, count_b, inputs, alls, sems):
        self.count_b = count_b
        self.inputs, self.alls = inputs, alls
        self.send, self.recv = sems
        self.dp = lax.axis_index("dp")
        self.mp = lax.axis_index("mp")
        self.core = self.mp % 2
        self.b = (self.mp // 2) % self.count_b
        self.a = self.mp // (2 * self.count_b)
        self.half = self.dp % 2
        self.keys = gather_keys(count_b)

    def index(self, a, s, other=False):
        core = 1 - self.core if other else self.core
        return (a * self.count_b + flip(self.b, s)) * 2 + core

    def at(self, d):
        if d in (2, 3):
            return self.a + d - 2 * d * ((self.a + d) // LINE)
        return self.a + d

    def inside(self, d):
        if d == 1:
            return self.a < LINE - 1
        if d == -1:
            return self.a > 0
        if d == 3:
            return self.a % 3 == 0
        return None

    def gets(self, key):
        kind, s, d, part = key
        if kind != "z":
            return self.inside(d)
        return self.a + d < LINE if s == 1 else self.a >= d

    def sends(self, key):
        kind, s, d, part = key
        if kind != "z":
            return self.inside(d)
        low, high = (1, LINE - d) if s == 1 else (d - 1, LINE - 2)
        return (self.a >= low) & (self.a <= high)

    def copy(self, t, key, arriving):
        kind, s, d, part = key
        own = d == 0 and not arriving
        if kind == "z":
            own = d == 1 and not arriving
            target = (self.dp, self.index(self.a - s, 0))
            chunk = self.index(self.a + s * d, 0) if arriving else self.index(self.a + s * (d - 1), 0)
        elif kind == "x":
            target = (self.dp, self.index(self.a, s))
            chunk = self.index(self.at(d), s if arriving else 0)
        elif kind == "y":
            target = (flip(self.dp, 1), self.mp)
            chunk = self.index(self.at(d), s)
            own = False
        else:
            target = (self.dp, self.index(self.a, 0, True))
            chunk = self.index(self.at(d), s, arriving)
            own = own and s == 0
        ref = self.alls[t]
        rows = ref.shape[1]
        if part is None:
            span = pl.ds(0, rows)
        else:
            which = 1 - part if kind == "y" and arriving else part
            which = self.half if which == 0 else 1 - self.half
            span = pl.ds(pl.multiple_of(which * (rows // 2), 16), rows // 2)
        src = self.inputs[t].at[span] if own else ref.at[chunk, span]
        number = self.keys[key]
        return pltpu.make_async_remote_copy(
            src_ref=src, dst_ref=ref.at[chunk, span], send_sem=self.send.at[t, number], recv_sem=self.recv.at[t, number],
            device_id=target, device_id_type=pl.DeviceIdType.MESH)

    def start(self, t, *key):
        guarded(self.sends(key), lambda: self.copy(t, key, False).start())

    def arrive(self, t, key):
        self.copy(t, key, True).wait_recv()

    def greet(self):
        barrier = pltpu.get_barrier_semaphore()
        partners = [(self.inside(d), (self.dp, self.index(self.a + d, 0))) for d in (1, -1)]
        partners += [(None, (self.dp, self.index(self.a, s))) for s in range(1, self.count_b)]
        partners += [(None, (self.dp, self.index(self.a, 0, True))), (None, (flip(self.dp, 1), self.mp))]
        for condition, device in partners:
            guarded(condition, lambda: pl.semaphore_signal(
                barrier, inc=1, device_id=device, device_id_type=pl.DeviceIdType.MESH))
        ends = 1 - (self.a % 3 + 1) // 2
        pl.semaphore_wait(barrier, len(partners) - ends)

    def open(self, t):
        for side in (1, -1):
            self.start(t, "z", side, 1, 0)
        for s in range(1, self.count_b):
            self.start(t, "x", s, 0, 0)
        self.start(t, "core", 0, 0, None)

    def pass_on(self, t, key):
        kind, s, d, part = key

        def body():
            self.arrive(t, key)
            if kind == "z":
                if d < (3 if part == 0 else 2):
                    self.start(t, "z", s, d + 1, part)
                at = s if d == 1 else d
                if part == 0:
                    for other in range(1, self.count_b):
                        self.start(t, "x", other, at, 0)
                    if d == 3:
                        self.start(t, "y", 0, 3, 0)
                self.start(t, "core", 0, at, part)
            elif kind == "x":
                if d != 3:
                    self.start(t, "y", s, d, 0)
                self.start(t, "core", s, d, part)
            else:
                if d == 3:
                    for other in range(1, self.count_b):
                        self.start(t, "x", other, 3, 1)
                self.start(t, "core", s, d, 1)

        guarded(self.gets(key), body)

    def level(self, t, n, along):
        for key in gather_events(self.count_b)[n]:
            if (key[0] == "z") == along:
                self.pass_on(t, key)
        if along and n < LINE - 1:
            for side in (1, -1):
                sent = LINE - 1 - self.a if side == 1 else self.a
                pl.when(sent == n)(lambda: self.start(t, "z", side, 1, 1))

    def from_core(self, n, along):
        keys = []
        for kind, s, d, part in gather_events(self.count_b)[n]:
            if (kind == "z") == along:
                if kind == "z":
                    key = ("core", 0, s if d == 1 else d, part)
                else:
                    key = ("core", s, d, 1 if kind == "y" else part)
                if key not in keys:
                    keys.append(key)
        for t in range(2):
            for key in keys:
                guarded(self.gets(key), lambda: self.arrive(t, key))

    def chip(self, o):
        n = self.count_b - 1
        end = self.a % 3 == 0
        one, two, three = 1 + n, 1 + 2 * n, 4 + 2 * n
        rank = jnp.where(o < one, 0, jnp.where(o <= two, 1, jnp.where(o == two + 1, jnp.where(end, 3, 2), jnp.where(
            o == two + 2, jnp.where(end, 2, 3), jnp.where(o < three + n, 2, 3)))))
        s = jnp.where(o < one, o, jnp.where(o < two, o - one + 1, jnp.where(o < three, 0, jnp.where(
            o < three + n, o - three + 1, o - three - n + 1))))
        a = jnp.where(rank == 0, self.a, jnp.where(rank == 1, 1 + self.a % 2, jnp.where(
            rank == 2, (2 + 3 * self.a) % 5, 3 - 3 * (self.a // 2))))
        return a * self.count_b + (self.b + s) % self.count_b

    def close(self, t):
        for key in self.keys:
            guarded(self.sends(key), lambda: self.copy(t, key, False).wait_send())


def forward_kernel(count_b, tok_ref, wqkv_hbm, seg_ref, pk_ref, pv_ref, wo_ref, bo_ref, g1_ref, s1_ref, db_ref, up_in, down_in,
                   q_hbm, k_hbm, v_hbm, mix_hbm, p_out, res_hbm, two_hbm, up_all, down_all, slope_out,
                   q_out, k_out, v_out, mix_out, res_out, two, wqkv_ref, vt, pvt, segc, bias, sbuf, mixt, low, up_v, down_v, pre, hid, slope, send, recv, wsem, qsem, osem, xsem):
    qb = pl.program_id(0)

    def copy_out(n):
        src = (q_out, k_out, v_out, mix_out, res_out, two)[n]
        return pltpu.make_async_copy(src, (q_hbm, k_hbm, v_hbm, mix_hbm, res_hbm, two_hbm)[n], xsem.at[n])

    gather = Gather(count_b, (up_in, down_in), (up_all, down_all), (send, recv))

    def pass_on(now):
        for slot, t, n, along in GATHER_SLOTS:
            if slot == now:
                gather.level(t, n, along)

    length, width = tok_ref.shape
    window = bias.shape[0]
    pairs = width // PAIR

    @pl.when(qb == 0)
    def _():
        def weights(part):
            cols = pl.ds(part * width, width)
            return pltpu.make_async_copy(wqkv_hbm.at[:, cols], wqkv_ref.at[:, cols], qsem.at[part])

        for part in range(3):
            weights(part).start()
        gather.greet()
        gather.open(0)
        gather.open(1)
        tile = 256
        for part, ref in enumerate((q_out, k_out, v_out)):
            weights(part).wait()
            for j in range(width // tile):
                x = dot(tok_ref[...], wqkv_ref[:, part * width + j * tile:part * width + (j + 1) * tile]).astype(BF16)
                if part == 0:
                    x = x * jnp.asarray(HEAD_DIM ** -0.5, BF16)
                ref[:, j * tile:(j + 1) * tile] = x
            copy_out(part).start()
        big = eye(256)
        for j in range(width // 256):
            cols = slice(j * 256, (j + 1) * 256)
            vt[cols, :] = dot_t(big, v_out[:, cols]).astype(BF16)
            pvt[cols, :] = dot_t(big, pv_ref[:, cols]).astype(BF16)
        pass_on(0)
        ident = eye(QB)
        seg = jnp.broadcast_to(seg_ref[...].astype(F32), (QB, length)).astype(BF16)
        for j in range(length // QB):
            segc[j * QB:(j + 1) * QB, :] = dot_t(ident, seg[:, j * QB:(j + 1) * QB])

    for slot in range(1, length // QB):

        @pl.when(qb == slot)
        def _():
            pass_on(slot)

    start = pl.multiple_of(jnp.clip(qb * QB - QB, 0, length - window), QB)
    win = pl.ds(start, window)
    rows = pl.ds(pl.multiple_of(qb * QB, QB), QB)
    segq = seg_ref[:, rows].astype(F32)
    bias[...] = jnp.where(segc[win, :] == segq, 0.0, MASK_FILL)

    def score(pair):
        cols = slice(pair * PAIR, (pair + 1) * PAIR)
        keys = jnp.concatenate([k_out[win, cols], pk_ref[:, cols]], axis=0)
        sbuf[pair % 2] = dot_t(keys, split_heads(q_out[rows, cols]))

    def soft(pair):
        both = jnp.concatenate([bias[...], bias[...]], axis=1)
        sw = sbuf[pair % 2, :window] + both
        sp = sbuf[pair % 2, window:]
        top = jnp.maximum(jnp.max(sw, 0, keepdims=True), jnp.max(sp, 0, keepdims=True))
        ew = jnp.exp(sw - top)
        ep = jnp.exp(sp - top)
        inv = 1.0 / (jnp.sum(ew, 0, keepdims=True) + jnp.sum(ep, 0, keepdims=True))
        p_out[0, pair, :window] = (ew * inv).astype(BF16)
        p_out[0, pair, window:] = (ep * inv).astype(BF16)

    def mixing(pair):
        cols = slice(pair * PAIR, (pair + 1) * PAIR)
        vals = jnp.concatenate([vt[cols, win], pvt[cols, :]], axis=1)
        mixt[cols, rows] = own_blocks(dot(vals, p_out[0, pair])).astype(BF16)

    for i in range(pairs + 2):
        if i < pairs:
            score(i)
        if 0 <= i - 1 < pairs:
            soft(i - 1)
        if 0 <= i - 2 < pairs:
            mixing(i - 2)

    @pl.when(qb == pl.num_programs(0) - 1)
    def _():
        pass_on(8)
        big = eye(256)
        for r in range(length // 256):
            rr = slice(r * 256, (r + 1) * 256)
            mix_out[rr] = dot_t(big, mixt[:, rr]).astype(BF16)
        copy_out(3).start()
        for r in range(length // 256):
            rr = slice(r * 256, (r + 1) * 256)
            res = tok_ref[rr].astype(F32) + dot(mix_out[rr], wo_ref[...]) + bo_ref[...]
            res_out[rr] = res
            first = normalize(res)[0] * g1_ref[...] + s1_ref[...]
            low[rr] = first.astype(BF16)
            two[rr] = first + db_ref[...]
        copy_out(4).start()
        pass_on(9)

        chips = LINE * count_b
        ffl = down_in.shape[0]
        per = length // 256

        def loads(o):
            chip = gather.chip(o)
            out = []
            for c in range(2):
                core = gather.core if c else 1 - gather.core
                cols = pl.ds(pl.multiple_of(core * ffl, 128), ffl)
                own = isinstance(o, int) and o == 0 and c == 1
                for t, to in ((0, up_v.at[o % 3, :, cols]), (1, down_v.at[o % 3, cols])):
                    src = (up_in, down_in)[t] if own else (up_all, down_all)[t].at[2 * chip + core]
                    out.append(pltpu.make_async_copy(src, to, wsem.at[o % 3, t, c]))
            return out

        def load(o):
            for copy in loads(o):
                copy.start()

        def loaded(o):
            for copy in loads(o):
                copy.wait()

        def rows_of(b):
            return slice(b * 256, (b + 1) * 256)

        def up(o, b):
            pre[b % 2] = dot(low[rows_of(b)], up_v[o % 3, :width, :])

        def act(o, b):
            u = pre[b % 2] + up_v[o % 3, width:width + 1, :].astype(F32)
            half = 0.5 * lax.erf(u * ROOT_HALF) + 0.5
            hid[b % 2] = (u * half).astype(BF16)
            slope[o, rows_of(b)] = (half + u * (jnp.exp(-0.5 * u * u) * INV_ROOT_TWOPI)).astype(BF16)

        def down(o, b):
            two[rows_of(b)] += dot(hid[b % 2], down_v[o % 3])

        def earlier(o, b, n):
            return (o, b - n) if b >= n else (o - 1, b - n + per)

        def chip_steps(o, ahead):
            loaded(o)
            for b in range(per):
                if b == 2:
                    ahead()
                up(o, b)
                if b >= 1 or not (isinstance(o, int) and o == 0):
                    act(*earlier(o, b, 1))
                if b >= 2 or not (isinstance(o, int) and o == 0):
                    down(*earlier(o, b, 2))

        def keep(o):
            return pltpu.make_async_copy(slope.at[o], slope_out.at[gather.chip(o)], osem.at[o])

        def more():
            pass_on(10)
            for n in range(2):
                for along in (True, False):
                    gather.from_core(n, along)

        for t in range(2):
            gather.arrive(t, ("core", 0, 0, None))
        load(0)

        def first_ahead():
            more()
            load(1)

        chip_steps(0, first_ahead)
        others = count_b - 1
        needs = ((others, 11, 2, (True, False)), (2 * others, 12, 3, (True,)), (2 * others + 1, 13, 3, (False,)),
                 (2 * others + 2, 14, 4, (True,)), (2 * others + 3, 15, 4, (False,)))

        def chip_step(o, carry):
            def ahead():
                for at, slot, n, kinds in needs:

                    @pl.when(o == at)
                    def _():
                        pass_on(slot)
                        for along in kinds:
                            gather.from_core(n, along)

                @pl.when(o < chips - 1)
                def _():
                    load(o + 1)

            chip_steps(o, ahead)
            return carry

        lax.fori_loop(1, chips, chip_step, 0)
        act(chips - 1, per - 1)
        down(chips - 1, per - 2)
        down(chips - 1, per - 1)
        copy_out(5).start()
        for o in range(chips):
            keep(o).start()
        for t in range(2):
            gather.close(t)
        for o in range(chips):
            keep(o).wait()
        for n in range(6):
            copy_out(n).wait()


def attend_forward(tok, wqkv, seg, pk, pv, wo, bo, g1, s1, db, up, down, group):
    length, width = tok.shape
    pre = pk.shape[0]
    window = 3 * QB
    pairs, blocks = width // PAIR, length // QB
    hbm = pl.BlockSpec(memory_space=pl.ANY)
    square, wide = jax.ShapeDtypeStruct((length, width), BF16), jax.ShapeDtypeStruct((length, width), F32)
    outs = [(hbm, square)] * 4 + [
        (pl.BlockSpec((1, pairs, window + pre, 2 * QB), lambda i: (i, 0, 0, 0)),
         jax.ShapeDtypeStruct((blocks, pairs, window + pre, 2 * QB), BF16)),
        (hbm, wide), (hbm, wide)]
    outs += [(hbm, jax.ShapeDtypeStruct((group,) + a.shape, BF16)) for a in (up, down)]
    chips, part = group // 2, 2 * down.shape[0]
    outs += [(hbm, jax.ShapeDtypeStruct((chips, length, part), BF16))]
    count_b = group // (2 * LINE)
    pieces = len(gather_keys(count_b))
    return pl.pallas_call(
        functools.partial(forward_kernel, count_b),
        grid=(blocks,),
        in_specs=[whole(tok), hbm] + [whole(a) for a in (seg, pk, pv, wo, bo, g1, s1, db)] + [hbm, hbm],
        out_specs=[o[0] for o in outs],
        out_shape=[o[1] for o in outs],
        scratch_shapes=[pltpu.VMEM((length, width), t) for t in (BF16, BF16, BF16, BF16, F32, F32)] + [
            pltpu.VMEM(wqkv.shape, BF16),
            pltpu.VMEM((width, length), BF16),
            pltpu.VMEM((width, pre), BF16),
            pltpu.VMEM((length, QB), F32),
            pltpu.VMEM((window, QB), F32),
            pltpu.VMEM((2, window + pre, 2 * QB), F32),
            pltpu.VMEM((width, length), BF16),
            pltpu.VMEM((length, width), BF16),
            pltpu.VMEM((3, up.shape[0], part), BF16),
            pltpu.VMEM((3, part, width), BF16),
            pltpu.VMEM((2, 256, part), F32),
            pltpu.VMEM((2, 256, part), BF16),
            pltpu.VMEM((chips, length, part), BF16),
            pltpu.SemaphoreType.DMA((2, pieces)),
            pltpu.SemaphoreType.DMA((2, pieces)),
            pltpu.SemaphoreType.DMA((3, 2, 2)),
            pltpu.SemaphoreType.DMA((3,)),
            pltpu.SemaphoreType.DMA((chips,)),
            pltpu.SemaphoreType.DMA((6,)),
        ],
        compiler_params=pltpu.CompilerParams(vmem_limit_bytes=VMEM_LIMIT, collective_id=0, has_side_effects=True),
        name="attend_forward",
    )(tok, wqkv, seg, pk, pv, wo, bo, g1, s1, db, up, down)


def ffn_kernel(res_ref, two_ref, dy_ref, slope_ref, up_hbm, down_hbm, up_own, down_own, wo_ref, g1_ref, g2_ref, s2_ref,
               out_ref, gone_ref, gmix_ref, up, down, hid, low, acc, sems):
    step = pl.program_id(0)
    width = up.shape[0]
    parts, part, _ = down_hbm.shape
    count, _, chunk = slope_ref.shape
    me = lax.axis_index("mp")

    def fetch(d, t, own):
        cols = pl.ds(d * part, part)
        up_src, down_src = (up_own, down_own) if own else (up_hbm.at[d], down_hbm.at[d])
        src, dst = ((up_src.at[pl.ds(0, width)], up.at[:, cols]), (down_src, down.at[cols]))[t]
        return pltpu.make_async_copy(src, dst, sems.at[t, d])

    @pl.when(step == 0)
    def _():
        for t in (1, 0):
            for d in range(parts):

                @pl.when(me == d)
                def _():
                    fetch(d, t, True).start()

                @pl.when(me != d)
                def _():
                    fetch(d, t, False).start()

    hat2, inv2 = normalize(two_ref[...])
    out_ref[...] = (hat2 * g2_ref[...] + s2_ref[...]).astype(BF16)
    grad_two = norm_back(dy_ref[...].astype(F32), hat2, inv2, g2_ref[...])
    acc[...] = grad_two
    low[...] = grad_two.astype(BF16)

    @pl.when(step == 0)
    def _():
        for d in range(parts):
            fetch(d, 1, False).wait()

    def cols_of(j):
        return slice(j * chunk, (j + 1) * chunk)

    def back_down(j):
        gh = dot_t(low[...], down[cols_of(j)])
        hid[j % 2] = (gh * slope_ref[j].astype(F32)).astype(BF16)

    def back_up(j):
        acc[...] += dot_t(hid[j % 2], up[:, cols_of(j)])

    for j in range(count + 1):
        if j < count:
            back_down(j)
        if j == 1:

            @pl.when(step == 0)
            def _():
                for d in range(parts):
                    fetch(d, 0, False).wait()

        if j >= 1:
            back_up(j - 1)

    hat, inv1 = normalize(res_ref[...])
    grad_one = norm_back(acc[...], hat, inv1, g1_ref[...])
    gone_ref[...] = grad_one
    gmix_ref[...] = dot_t(grad_one.astype(BF16), wo_ref[...]).astype(BF16)


def feed_forward_backward(res, two, dy, slope, up, down, up_own, down_own, wo, g1, g2, s2, tb=256):
    rows, width = res.shape
    parts, ffl, _ = down.shape
    ff = parts * ffl
    chips, _, part = slope.shape
    block = pl.BlockSpec((tb, width), lambda i: (i, 0))
    hbm = pl.BlockSpec(memory_space=pl.ANY)
    return pl.pallas_call(
        ffn_kernel,
        grid=(rows // tb,),
        in_specs=[block] * 3 + [pl.BlockSpec((chips, tb, part), lambda i: (0, i, 0))] + [hbm] * 4
        + [whole(a) for a in (wo, g1, g2, s2)],
        out_specs=[block] * 3,
        out_shape=[jax.ShapeDtypeStruct((rows, width), t) for t in (BF16, F32, BF16)],
        scratch_shapes=[
            pltpu.VMEM((width, ff), BF16),
            pltpu.VMEM((ff, width), BF16),
            pltpu.VMEM((2, tb, part), BF16),
            pltpu.VMEM((tb, width), BF16),
            pltpu.VMEM((tb, width), F32),
            pltpu.SemaphoreType.DMA((2, parts)),
        ],
        compiler_params=pltpu.CompilerParams(vmem_limit_bytes=VMEM_LIMIT),
        name="feed_forward_backward",
    )(res, two, dy, slope, up, down, up_own, down_own, wo, g1, g2, s2)


class Total:
    def __init__(self, count_dp, count_mp, low, slots, parts, result, sems):
        self.low, self.slots, self.parts, self.result = low, slots, parts, result
        self.sems = sems
        self.count_b = count_mp // (2 * LINE)
        self.high_b, self.high_dp = self.count_b // 2, count_dp // 2
        self.count_q = LINE * self.high_b * self.high_dp
        dp, mp = lax.axis_index("dp"), lax.axis_index("mp")
        b = (mp // 2) % self.count_b
        a = mp // (2 * self.count_b)
        self.g = ((dp % 2) * 2 + b % 2) * 2 + mp % 2
        self.q = (a * self.high_b + b // 2) * self.high_dp + dp // 2

    def device(self, g, q):
        a, high = q // (self.high_b * self.high_dp), q % (self.high_b * self.high_dp)
        dp = (high % self.high_dp) * 2 + g // 4
        b = (high // self.high_dp) * 2 + (g // 2) % 2
        return dp, (a * self.count_b + b) * 2 + g % 2

    def near(self, j):
        return self.device((self.g + j) % 8, self.q)

    def far(self, i):
        return self.device(self.g, (self.q + i) % self.count_q)

    def copy(self, phase, j, arriving=False):
        if phase == 0:
            src, dst, to = self.low.at[(self.g + j) % 8], self.slots.at[j], self.near(j)
        elif phase == 1:
            at = (self.q + self.count_q - j) % self.count_q if arriving else self.q
            src, dst, to = self.parts.at[at], self.parts.at[at], self.far(j)
        else:
            at = (self.g + 8 - j) % 8 if arriving else self.g
            src, dst, to = self.result.at[at], self.result.at[at], self.near(j)
        send, recv = self.sems[phase]
        return pltpu.make_async_remote_copy(
            src_ref=src, dst_ref=dst, send_sem=send.at[j], recv_sem=recv.at[j], device_id=to,
            device_id_type=pl.DeviceIdType.MESH)

    def peers(self, phase):
        return range(1, self.count_q if phase == 1 else 8)

    def greet(self):
        barrier = pltpu.get_barrier_semaphore()
        partners = [self.near(j) for j in self.peers(0)] + [self.far(i) for i in self.peers(1)]
        for device in partners:
            pl.semaphore_signal(barrier, inc=1, device_id=device, device_id_type=pl.DeviceIdType.MESH)
        pl.semaphore_wait(barrier, len(partners))

    def start(self, phase):
        for j in self.peers(phase):
            self.copy(phase, j).start()

    def arrive(self, phase):
        for j in self.peers(phase):
            self.copy(phase, j, True).wait_recv()

    def first(self):
        self.greet()
        self.start(0)

    def second(self):
        self.arrive(0)
        total = self.low[self.g].astype(F32)
        for j in self.peers(0):
            total = total + self.slots[j].astype(F32)
        self.parts[self.q] = total.astype(BF16)
        self.start(1)

    def third(self):
        self.arrive(1)
        total = self.parts[0].astype(F32)
        for i in range(1, self.count_q):
            total = total + self.parts[i].astype(F32)
        self.result[self.g] = total.astype(BF16)
        self.start(2)

    def last(self):
        self.arrive(2)
        for phase in range(3):
            for j in self.peers(phase):
                self.copy(phase, j).wait_send()


def backward_kernel(counts, p_ref, q_ref, k_ref, v_ref, mix_ref, do_ref, pk_ref, pv_ref, w_hbm, gone_hbm,
                    out_ref, gk_ref, gv_ref, w_ref, gone_ref, kt, dk, dv, gj, delta, gbuf, ds_all, dqt, low, slots, parts, result,
                    send0, recv0, send1, recv1, send2, recv2, late):
    pair = pl.program_id(0)
    loads = [pltpu.make_async_copy(w_hbm, w_ref, late.at[0]), pltpu.make_async_copy(gone_hbm, gone_ref, late.at[1])]

    @pl.when(pair == 0)
    def _():
        for copy in loads:
            copy.start()

    length = q_ref.shape[0]
    pre = pk_ref.shape[0]
    pairs, width = ds_all.shape[0], out_ref.shape[1]
    blocks = length // QB
    depth = p_ref.shape[2]
    window = depth - pre
    ident = eye(QB)
    sub = lax.broadcasted_iota(jnp.int32, (8, PAIR), 0)
    lane = lax.broadcasted_iota(jnp.int32, (8, PAIR), 1)
    pick = jnp.where((sub == 0) == (lane < HEAD_DIM), 1.0, 0.0).astype(BF16)
    dk[...] = jnp.zeros_like(dk)
    dv[...] = jnp.zeros_like(dv)
    kt[pair, :, :length] = dot_t(ident, k_ref[...]).astype(BF16)
    kt[pair, :, length:] = dot_t(ident, pk_ref[...]).astype(BF16)
    prod = do_ref[...].astype(F32) * mix_ref[...].astype(F32)
    high = prod.astype(BF16)
    rest = (prod - high.astype(F32)).astype(BF16)
    delta[...] = dot_t(pick, high) + dot_t(pick, rest)

    def where_of(qb):
        start = min(max(qb * QB - QB, 0), length - window)
        return slice(start, start + window), slice(qb * QB, (qb + 1) * QB)

    def grad_probs(qb):
        win, rows = where_of(qb)
        vals = jnp.concatenate([v_ref[win], pv_ref[...]], axis=0)
        gbuf[qb % 2] = dot_t(vals, split_heads(do_ref[rows]))

    def grad_scores(qb):
        win, rows = where_of(qb)
        d = jnp.concatenate([delta[0:1, rows], delta[1:2, rows]], axis=1)
        ds_all[pair, qb] = (p_ref[qb, 0].astype(F32) * (gbuf[qb % 2] - d)).astype(BF16)

    def grads(qb):
        win, rows = where_of(qb)
        dva = dot(p_ref[qb, 0], split_heads(do_ref[rows]))
        dv[win] += dva[:window]
        dv[length:] += dva[window:]
        dka = dot(ds_all[pair, qb], split_heads(q_ref[rows]))
        dk[win] += dka[:window]
        dk[length:] += dka[window:]

    for i in range(blocks + 2):
        if i < blocks:
            grad_probs(i)
        if 0 <= i - 1 < blocks:
            grad_scores(i - 1)
        if 0 <= i - 2 < blocks:
            grads(i - 2)
    gj[pair, :, 0:PAIR] = dk[:length].astype(BF16)
    gj[pair, :, PAIR:] = dv[:length].astype(BF16)
    cols = pl.ds(pl.multiple_of(pair * PAIR, PAIR), PAIR)
    each = 2 * pre // 8
    for part, ref in enumerate((dk, dv)):
        for i in range(4):
            low[part * 4 + i, :, cols] = ref[length + i * each:length + (i + 1) * each].astype(BF16)

    @pl.when(pair == pl.num_programs(0) - 1)
    def _():
        total = Total(*counts, low, slots, parts, result, ((send0, recv0), (send1, recv1), (send2, recv2)))
        total.first()

        def query_grads(i, carry):
            rows_of = pl.ds(pl.multiple_of(i * PAIR, PAIR), PAIR)
            for qb in range(blocks):
                win, rows = where_of(qb)
                keys = jnp.concatenate([kt[i, :, win], kt[i, :, length:]], axis=1)
                dqt[rows_of, rows] = own_blocks(dot(keys, ds_all[i, qb]) * HEAD_DIM ** -0.5).astype(BF16)
            return carry

        lax.fori_loop(0, pairs // 2, query_grads, 0)
        total.second()
        lax.fori_loop(pairs // 2, pairs, query_grads, 0)
        total.third()
        for copy in loads:
            copy.wait()
        big = eye(256)
        for r in range(length // 256):
            rr = slice(r * 256, (r + 1) * 256)
            acc = gone_ref[rr] + dot_t(dot_t(big, dqt[:, rr]).astype(BF16), w_ref[:, :width])
            for part in range(2):
                x = jnp.concatenate([gj[i, rr, part * PAIR:(part + 1) * PAIR] for i in range(pairs)], axis=1)
                acc = acc + dot_t(x, w_ref[:, (part + 1) * width:(part + 2) * width])
            out_ref[rr] = acc.astype(BF16)
        total.last()
        for i in range(4):
            gk_ref[i * each:(i + 1) * each] = result[i].astype(F32)
            gv_ref[i * each:(i + 1) * each] = result[4 + i].astype(F32)


def attend_backward(p, q, k, v, mix, do, pk, pv, wqkv, gone, counts):
    length, width = q.shape
    pre = pk.shape[0]
    blocks, pairs, depth, _ = p.shape

    def col(a):
        return pl.BlockSpec((a.shape[0], PAIR), lambda i: (0, i))

    outs = [kept((length, width), BF16)] + [kept((pre, width), F32)] * 2
    count_q = counts[0] * counts[1] // 8
    piece = (2 * pre // 8, width)
    return pl.pallas_call(
        functools.partial(backward_kernel, counts),
        grid=(pairs,),
        in_specs=[pl.BlockSpec((blocks, 1, depth, 2 * QB), lambda i: (0, i, 0, 0))]
        + [col(a) for a in (q, k, v, mix, do, pk, pv)] + [pl.BlockSpec(memory_space=pl.ANY)] * 2,
        out_specs=[o[0] for o in outs],
        out_shape=[o[1] for o in outs],
        scratch_shapes=[
            pltpu.VMEM(wqkv.shape, BF16),
            pltpu.VMEM((length, width), F32),
            pltpu.VMEM((pairs, PAIR, length + pre), BF16),
            pltpu.VMEM((length + pre, PAIR), F32),
            pltpu.VMEM((length + pre, PAIR), F32),
            pltpu.VMEM((pairs, length, 2 * PAIR), BF16),
            pltpu.VMEM((8, length), F32),
            pltpu.VMEM((2, depth, 2 * QB), F32),
            pltpu.VMEM((pairs, blocks, depth, 2 * QB), BF16),
            pltpu.VMEM((width, length), BF16),
            pltpu.VMEM((8,) + piece, BF16),
            pltpu.VMEM((8,) + piece, BF16),
            pltpu.VMEM((count_q,) + piece, BF16),
            pltpu.VMEM((8,) + piece, BF16),
        ] + [pltpu.SemaphoreType.DMA((n,)) for n in (8, 8, count_q, count_q, 8, 8, 2)],
        compiler_params=pltpu.CompilerParams(vmem_limit_bytes=VMEM_LIMIT, collective_id=1, has_side_effects=True),
        name="attend_backward",
    )(p, q, k, v, mix, do, pk, pv, wqkv, gone)


def on_device(counts, tokens, segment_ids, qkv_weight, prefix_keys, prefix_values, out_weight, out_bias, norm1_gain,
              norm1_shift, up_weight, up_bias, down_weight, down_bias, norm2_gain, norm2_shift, out_grad):
    row = lambda a: a.reshape(1, -1)
    up_part = jnp.concatenate([up_weight, jnp.broadcast_to(row(up_bias), (BIAS_ROWS, up_bias.shape[0]))], axis=0)
    q, k, v, mix, probs, res, two, up_all, down_all, slope = attend_forward(
        tokens[0], qkv_weight, segment_ids, prefix_keys, prefix_values, out_weight, row(out_bias), row(norm1_gain),
        row(norm1_shift), row(down_bias), up_part, down_weight, counts[1])
    out, grad_one, grad_mixed = feed_forward_backward(
        res, two, out_grad[0], slope, up_all, down_all, up_part, down_weight, out_weight, row(norm1_gain), row(norm2_gain),
        row(norm2_shift))
    grad_tokens, total_k, total_v = attend_backward(
        probs, q, k, v, mix, grad_mixed, prefix_keys, prefix_values, qkv_weight, grad_one, counts)
    return out[None], grad_tokens[None], total_k, total_v


def solution(mesh):
    rows = P(("dp", "mp"), None, None)
    return jax.shard_map(
        functools.partial(on_device, (mesh.shape["dp"], mesh.shape["mp"])),
        mesh=mesh,
        in_specs=(rows, P(("dp", "mp"), None), P(), P(), P(), P(), P(), P(), P(), P(None, "mp"), P("mp"), P("mp", None),
                  P(), P(), P(), rows),
        out_specs=(rows, rows, P(), P()),
        check_vma=False,
    )
```

```python
import functools

import jax
import jax.numpy as jnp
from jax import lax
from jax.experimental import pallas as pl
from jax.experimental.pallas import tpu as pltpu
from jax.sharding import PartitionSpec as P

EPSILON = 1e-05
ROOT_HALF = 0.7071067811865476
INV_ROOT_TWOPI = 0.3989422804014327
MASK_FILL = -1e30
HEAD_DIM = 64
PAIR = 2 * HEAD_DIM
QB = 128
F32 = jnp.float32
BF16 = jnp.bfloat16
VMEM_LIMIT = 62 * 1024 * 1024
BACKWARD_LIMIT = 56 * 1024 * 1024
BIAS_ROWS = 32
QKV_SLOT = (1, 1)
GATHER_SLOTS = (
    (16, 0, 0, True), (16, 0, 0, False),
    (2, 1, 0, True), (2, 1, 0, False),
    (4, 0, 1, True),
    (6, 1, 1, True), (6, 0, 1, False),
    (7, 0, 2, True),
    (8, 1, 1, False),
    (9, 1, 2, True), (9, 0, 2, False),
    (11, 0, 3, True), (11, 1, 2, False),
    (12, 1, 3, True), (12, 0, 3, False),
    (13, 1, 3, False),
    (14, 0, 4, True), (14, 1, 4, True),
    (15, 0, 4, False), (15, 1, 4, False),
)


def dot(a, b):
    return lax.dot_general(a, b, (((1,), (0,)), ((), ())), preferred_element_type=F32)


def dot_t(a, b):
    return lax.dot_general(a, b, (((1,), (1,)), ((), ())), preferred_element_type=F32)


def eye(n):
    r = lax.broadcasted_iota(jnp.int32, (n, n), 0)
    c = lax.broadcasted_iota(jnp.int32, (n, n), 1)
    return jnp.where(r == c, 1.0, 0.0).astype(BF16)


def split_heads(x):
    lane = lax.broadcasted_iota(jnp.int32, x.shape, 1)
    zero = jnp.zeros_like(x)
    return jnp.concatenate([jnp.where(lane < HEAD_DIM, x, zero), jnp.where(lane < HEAD_DIM, zero, x)], axis=0)


def own_blocks(x):
    return jnp.concatenate([x[:HEAD_DIM, :QB], x[HEAD_DIM:, QB:]], axis=0)


def normalize(x):
    scale = 1.0 / x.shape[-1]
    cen = x - jnp.sum(x, -1, keepdims=True) * scale
    inv = lax.rsqrt(jnp.sum(cen * cen, -1, keepdims=True) * scale + EPSILON)
    return cen * inv, inv


def norm_back(grad, hat, inv, gain):
    scale = 1.0 / grad.shape[-1]
    sc = grad * gain
    mean1 = jnp.sum(sc, -1, keepdims=True) * scale
    mean2 = jnp.sum(sc * hat, -1, keepdims=True) * scale
    return (sc - mean1 - hat * mean2) * inv


def whole(a):
    return pl.BlockSpec(a.shape, lambda i: (0,) * a.ndim, pipeline_mode=pl.Buffered(1))


def kept(shape, dtype):
    spec = pl.BlockSpec(shape, lambda i: (0,) * len(shape), pipeline_mode=pl.Buffered(1))
    return spec, jax.ShapeDtypeStruct(shape, dtype)


LINE = 4


def flip(x, bits):
    bit = 1
    while bit <= bits:
        if bits & bit:
            x = x + bit - 2 * bit * ((x // bit) % 2)
        bit *= 2
    return x


def guarded(condition, body):
    if condition is None:
        body()
    else:
        pl.when(condition)(body)


def gather_keys(count_b):
    others = range(1, count_b)
    keys = [("z", side, d, 0) for side in (1, -1) for d in (1, 2, 3)]
    keys += [("z", side, d, 1) for side in (1, -1) for d in (1, 2)]
    for s in others:
        keys += [("x", s, d, 0) for d in (0, 1, -1, 2, 3)] + [("x", s, 3, 1)]
        keys += [("y", s, d, 0) for d in (0, 1, -1, 2)]
    keys.append(("y", 0, 3, 0))
    keys.append(("core", 0, 0, None))
    for s in range(count_b):
        keys += [("core", s, d, part) for d in (0, 1, -1, 2, 3) for part in (0, 1) if (s, d) != (0, 0)]
    return {key: i for i, key in enumerate(keys)}


def gather_events(count_b):
    others = range(1, count_b)
    sides = (1, -1)
    return [
        [("x", s, 0, 0) for s in others] + [("z", side, 1, 0) for side in sides],
        [("z", side, 2, 0) for side in sides] + [("x", s, d, 0) for s in others for d in sides] + [("y", s, 0, 0) for s in others],
        [("z", side, 3, 0) for side in sides] + [("x", s, 2, 0) for s in others] + [("y", s, d, 0) for s in others for d in sides],
        [("z", side, 1, 1) for side in sides] + [("y", 0, 3, 0)] + [("x", s, 3, 0) for s in others],
        [("z", side, 2, 1) for side in sides] + [("y", s, 2, 0) for s in others] + [("x", s, 3, 1) for s in others],
    ]


class Gather:
    def __init__(self, count_b, inputs, alls, sems):
        self.count_b = count_b
        self.inputs, self.alls = inputs, alls
        self.send, self.recv = sems
        self.dp = lax.axis_index("dp")
        self.mp = lax.axis_index("mp")
        self.core = self.mp % 2
        self.b = (self.mp // 2) % self.count_b
        self.a = self.mp // (2 * self.count_b)
        self.half = self.dp % 2
        self.keys = gather_keys(count_b)

    def index(self, a, s, other=False):
        core = 1 - self.core if other else self.core
        return (a * self.count_b + flip(self.b, s)) * 2 + core

    def at(self, d):
        if d in (2, 3):
            return self.a + d - 2 * d * ((self.a + d) // LINE)
        return self.a + d

    def inside(self, d):
        if d == 1:
            return self.a < LINE - 1
        if d == -1:
            return self.a > 0
        if d == 3:
            return self.a % 3 == 0
        return None

    def gets(self, key):
        kind, s, d, part = key
        if kind != "z":
            return self.inside(d)
        return self.a + d < LINE if s == 1 else self.a >= d

    def sends(self, key):
        kind, s, d, part = key
        if kind != "z":
            return self.inside(d)
        low, high = (1, LINE - d) if s == 1 else (d - 1, LINE - 2)
        return (self.a >= low) & (self.a <= high)

    def copy(self, t, key, arriving):
        kind, s, d, part = key
        own = d == 0 and not arriving
        if kind == "z":
            own = d == 1 and not arriving
            target = (self.dp, self.index(self.a - s, 0))
            chunk = self.index(self.a + s * d, 0) if arriving else self.index(self.a + s * (d - 1), 0)
        elif kind == "x":
            target = (self.dp, self.index(self.a, s))
            chunk = self.index(self.at(d), s if arriving else 0)
        elif kind == "y":
            target = (flip(self.dp, 1), self.mp)
            chunk = self.index(self.at(d), s)
            own = False
        else:
            target = (self.dp, self.index(self.a, 0, True))
            chunk = self.index(self.at(d), s, arriving)
            own = own and s == 0
        ref = self.alls[t]
        rows = ref.shape[1]
        if part is None:
            span = pl.ds(0, rows)
        else:
            which = 1 - part if kind == "y" and arriving else part
            which = self.half if which == 0 else 1 - self.half
            span = pl.ds(pl.multiple_of(which * (rows // 2), 16), rows // 2)
        src = self.inputs[t].at[span] if own else ref.at[chunk, span]
        number = self.keys[key]
        return pltpu.make_async_remote_copy(
            src_ref=src, dst_ref=ref.at[chunk, span], send_sem=self.send.at[t, number], recv_sem=self.recv.at[t, number],
            device_id=target, device_id_type=pl.DeviceIdType.MESH)

    def start(self, t, *key):
        guarded(self.sends(key), lambda: self.copy(t, key, False).start())

    def arrive(self, t, key):
        self.copy(t, key, True).wait_recv()

    def greet(self):
        barrier = pltpu.get_barrier_semaphore()
        partners = [(self.inside(d), (self.dp, self.index(self.a + d, 0))) for d in (1, -1)]
        partners += [(None, (self.dp, self.index(self.a, s))) for s in range(1, self.count_b)]
        partners += [(None, (self.dp, self.index(self.a, 0, True))), (None, (flip(self.dp, 1), self.mp))]
        for condition, device in partners:
            guarded(condition, lambda: pl.semaphore_signal(
                barrier, inc=1, device_id=device, device_id_type=pl.DeviceIdType.MESH))
        ends = 1 - (self.a % 3 + 1) // 2
        pl.semaphore_wait(barrier, len(partners) - ends)

    def open(self, t):
        for side in (1, -1):
            self.start(t, "z", side, 1, 0)
        for s in range(1, self.count_b):
            self.start(t, "x", s, 0, 0)
        self.start(t, "core", 0, 0, None)

    def pass_on(self, t, key):
        kind, s, d, part = key

        def body():
            self.arrive(t, key)
            if kind == "z":
                if d < (3 if part == 0 else 2):
                    self.start(t, "z", s, d + 1, part)
                at = s if d == 1 else d
                if part == 0:
                    for other in range(1, self.count_b):
                        self.start(t, "x", other, at, 0)
                    if d == 3:
                        self.start(t, "y", 0, 3, 0)
                self.start(t, "core", 0, at, part)
            elif kind == "x":
                if d != 3:
                    self.start(t, "y", s, d, 0)
                self.start(t, "core", s, d, part)
            else:
                if d == 3:
                    for other in range(1, self.count_b):
                        self.start(t, "x", other, 3, 1)
                self.start(t, "core", s, d, 1)

        guarded(self.gets(key), body)

    def level(self, t, n, along):
        for key in gather_events(self.count_b)[n]:
            if (key[0] == "z") == along:
                self.pass_on(t, key)
        if along and n < LINE - 1:
            for side in (1, -1):
                sent = LINE - 1 - self.a if side == 1 else self.a
                pl.when(sent == n)(lambda: self.start(t, "z", side, 1, 1))

    def from_core(self, n, along):
        keys = []
        for kind, s, d, part in gather_events(self.count_b)[n]:
            if (kind == "z") == along:
                if kind == "z":
                    key = ("core", 0, s if d == 1 else d, part)
                else:
                    key = ("core", s, d, 1 if kind == "y" else part)
                if key not in keys:
                    keys.append(key)
        for t in range(2):
            for key in keys:
                guarded(self.gets(key), lambda: self.arrive(t, key))

    def chip(self, o):
        n = self.count_b - 1
        end = self.a % 3 == 0
        one, two, three = 1 + n, 1 + 2 * n, 4 + 2 * n
        rank = jnp.where(o < one, 0, jnp.where(o <= two, 1, jnp.where(o == two + 1, jnp.where(end, 3, 2), jnp.where(
            o == two + 2, jnp.where(end, 2, 3), jnp.where(o < three + n, 2, 3)))))
        s = jnp.where(o < one, o, jnp.where(o < two, o - one + 1, jnp.where(o < three, 0, jnp.where(
            o < three + n, o - three + 1, o - three - n + 1))))
        a = jnp.where(rank == 0, self.a, jnp.where(rank == 1, 1 + self.a % 2, jnp.where(
            rank == 2, (2 + 3 * self.a) % 5, 3 - 3 * (self.a // 2))))
        return a * self.count_b + (self.b + s) % self.count_b

    def close(self, t):
        for key in self.keys:
            guarded(self.sends(key), lambda: self.copy(t, key, False).wait_send())


def forward_kernel(count_b, tok_hbm, wqkv_hbm, wo_hbm, up_hbm, down_in, seg_ref, pk_ref, pv_ref, bo_ref, g1_ref, s1_ref, db_ref, ub_ref,
                   q_hbm, k_hbm, v_hbm, mix_hbm, p_out, res_hbm, two_hbm, up_all, down_all, slope_out,
                   q_out, k_out, v_out, mix_out, res_out, two, tok_ref, wo_ref, up_in, wqkv_ref, vt, pvt, segc, bias, sbuf, mixt, low, up_v, down_v, pre, hid, slope, send, recv, wsem, qsem, osem, xsem):
    qb = pl.program_id(0)

    def copy_out(n):
        src = (q_out, k_out, v_out, mix_out, res_out, two)[n]
        return pltpu.make_async_copy(src, (q_hbm, k_hbm, v_hbm, mix_hbm, res_hbm, two_hbm)[n], xsem.at[n])

    gather = Gather(count_b, (up_in, down_in), (up_all, down_all), (send, recv))

    def pass_on(now):
        for slot, t, n, along in GATHER_SLOTS:
            if slot == now:
                gather.level(t, n, along)

    length, width = tok_ref.shape
    window = bias.shape[0]
    pairs = width // PAIR

    @pl.when(qb == 0)
    def _():
        def weights(part):
            cols = pl.ds(part * width, width)
            return pltpu.make_async_copy(wqkv_hbm.at[:, cols], wqkv_ref.at[:, cols], qsem.at[part])

        whole_in = [pltpu.make_async_copy(src, dst, qsem.at[3 + n]) for n, (src, dst) in enumerate((
            (up_hbm, up_in.at[pl.ds(0, width)]), (tok_hbm, tok_ref), (wo_hbm, wo_ref)))]
        whole_in[0].start()
        whole_in[1].start()
        for part in range(3):
            weights(part).start()
        whole_in[2].start()
        up_in[width:] = jnp.broadcast_to(ub_ref[...].astype(F32), (BIAS_ROWS, ub_ref.shape[1])).astype(BF16)
        gather.greet()
        whole_in[0].wait()
        gather.open(0)
        gather.open(1)
        tile = 256
        whole_in[1].wait()
        for part, ref in enumerate((q_out, k_out, v_out)):
            weights(part).wait()
            for j in range(width // tile):
                x = dot(tok_ref[...], wqkv_ref[:, part * width + j * tile:part * width + (j + 1) * tile]).astype(BF16)
                if part == 0:
                    x = x * jnp.asarray(HEAD_DIM ** -0.5, BF16)
                ref[:, j * tile:(j + 1) * tile] = x
                if (part, j) == QKV_SLOT:
                    pass_on(16)
            copy_out(part).start()
        whole_in[2].wait()
        big = eye(256)
        for j in range(width // 256):
            cols = slice(j * 256, (j + 1) * 256)
            vt[cols, :] = dot_t(big, v_out[:, cols]).astype(BF16)
            pvt[cols, :] = dot_t(big, pv_ref[:, cols]).astype(BF16)
        pass_on(0)
        ident = eye(QB)
        seg = jnp.broadcast_to(seg_ref[...].astype(F32), (QB, length)).astype(BF16)
        for j in range(length // QB):
            segc[j * QB:(j + 1) * QB, :] = dot_t(ident, seg[:, j * QB:(j + 1) * QB])

    for slot in range(1, length // QB):

        @pl.when(qb == slot)
        def _():
            pass_on(slot)

    start = pl.multiple_of(jnp.clip(qb * QB - QB, 0, length - window), QB)
    win = pl.ds(start, window)
    rows = pl.ds(pl.multiple_of(qb * QB, QB), QB)
    segq = seg_ref[:, rows].astype(F32)
    bias[...] = jnp.where(segc[win, :] == segq, 0.0, MASK_FILL)

    def score(pair):
        cols = slice(pair * PAIR, (pair + 1) * PAIR)
        keys = jnp.concatenate([k_out[win, cols], pk_ref[:, cols]], axis=0)
        sbuf[pair % 2] = dot_t(keys, split_heads(q_out[rows, cols]))

    def soft(pair):
        both = jnp.concatenate([bias[...], bias[...]], axis=1)
        sw = sbuf[pair % 2, :window] + both
        sp = sbuf[pair % 2, window:]
        top = jnp.maximum(jnp.max(sw, 0, keepdims=True), jnp.max(sp, 0, keepdims=True))
        ew = jnp.exp(sw - top)
        ep = jnp.exp(sp - top)
        inv = 1.0 / (jnp.sum(ew, 0, keepdims=True) + jnp.sum(ep, 0, keepdims=True))
        p_out[0, pair, :window] = (ew * inv).astype(BF16)
        p_out[0, pair, window:] = (ep * inv).astype(BF16)

    def mixing(pair):
        cols = slice(pair * PAIR, (pair + 1) * PAIR)
        vals = jnp.concatenate([vt[cols, win], pvt[cols, :]], axis=1)
        mixt[cols, rows] = own_blocks(dot(vals, p_out[0, pair])).astype(BF16)

    for i in range(pairs + 2):
        if i < pairs:
            score(i)
        if 0 <= i - 1 < pairs:
            soft(i - 1)
        if 0 <= i - 2 < pairs:
            mixing(i - 2)

    @pl.when(qb == pl.num_programs(0) - 1)
    def _():
        pass_on(8)
        big = eye(256)
        for r in range(length // 256):
            rr = slice(r * 256, (r + 1) * 256)
            mix_out[rr] = dot_t(big, mixt[:, rr]).astype(BF16)
        copy_out(3).start()
        for r in range(length // 256):
            rr = slice(r * 256, (r + 1) * 256)
            res = tok_ref[rr].astype(F32) + dot(mix_out[rr], wo_ref[...]) + bo_ref[...]
            res_out[rr] = res
            first = normalize(res)[0] * g1_ref[...] + s1_ref[...]
            low[rr] = first.astype(BF16)
            two[rr] = first + db_ref[...]
        copy_out(4).start()
        pass_on(9)

        chips = LINE * count_b
        ffl = down_in.shape[0]
        per = length // 256

        def loads(o):
            chip = gather.chip(o)
            out = []
            for c in range(2):
                core = gather.core if c else 1 - gather.core
                cols = pl.ds(pl.multiple_of(core * ffl, 128), ffl)
                own = isinstance(o, int) and o == 0 and c == 1
                for t, to in ((0, up_v.at[o % 3, :, cols]), (1, down_v.at[o % 3, cols])):
                    src = (up_in, down_in)[t] if own else (up_all, down_all)[t].at[2 * chip + core]
                    out.append(pltpu.make_async_copy(src, to, wsem.at[o % 3, t, c]))
            return out

        def load(o):
            for copy in loads(o):
                copy.start()

        def loaded(o):
            for copy in loads(o):
                copy.wait()

        def rows_of(b):
            return slice(b * 256, (b + 1) * 256)

        def up(o, b):
            pre[b % 2] = dot(low[rows_of(b)], up_v[o % 3, :width, :])

        def act(o, b):
            u = pre[b % 2] + up_v[o % 3, width:width + 1, :].astype(F32)
            half = 0.5 * lax.erf(u * ROOT_HALF) + 0.5
            hid[b % 2] = (u * half).astype(BF16)
            slope[o, rows_of(b)] = (half + u * (jnp.exp(-0.5 * u * u) * INV_ROOT_TWOPI)).astype(BF16)

        def down(o, b):
            two[rows_of(b)] += dot(hid[b % 2], down_v[o % 3])

        def earlier(o, b, n):
            return (o, b - n) if b >= n else (o - 1, b - n + per)

        def chip_steps(o, ahead):
            loaded(o)
            ahead()
            for b in range(per):
                up(o, b)
                if b >= 1 or not (isinstance(o, int) and o == 0):
                    act(*earlier(o, b, 1))
                if b >= 2 or not (isinstance(o, int) and o == 0):
                    down(*earlier(o, b, 2))

        def keep(o):
            return pltpu.make_async_copy(slope.at[o], slope_out.at[gather.chip(o)], osem.at[o])

        def more():
            pass_on(10)
            for n in range(2):
                for along in (True, False):
                    gather.from_core(n, along)

        for t in range(2):
            gather.arrive(t, ("core", 0, 0, None))
        load(0)

        def first_ahead():
            more()
            load(1)

        chip_steps(0, first_ahead)
        others = count_b - 1
        needs = ((others, 11, 2, (True, False)), (2 * others, 12, 3, (True,)), (2 * others + 1, 13, 3, (False,)),
                 (2 * others + 2, 14, 4, (True,)), (2 * others + 3, 15, 4, (False,)))

        def chip_step(o, carry):
            def ahead():
                for at, slot, n, kinds in needs:

                    @pl.when(o == at)
                    def _():
                        pass_on(slot)
                        for along in kinds:
                            gather.from_core(n, along)

                @pl.when(o < chips - 1)
                def _():
                    load(o + 1)

            chip_steps(o, ahead)
            keep(o - 1).start()
            return carry

        lax.fori_loop(1, chips, chip_step, 0)
        act(chips - 1, per - 1)
        down(chips - 1, per - 2)
        down(chips - 1, per - 1)
        copy_out(5).start()
        keep(chips - 1).start()
        for t in range(2):
            gather.close(t)
        for o in range(chips):
            keep(o).wait()
        for n in range(6):
            copy_out(n).wait()


def attend_forward(tok, wqkv, wo, up, down, seg, pk, pv, bo, g1, s1, db, ub, group):
    length, width = tok.shape
    pre = pk.shape[0]
    window = 3 * QB
    pairs, blocks = width // PAIR, length // QB
    hbm = pl.BlockSpec(memory_space=pl.ANY)
    square, wide = jax.ShapeDtypeStruct((length, width), BF16), jax.ShapeDtypeStruct((length, width), F32)
    outs = [(hbm, square)] * 4 + [
        (pl.BlockSpec((1, pairs, window + pre, 2 * QB), lambda i: (i, 0, 0, 0)),
         jax.ShapeDtypeStruct((blocks, pairs, window + pre, 2 * QB), BF16)),
        (hbm, wide), (hbm, wide)]
    up_shape = (width + BIAS_ROWS, up.shape[1])
    outs += [(hbm, jax.ShapeDtypeStruct((group,) + shape, BF16)) for shape in (up_shape, down.shape)]
    chips, part = group // 2, 2 * down.shape[0]
    outs += [(hbm, jax.ShapeDtypeStruct((chips, length, part), BF16))]
    count_b = group // (2 * LINE)
    pieces = len(gather_keys(count_b))
    return pl.pallas_call(
        functools.partial(forward_kernel, count_b),
        grid=(blocks,),
        in_specs=[hbm] * 5 + [whole(a) for a in (seg, pk, pv, bo, g1, s1, db, ub)],
        out_specs=[o[0] for o in outs],
        out_shape=[o[1] for o in outs],
        scratch_shapes=[pltpu.VMEM((length, width), t) for t in (BF16, BF16, BF16, BF16, F32, F32, BF16)] + [
            pltpu.VMEM((width, width), BF16),
            pltpu.VMEM(up_shape, BF16),
            pltpu.VMEM(wqkv.shape, BF16),
            pltpu.VMEM((width, length), BF16),
            pltpu.VMEM((width, pre), BF16),
            pltpu.VMEM((length, QB), F32),
            pltpu.VMEM((window, QB), F32),
            pltpu.VMEM((2, window + pre, 2 * QB), F32),
            pltpu.VMEM((width, length), BF16),
            pltpu.VMEM((length, width), BF16),
            pltpu.VMEM((3, up_shape[0], part), BF16),
            pltpu.VMEM((3, part, width), BF16),
            pltpu.VMEM((2, 256, part), F32),
            pltpu.VMEM((2, 256, part), BF16),
            pltpu.VMEM((chips, length, part), BF16),
            pltpu.SemaphoreType.DMA((2, pieces)),
            pltpu.SemaphoreType.DMA((2, pieces)),
            pltpu.SemaphoreType.DMA((3, 2, 2)),
            pltpu.SemaphoreType.DMA((6,)),
            pltpu.SemaphoreType.DMA((chips,)),
            pltpu.SemaphoreType.DMA((6,)),
        ],
        compiler_params=pltpu.CompilerParams(vmem_limit_bytes=VMEM_LIMIT, collective_id=0, has_side_effects=True),
        name="attend_forward",
    )(tok, wqkv, wo, up, down, seg, pk, pv, bo, g1, s1, db, ub)


def ffn_kernel(res_ref, two_ref, dy_ref, slope_ref, up_hbm, down_hbm, up_own, down_own, wo_ref, g1_ref, g2_ref, s2_ref,
               out_ref, gone_ref, gmix_ref, up, down, hid, low, acc, sems):
    step = pl.program_id(0)
    width = up.shape[0]
    parts, part, _ = down_hbm.shape
    count, _, chunk = slope_ref.shape
    me = lax.axis_index("mp")

    def fetch(d, t, own):
        cols = pl.ds(d * part, part)
        up_src, down_src = (up_own, down_own) if own else (up_hbm.at[d], down_hbm.at[d])
        src, dst = ((up_src.at[pl.ds(0, width)], up.at[:, cols]), (down_src, down.at[cols]))[t]
        return pltpu.make_async_copy(src, dst, sems.at[t, d])

    @pl.when(step == 0)
    def _():
        for t in (1, 0):
            for d in range(parts):

                @pl.when(me == d)
                def _():
                    fetch(d, t, True).start()

                @pl.when(me != d)
                def _():
                    fetch(d, t, False).start()

    hat2, inv2 = normalize(two_ref[...])
    out_ref[...] = (hat2 * g2_ref[...] + s2_ref[...]).astype(BF16)
    grad_two = norm_back(dy_ref[...].astype(F32), hat2, inv2, g2_ref[...])
    acc[...] = grad_two
    low[...] = grad_two.astype(BF16)

    @pl.when(step == 0)
    def _():
        for d in range(parts):
            fetch(d, 1, False).wait()

    def cols_of(j):
        return slice(j * chunk, (j + 1) * chunk)

    def back_down(j):
        gh = dot_t(low[...], down[cols_of(j)])
        hid[j % 2] = (gh * slope_ref[j].astype(F32)).astype(BF16)

    def back_up(j):
        acc[...] += dot_t(hid[j % 2], up[:, cols_of(j)])

    for j in range(count + 1):
        if j < count:
            back_down(j)
        if j == 1:

            @pl.when(step == 0)
            def _():
                for d in range(parts):
                    fetch(d, 0, False).wait()

        if j >= 1:
            back_up(j - 1)

    hat, inv1 = normalize(res_ref[...])
    grad_one = norm_back(acc[...], hat, inv1, g1_ref[...])
    gone_ref[...] = grad_one
    gmix_ref[...] = dot_t(grad_one.astype(BF16), wo_ref[...]).astype(BF16)


def feed_forward_backward(res, two, dy, slope, up, down, up_own, down_own, wo, g1, g2, s2, tb=256):
    rows, width = res.shape
    parts, ffl, _ = down.shape
    ff = parts * ffl
    chips, _, part = slope.shape
    block = pl.BlockSpec((tb, width), lambda i: (i, 0))
    hbm = pl.BlockSpec(memory_space=pl.ANY)
    return pl.pallas_call(
        ffn_kernel,
        grid=(rows // tb,),
        in_specs=[block] * 3 + [pl.BlockSpec((chips, tb, part), lambda i: (0, i, 0))] + [hbm] * 4
        + [whole(a) for a in (wo, g1, g2, s2)],
        out_specs=[block] * 3,
        out_shape=[jax.ShapeDtypeStruct((rows, width), t) for t in (BF16, F32, BF16)],
        scratch_shapes=[
            pltpu.VMEM((width, ff), BF16),
            pltpu.VMEM((ff, width), BF16),
            pltpu.VMEM((2, tb, part), BF16),
            pltpu.VMEM((tb, width), BF16),
            pltpu.VMEM((tb, width), F32),
            pltpu.SemaphoreType.DMA((2, parts)),
        ],
        compiler_params=pltpu.CompilerParams(vmem_limit_bytes=VMEM_LIMIT),
        name="feed_forward_backward",
    )(res, two, dy, slope, up, down, up_own, down_own, wo, g1, g2, s2)


class Total:
    def __init__(self, count_dp, count_mp, low, slots, parts, result, sems):
        self.low, self.slots, self.parts, self.result = low, slots, parts, result
        self.sems = sems
        self.count_b = count_mp // (2 * LINE)
        self.high_b, self.high_dp = self.count_b // 2, count_dp // 2
        self.count_q = LINE * self.high_b * self.high_dp
        dp, mp = lax.axis_index("dp"), lax.axis_index("mp")
        b = (mp // 2) % self.count_b
        a = mp // (2 * self.count_b)
        self.g = ((dp % 2) * 2 + b % 2) * 2 + mp % 2
        self.q = (a * self.high_b + b // 2) * self.high_dp + dp // 2

    def device(self, g, q):
        a, high = q // (self.high_b * self.high_dp), q % (self.high_b * self.high_dp)
        dp = (high % self.high_dp) * 2 + g // 4
        b = (high // self.high_dp) * 2 + (g // 2) % 2
        return dp, (a * self.count_b + b) * 2 + g % 2

    def near(self, j):
        return self.device((self.g + j) % 8, self.q)

    def far(self, i):
        return self.device(self.g, (self.q + i) % self.count_q)

    def copy(self, phase, j, arriving=False):
        if phase == 0:
            src, dst, to = self.low.at[(self.g + j) % 8], self.slots.at[j], self.near(j)
        elif phase == 1:
            at = (self.q + self.count_q - j) % self.count_q if arriving else self.q
            src, dst, to = self.parts.at[at], self.parts.at[at], self.far(j)
        else:
            at = (self.g + 8 - j) % 8 if arriving else self.g
            src, dst, to = self.result.at[at], self.result.at[at], self.near(j)
        send, recv = self.sems[phase]
        return pltpu.make_async_remote_copy(
            src_ref=src, dst_ref=dst, send_sem=send.at[j], recv_sem=recv.at[j], device_id=to,
            device_id_type=pl.DeviceIdType.MESH)

    def peers(self, phase):
        return range(1, self.count_q if phase == 1 else 8)

    def greet(self):
        barrier = pltpu.get_barrier_semaphore()
        partners = [self.near(j) for j in self.peers(0)] + [self.far(i) for i in self.peers(1)]
        for device in partners:
            pl.semaphore_signal(barrier, inc=1, device_id=device, device_id_type=pl.DeviceIdType.MESH)
        pl.semaphore_wait(barrier, len(partners))

    def start(self, phase):
        for j in self.peers(phase):
            self.copy(phase, j).start()

    def arrive(self, phase):
        for j in self.peers(phase):
            self.copy(phase, j, True).wait_recv()

    def first(self):
        self.greet()
        self.start(0)

    def second(self):
        self.arrive(0)
        total = self.low[self.g].astype(F32)
        for j in self.peers(0):
            total = total + self.slots[j].astype(F32)
        self.parts[self.q] = total.astype(BF16)
        self.start(1)

    def third(self):
        self.arrive(1)
        total = self.parts[0].astype(F32)
        for i in range(1, self.count_q):
            total = total + self.parts[i].astype(F32)
        self.result[self.g] = total.astype(BF16)
        self.start(2)

    def last(self):
        self.arrive(2)
        for phase in range(3):
            for j in self.peers(phase):
                self.copy(phase, j).wait_send()


def backward_kernel(counts, p_ref, q_ref, k_ref, v_ref, mix_ref, do_ref, pk_ref, pv_ref, w_hbm, gone_hbm,
                    out_ref, gk_ref, gv_ref, w_ref, gone_ref, kt, dk, dv, gj, delta, gbuf, ds_all, dqt, low, slots, parts, result,
                    send0, recv0, send1, recv1, send2, recv2, late):
    pair = pl.program_id(0)
    loads = [pltpu.make_async_copy(w_hbm, w_ref, late.at[0]), pltpu.make_async_copy(gone_hbm, gone_ref, late.at[1])]

    @pl.when(pair == 0)
    def _():
        for copy in loads:
            copy.start()

    length = q_ref.shape[0]
    pre = pk_ref.shape[0]
    pairs, width = ds_all.shape[0], out_ref.shape[1]
    blocks = length // QB
    depth = p_ref.shape[2]
    window = depth - pre
    ident = eye(QB)
    sub = lax.broadcasted_iota(jnp.int32, (8, PAIR), 0)
    lane = lax.broadcasted_iota(jnp.int32, (8, PAIR), 1)
    pick = jnp.where((sub == 0) == (lane < HEAD_DIM), 1.0, 0.0).astype(BF16)
    dk[...] = jnp.zeros_like(dk)
    dv[...] = jnp.zeros_like(dv)
    kt[pair, :, :length] = dot_t(ident, k_ref[...]).astype(BF16)
    kt[pair, :, length:] = dot_t(ident, pk_ref[...]).astype(BF16)
    prod = do_ref[...].astype(F32) * mix_ref[...].astype(F32)
    high = prod.astype(BF16)
    rest = (prod - high.astype(F32)).astype(BF16)
    delta[...] = dot_t(pick, high) + dot_t(pick, rest)

    def where_of(qb):
        start = min(max(qb * QB - QB, 0), length - window)
        return slice(start, start + window), slice(qb * QB, (qb + 1) * QB)

    def grad_probs(qb):
        win, rows = where_of(qb)
        vals = jnp.concatenate([v_ref[win], pv_ref[...]], axis=0)
        gbuf[qb % 2] = dot_t(vals, split_heads(do_ref[rows]))

    def grad_scores(qb):
        win, rows = where_of(qb)
        d = jnp.concatenate([delta[0:1, rows], delta[1:2, rows]], axis=1)
        ds_all[pair, qb] = (p_ref[qb, 0].astype(F32) * (gbuf[qb % 2] - d)).astype(BF16)

    def grads(qb):
        win, rows = where_of(qb)
        dva = dot(p_ref[qb, 0], split_heads(do_ref[rows]))
        dv[win] += dva[:window]
        dv[length:] += dva[window:]
        dka = dot(ds_all[pair, qb], split_heads(q_ref[rows]))
        dk[win] += dka[:window]
        dk[length:] += dka[window:]

    for i in range(blocks + 2):
        if i < blocks:
            grad_probs(i)
        if 0 <= i - 1 < blocks:
            grad_scores(i - 1)
        if 0 <= i - 2 < blocks:
            grads(i - 2)
    gj[pair, :, 0:PAIR] = dk[:length].astype(BF16)
    gj[pair, :, PAIR:] = dv[:length].astype(BF16)
    cols = pl.ds(pl.multiple_of(pair * PAIR, PAIR), PAIR)
    each = 2 * pre // 8
    for part, ref in enumerate((dk, dv)):
        for i in range(4):
            low[part * 4 + i, :, cols] = ref[length + i * each:length + (i + 1) * each].astype(BF16)

    @pl.when(pair == pl.num_programs(0) - 1)
    def _():
        total = Total(*counts, low, slots, parts, result, ((send0, recv0), (send1, recv1), (send2, recv2)))
        total.first()

        def query_grads(i, carry):
            rows_of = pl.ds(pl.multiple_of(i * PAIR, PAIR), PAIR)
            for qb in range(blocks):
                win, rows = where_of(qb)
                keys = jnp.concatenate([kt[i, :, win], kt[i, :, length:]], axis=1)
                dqt[rows_of, rows] = own_blocks(dot(keys, ds_all[i, qb]) * HEAD_DIM ** -0.5).astype(BF16)
            return carry

        lax.fori_loop(0, pairs // 2, query_grads, 0)
        total.second()
        lax.fori_loop(pairs // 2, pairs, query_grads, 0)
        total.third()
        for copy in loads:
            copy.wait()
        big = eye(256)
        for r in range(length // 256):
            rr = slice(r * 256, (r + 1) * 256)
            acc = gone_ref[rr] + dot_t(dot_t(big, dqt[:, rr]).astype(BF16), w_ref[:, :width])
            for part in range(2):
                x = jnp.concatenate([gj[i, rr, part * PAIR:(part + 1) * PAIR] for i in range(pairs)], axis=1)
                acc = acc + dot_t(x, w_ref[:, (part + 1) * width:(part + 2) * width])
            out_ref[rr] = acc.astype(BF16)
        total.last()
        for i in range(4):
            gk_ref[i * each:(i + 1) * each] = result[i].astype(F32)
            gv_ref[i * each:(i + 1) * each] = result[4 + i].astype(F32)


def attend_backward(p, q, k, v, mix, do, pk, pv, wqkv, gone, counts):
    length, width = q.shape
    pre = pk.shape[0]
    blocks, pairs, depth, _ = p.shape

    def col(a):
        return pl.BlockSpec((a.shape[0], PAIR), lambda i: (0, i))

    vmem = pl.BlockSpec(memory_space=pltpu.VMEM)
    outs = [(vmem, jax.ShapeDtypeStruct((length, width), BF16))] + [(vmem, jax.ShapeDtypeStruct((pre, width), F32))] * 2
    count_q = counts[0] * counts[1] // 8
    piece = (2 * pre // 8, width)
    return pl.pallas_call(
        functools.partial(backward_kernel, counts),
        grid=(pairs,),
        in_specs=[pl.BlockSpec((blocks, 1, depth, 2 * QB), lambda i: (0, i, 0, 0))]
        + [col(a) for a in (q, k, v, mix, do, pk, pv)] + [pl.BlockSpec(memory_space=pl.ANY)] * 2,
        out_specs=[o[0] for o in outs],
        out_shape=[o[1] for o in outs],
        scratch_shapes=[
            pltpu.VMEM(wqkv.shape, BF16),
            pltpu.VMEM((length, width), F32),
            pltpu.VMEM((pairs, PAIR, length + pre), BF16),
            pltpu.VMEM((length + pre, PAIR), F32),
            pltpu.VMEM((length + pre, PAIR), F32),
            pltpu.VMEM((pairs, length, 2 * PAIR), BF16),
            pltpu.VMEM((8, length), F32),
            pltpu.VMEM((2, depth, 2 * QB), F32),
            pltpu.VMEM((pairs, blocks, depth, 2 * QB), BF16),
            pltpu.VMEM((width, length), BF16),
            pltpu.VMEM((8,) + piece, BF16),
            pltpu.VMEM((8,) + piece, BF16),
            pltpu.VMEM((count_q,) + piece, BF16),
            pltpu.VMEM((8,) + piece, BF16),
        ] + [pltpu.SemaphoreType.DMA((n,)) for n in (8, 8, count_q, count_q, 8, 8, 2)],
        compiler_params=pltpu.CompilerParams(vmem_limit_bytes=BACKWARD_LIMIT, collective_id=1, has_side_effects=True),
        name="attend_backward",
    )(p, q, k, v, mix, do, pk, pv, wqkv, gone)


def on_device(counts, tokens, segment_ids, qkv_weight, prefix_keys, prefix_values, out_weight, out_bias, norm1_gain,
              norm1_shift, up_weight, up_bias, down_weight, down_bias, norm2_gain, norm2_shift, out_grad):
    row = lambda a: a.reshape(1, -1)
    q, k, v, mix, probs, res, two, up_all, down_all, slope = attend_forward(
        tokens[0], qkv_weight, out_weight, up_weight, down_weight, segment_ids, prefix_keys, prefix_values, row(out_bias),
        row(norm1_gain), row(norm1_shift), row(down_bias), row(up_bias), counts[1])
    out, grad_one, grad_mixed = feed_forward_backward(
        res, two, out_grad[0], slope, up_all, down_all, up_weight, down_weight, out_weight, row(norm1_gain), row(norm2_gain),
        row(norm2_shift))
    grad_tokens, total_k, total_v = attend_backward(
        probs, q, k, v, mix, grad_mixed, prefix_keys, prefix_values, qkv_weight, grad_one, counts)
    return out[None], grad_tokens[None], total_k, total_v


def solution(mesh):
    rows = P(("dp", "mp"), None, None)
    return jax.shard_map(
        functools.partial(on_device, (mesh.shape["dp"], mesh.shape["mp"])),
        mesh=mesh,
        in_specs=(rows, P(("dp", "mp"), None), P(), P(), P(), P(), P(), P(), P(), P(None, "mp"), P("mp"), P("mp", None),
                  P(), P(), P(), rows),
        out_specs=(rows, rows, P(), P()),
        check_vma=False,
    )
```

```python
import functools

import jax
import jax.numpy as jnp
from jax import lax
from jax.experimental import pallas as pl
from jax.experimental.pallas import tpu as pltpu
from jax.sharding import PartitionSpec as P

EPSILON = 1e-05
ROOT_HALF = 0.7071067811865476
INV_ROOT_TWOPI = 0.3989422804014327
MASK_FILL = -1e30
HEAD_DIM = 64
PAIR = 2 * HEAD_DIM
QB = 128
F32 = jnp.float32
BF16 = jnp.bfloat16
VMEM_LIMIT = 62 * 1024 * 1024
BACKWARD_LIMIT = 56 * 1024 * 1024
BIAS_ROWS = 32
QKV_SLOT = (1, 1)
GATHER_SLOTS = (
    (16, 0, 0, True), (16, 0, 0, False),
    (2, 1, 0, True), (2, 1, 0, False),
    (4, 0, 1, True),
    (6, 1, 1, True), (6, 0, 1, False),
    (7, 0, 2, True),
    (8, 1, 1, False),
    (9, 1, 2, True), (9, 0, 2, False),
    (11, 0, 3, True), (11, 1, 2, False),
    (12, 1, 3, True), (12, 0, 3, False),
    (13, 1, 3, False),
    (14, 0, 4, True), (14, 1, 4, True),
    (15, 0, 4, False), (15, 1, 4, False),
)


def dot(a, b):
    return lax.dot_general(a, b, (((1,), (0,)), ((), ())), preferred_element_type=F32)


def dot_t(a, b):
    return lax.dot_general(a, b, (((1,), (1,)), ((), ())), preferred_element_type=F32)


def eye(n):
    r = lax.broadcasted_iota(jnp.int32, (n, n), 0)
    c = lax.broadcasted_iota(jnp.int32, (n, n), 1)
    return jnp.where(r == c, 1.0, 0.0).astype(BF16)


def split_heads(x):
    lane = lax.broadcasted_iota(jnp.int32, x.shape, 1)
    zero = jnp.zeros_like(x)
    return jnp.concatenate([jnp.where(lane < HEAD_DIM, x, zero), jnp.where(lane < HEAD_DIM, zero, x)], axis=0)


def own_blocks(x):
    return jnp.concatenate([x[:HEAD_DIM, :QB], x[HEAD_DIM:, QB:]], axis=0)


def normalize(x):
    scale = 1.0 / x.shape[-1]
    cen = x - jnp.sum(x, -1, keepdims=True) * scale
    inv = lax.rsqrt(jnp.sum(cen * cen, -1, keepdims=True) * scale + EPSILON)
    return cen * inv, inv


def norm_back(grad, hat, inv, gain):
    scale = 1.0 / grad.shape[-1]
    sc = grad * gain
    mean1 = jnp.sum(sc, -1, keepdims=True) * scale
    mean2 = jnp.sum(sc * hat, -1, keepdims=True) * scale
    return (sc - mean1 - hat * mean2) * inv


def whole(a):
    return pl.BlockSpec(a.shape, lambda i: (0,) * a.ndim, pipeline_mode=pl.Buffered(1))


def kept(shape, dtype):
    spec = pl.BlockSpec(shape, lambda i: (0,) * len(shape), pipeline_mode=pl.Buffered(1))
    return spec, jax.ShapeDtypeStruct(shape, dtype)


LINE = 4


def flip(x, bits):
    bit = 1
    while bit <= bits:
        if bits & bit:
            x = x + bit - 2 * bit * ((x // bit) % 2)
        bit *= 2
    return x


def guarded(condition, body):
    if condition is None:
        body()
    else:
        pl.when(condition)(body)


def gather_keys(count_b):
    others = range(1, count_b)
    keys = [("z", side, d, 0) for side in (1, -1) for d in (1, 2, 3)]
    keys += [("z", side, d, 1) for side in (1, -1) for d in (1, 2)]
    for s in others:
        keys += [("x", s, d, 0) for d in (0, 1, -1, 2, 3)] + [("x", s, 3, 1)]
        keys += [("y", s, d, 0) for d in (0, 1, -1, 2)]
    keys.append(("y", 0, 3, 0))
    keys.append(("core", 0, 0, None))
    for s in range(count_b):
        keys += [("core", s, d, part) for d in (0, 1, -1, 2, 3) for part in (0, 1) if (s, d) != (0, 0)]
    return {key: i for i, key in enumerate(keys)}


def gather_events(count_b):
    others = range(1, count_b)
    sides = (1, -1)
    return [
        [("x", s, 0, 0) for s in others] + [("z", side, 1, 0) for side in sides],
        [("z", side, 2, 0) for side in sides] + [("x", s, d, 0) for s in others for d in sides] + [("y", s, 0, 0) for s in others],
        [("z", side, 3, 0) for side in sides] + [("x", s, 2, 0) for s in others] + [("y", s, d, 0) for s in others for d in sides],
        [("z", side, 1, 1) for side in sides] + [("y", 0, 3, 0)] + [("x", s, 3, 0) for s in others],
        [("z", side, 2, 1) for side in sides] + [("y", s, 2, 0) for s in others] + [("x", s, 3, 1) for s in others],
    ]


class Gather:
    def __init__(self, count_b, inputs, alls, sems):
        self.count_b = count_b
        self.inputs, self.alls = inputs, alls
        self.send, self.recv = sems
        self.dp = lax.axis_index("dp")
        self.mp = lax.axis_index("mp")
        self.core = self.mp % 2
        self.b = (self.mp // 2) % self.count_b
        self.a = self.mp // (2 * self.count_b)
        self.half = self.dp % 2
        self.keys = gather_keys(count_b)

    def index(self, a, s, other=False):
        core = 1 - self.core if other else self.core
        return (a * self.count_b + flip(self.b, s)) * 2 + core

    def at(self, d):
        if d in (2, 3):
            return self.a + d - 2 * d * ((self.a + d) // LINE)
        return self.a + d

    def inside(self, d):
        if d == 1:
            return self.a < LINE - 1
        if d == -1:
            return self.a > 0
        if d == 3:
            return self.a % 3 == 0
        return None

    def gets(self, key):
        kind, s, d, part = key
        if kind != "z":
            return self.inside(d)
        return self.a + d < LINE if s == 1 else self.a >= d

    def sends(self, key):
        kind, s, d, part = key
        if kind != "z":
            return self.inside(d)
        low, high = (1, LINE - d) if s == 1 else (d - 1, LINE - 2)
        return (self.a >= low) & (self.a <= high)

    def copy(self, t, key, arriving):
        kind, s, d, part = key
        own = d == 0 and not arriving
        if kind == "z":
            own = d == 1 and not arriving
            target = (self.dp, self.index(self.a - s, 0))
            chunk = self.index(self.a + s * d, 0) if arriving else self.index(self.a + s * (d - 1), 0)
        elif kind == "x":
            target = (self.dp, self.index(self.a, s))
            chunk = self.index(self.at(d), s if arriving else 0)
        elif kind == "y":
            target = (flip(self.dp, 1), self.mp)
            chunk = self.index(self.at(d), s)
            own = False
        else:
            target = (self.dp, self.index(self.a, 0, True))
            chunk = self.index(self.at(d), s, arriving)
            own = own and s == 0
        ref = self.alls[t]
        rows = ref.shape[1]
        if part is None:
            span = pl.ds(0, rows)
        else:
            which = 1 - part if kind == "y" and arriving else part
            which = self.half if which == 0 else 1 - self.half
            span = pl.ds(pl.multiple_of(which * (rows // 2), 16), rows // 2)
        src = self.inputs[t].at[span] if own else ref.at[chunk, span]
        number = self.keys[key]
        return pltpu.make_async_remote_copy(
            src_ref=src, dst_ref=ref.at[chunk, span], send_sem=self.send.at[t, number], recv_sem=self.recv.at[t, number],
            device_id=target, device_id_type=pl.DeviceIdType.MESH)

    def start(self, t, *key):
        guarded(self.sends(key), lambda: self.copy(t, key, False).start())

    def arrive(self, t, key):
        self.copy(t, key, True).wait_recv()

    def greet(self):
        barrier = pltpu.get_barrier_semaphore()
        partners = [(self.inside(d), (self.dp, self.index(self.a + d, 0))) for d in (1, -1)]
        partners += [(None, (self.dp, self.index(self.a, s))) for s in range(1, self.count_b)]
        partners += [(None, (self.dp, self.index(self.a, 0, True))), (None, (flip(self.dp, 1), self.mp))]
        for condition, device in partners:
            guarded(condition, lambda: pl.semaphore_signal(
                barrier, inc=1, device_id=device, device_id_type=pl.DeviceIdType.MESH))
        ends = 1 - (self.a % 3 + 1) // 2
        pl.semaphore_wait(barrier, len(partners) - ends)

    def open(self, t):
        for side in (1, -1):
            self.start(t, "z", side, 1, 0)
        for s in range(1, self.count_b):
            self.start(t, "x", s, 0, 0)
        self.start(t, "core", 0, 0, None)

    def pass_on(self, t, key):
        kind, s, d, part = key

        def body():
            self.arrive(t, key)
            if kind == "z":
                if d < (3 if part == 0 else 2):
                    self.start(t, "z", s, d + 1, part)
                at = s if d == 1 else d
                if part == 0:
                    for other in range(1, self.count_b):
                        self.start(t, "x", other, at, 0)
                    if d == 3:
                        self.start(t, "y", 0, 3, 0)
                self.start(t, "core", 0, at, part)
            elif kind == "x":
                if d != 3:
                    self.start(t, "y", s, d, 0)
                self.start(t, "core", s, d, part)
            else:
                if d == 3:
                    for other in range(1, self.count_b):
                        self.start(t, "x", other, 3, 1)
                self.start(t, "core", s, d, 1)

        guarded(self.gets(key), body)

    def level(self, t, n, along):
        for key in gather_events(self.count_b)[n]:
            if (key[0] == "z") == along:
                self.pass_on(t, key)
        if along and n < LINE - 1:
            for side in (1, -1):
                sent = LINE - 1 - self.a if side == 1 else self.a
                pl.when(sent == n)(lambda: self.start(t, "z", side, 1, 1))

    def from_core(self, n, along):
        keys = []
        for kind, s, d, part in gather_events(self.count_b)[n]:
            if (kind == "z") == along:
                if kind == "z":
                    key = ("core", 0, s if d == 1 else d, part)
                else:
                    key = ("core", s, d, 1 if kind == "y" else part)
                if key not in keys:
                    keys.append(key)
        for t in range(2):
            for key in keys:
                guarded(self.gets(key), lambda: self.arrive(t, key))

    def chip(self, o):
        n = self.count_b - 1
        end = self.a % 3 == 0
        one, two, three = 1 + n, 1 + 2 * n, 4 + 2 * n
        rank = jnp.where(o < one, 0, jnp.where(o <= two, 1, jnp.where(o == two + 1, jnp.where(end, 3, 2), jnp.where(
            o == two + 2, jnp.where(end, 2, 3), jnp.where(o < three + n, 2, 3)))))
        s = jnp.where(o < one, o, jnp.where(o < two, o - one + 1, jnp.where(o < three, 0, jnp.where(
            o < three + n, o - three + 1, o - three - n + 1))))
        a = jnp.where(rank == 0, self.a, jnp.where(rank == 1, 1 + self.a % 2, jnp.where(
            rank == 2, (2 + 3 * self.a) % 5, 3 - 3 * (self.a // 2))))
        return a * self.count_b + (self.b + s) % self.count_b

    def close(self, t):
        for key in self.keys:
            guarded(self.sends(key), lambda: self.copy(t, key, False).wait_send())


def forward_kernel(count_b, tok_hbm, wqkv_hbm, wo_hbm, up_hbm, down_in, seg_ref, pk_ref, pv_ref, bo_ref, g1_ref, s1_ref, db_ref, ub_ref,
                   q_hbm, k_hbm, v_hbm, mix_hbm, p_out, hat_hbm, two_hbm, up_all, down_all, slope_out, inv_hbm,
                   q_out, k_out, v_out, mix_out, hat_v, two, inv_v, tok_ref, wo_ref, up_in, wqkv_ref, vt, pvt, segc, bias, sbuf, mixt, low, up_v, down_v, pre, hid, slope, send, recv, wsem, qsem, osem, xsem):
    qb = pl.program_id(0)

    def copy_out(n):
        src = (q_out, k_out, v_out, mix_out, hat_v, two, inv_v)[n]
        return pltpu.make_async_copy(src, (q_hbm, k_hbm, v_hbm, mix_hbm, hat_hbm, two_hbm, inv_hbm)[n], xsem.at[n])

    gather = Gather(count_b, (up_in, down_in), (up_all, down_all), (send, recv))

    def pass_on(now):
        for slot, t, n, along in GATHER_SLOTS:
            if slot == now:
                gather.level(t, n, along)

    length, width = tok_ref.shape
    window = bias.shape[0]
    pairs = width // PAIR

    @pl.when(qb == 0)
    def _():
        def weights(part):
            cols = pl.ds(part * width, width)
            return pltpu.make_async_copy(wqkv_hbm.at[:, cols], wqkv_ref.at[:, cols], qsem.at[part])

        whole_in = [pltpu.make_async_copy(src, dst, qsem.at[3 + n]) for n, (src, dst) in enumerate((
            (up_hbm, up_in.at[pl.ds(0, width)]), (tok_hbm, tok_ref), (wo_hbm, wo_ref)))]
        whole_in[0].start()
        whole_in[1].start()
        for part in range(3):
            weights(part).start()
        whole_in[2].start()
        up_in[width:] = jnp.broadcast_to(ub_ref[...].astype(F32), (BIAS_ROWS, ub_ref.shape[1])).astype(BF16)
        gather.greet()
        whole_in[0].wait()
        gather.open(0)
        gather.open(1)
        tile = 256
        whole_in[1].wait()
        for part, ref in enumerate((q_out, k_out, v_out)):
            weights(part).wait()
            for j in range(width // tile):
                x = dot(tok_ref[...], wqkv_ref[:, part * width + j * tile:part * width + (j + 1) * tile]).astype(BF16)
                if part == 0:
                    x = x * jnp.asarray(HEAD_DIM ** -0.5, BF16)
                ref[:, j * tile:(j + 1) * tile] = x
                if (part, j) == QKV_SLOT:
                    pass_on(16)
            copy_out(part).start()
        whole_in[2].wait()
        big = eye(256)
        for j in range(width // 256):
            cols = slice(j * 256, (j + 1) * 256)
            vt[cols, :] = dot_t(big, v_out[:, cols]).astype(BF16)
            pvt[cols, :] = dot_t(big, pv_ref[:, cols]).astype(BF16)
        pass_on(0)
        ident = eye(QB)
        seg = jnp.broadcast_to(seg_ref[...].astype(F32), (QB, length)).astype(BF16)
        for j in range(length // QB):
            segc[j * QB:(j + 1) * QB, :] = dot_t(ident, seg[:, j * QB:(j + 1) * QB])

    for slot in range(1, length // QB):

        @pl.when(qb == slot)
        def _():
            pass_on(slot)

    start = pl.multiple_of(jnp.clip(qb * QB - QB, 0, length - window), QB)
    win = pl.ds(start, window)
    rows = pl.ds(pl.multiple_of(qb * QB, QB), QB)
    segq = seg_ref[:, rows].astype(F32)
    bias[...] = jnp.where(segc[win, :] == segq, 0.0, MASK_FILL)

    def score(pair):
        cols = slice(pair * PAIR, (pair + 1) * PAIR)
        keys = jnp.concatenate([k_out[win, cols], pk_ref[:, cols]], axis=0)
        sbuf[pair % 2] = dot_t(keys, split_heads(q_out[rows, cols]))

    def soft(pair):
        both = jnp.concatenate([bias[...], bias[...]], axis=1)
        sw = sbuf[pair % 2, :window] + both
        sp = sbuf[pair % 2, window:]
        top = jnp.maximum(jnp.max(sw, 0, keepdims=True), jnp.max(sp, 0, keepdims=True))
        ew = jnp.exp(sw - top)
        ep = jnp.exp(sp - top)
        inv = 1.0 / (jnp.sum(ew, 0, keepdims=True) + jnp.sum(ep, 0, keepdims=True))
        p_out[0, pair, :window] = (ew * inv).astype(BF16)
        p_out[0, pair, window:] = (ep * inv).astype(BF16)

    def mixing(pair):
        cols = slice(pair * PAIR, (pair + 1) * PAIR)
        vals = jnp.concatenate([vt[cols, win], pvt[cols, :]], axis=1)
        mixt[cols, rows] = own_blocks(dot(vals, p_out[0, pair])).astype(BF16)

    for i in range(pairs + 2):
        if i < pairs:
            score(i)
        if 0 <= i - 1 < pairs:
            soft(i - 1)
        if 0 <= i - 2 < pairs:
            mixing(i - 2)

    @pl.when(qb == pl.num_programs(0) - 1)
    def _():
        pass_on(8)
        big = eye(256)
        for r in range(length // 256):
            rr = slice(r * 256, (r + 1) * 256)
            mix_out[rr] = dot_t(big, mixt[:, rr]).astype(BF16)
        copy_out(3).start()
        for r in range(length // 256):
            rr = slice(r * 256, (r + 1) * 256)
            res = tok_ref[rr].astype(F32) + dot(mix_out[rr], wo_ref[...]) + bo_ref[...]
            hat, inv = normalize(res)
            hat_v[rr] = hat
            inv_v[rr] = jnp.broadcast_to(inv, (256, 128))
            first = hat * g1_ref[...] + s1_ref[...]
            low[rr] = first.astype(BF16)
            two[rr] = first + db_ref[...]
        copy_out(4).start()
        copy_out(6).start()
        pass_on(9)

        chips = LINE * count_b
        ffl = down_in.shape[0]
        per = length // 256

        def loads(o):
            chip = gather.chip(o)
            out = []
            for c in range(2):
                core = gather.core if c else 1 - gather.core
                cols = pl.ds(pl.multiple_of(core * ffl, 128), ffl)
                own = isinstance(o, int) and o == 0 and c == 1
                for t, to in ((0, up_v.at[o % 3, :, cols]), (1, down_v.at[o % 3, cols])):
                    src = (up_in, down_in)[t] if own else (up_all, down_all)[t].at[2 * chip + core]
                    out.append(pltpu.make_async_copy(src, to, wsem.at[o % 3, t, c]))
            return out

        def load(o):
            for copy in loads(o):
                copy.start()

        def loaded(o):
            for copy in loads(o):
                copy.wait()

        def rows_of(b):
            return slice(b * 256, (b + 1) * 256)

        def up(o, b):
            pre[b % 2] = dot(low[rows_of(b)], up_v[o % 3, :width, :])

        def act(o, b):
            u = pre[b % 2] + up_v[o % 3, width:width + 1, :].astype(F32)
            half = 0.5 * lax.erf(u * ROOT_HALF) + 0.5
            hid[b % 2] = (u * half).astype(BF16)
            slope[o, rows_of(b)] = (half + u * (jnp.exp(-0.5 * u * u) * INV_ROOT_TWOPI)).astype(BF16)

        def down(o, b):
            two[rows_of(b)] += dot(hid[b % 2], down_v[o % 3])

        def earlier(o, b, n):
            return (o, b - n) if b >= n else (o - 1, b - n + per)

        def chip_steps(o, ahead):
            loaded(o)
            ahead()
            for b in range(per):
                up(o, b)
                if b >= 1 or not (isinstance(o, int) and o == 0):
                    act(*earlier(o, b, 1))
                if b >= 2 or not (isinstance(o, int) and o == 0):
                    down(*earlier(o, b, 2))

        def keep(o):
            return pltpu.make_async_copy(slope.at[o], slope_out.at[gather.chip(o)], osem.at[o])

        def more():
            pass_on(10)
            for n in range(2):
                for along in (True, False):
                    gather.from_core(n, along)

        for t in range(2):
            gather.arrive(t, ("core", 0, 0, None))
        load(0)

        def first_ahead():
            more()
            load(1)

        chip_steps(0, first_ahead)
        others = count_b - 1
        needs = ((others, 11, 2, (True, False)), (2 * others, 12, 3, (True,)), (2 * others + 1, 13, 3, (False,)),
                 (2 * others + 2, 14, 4, (True,)), (2 * others + 3, 15, 4, (False,)))

        def chip_step(o, carry):
            def ahead():
                for at, slot, n, kinds in needs:

                    @pl.when(o == at)
                    def _():
                        pass_on(slot)
                        for along in kinds:
                            gather.from_core(n, along)

                @pl.when(o < chips - 1)
                def _():
                    load(o + 1)

            chip_steps(o, ahead)
            keep(o - 1).start()
            return carry

        lax.fori_loop(1, chips, chip_step, 0)
        act(chips - 1, per - 1)
        down(chips - 1, per - 2)
        down(chips - 1, per - 1)
        copy_out(5).start()
        keep(chips - 1).start()
        for t in range(2):
            gather.close(t)
        for o in range(chips):
            keep(o).wait()
        for n in range(7):
            copy_out(n).wait()


def attend_forward(tok, wqkv, wo, up, down, seg, pk, pv, bo, g1, s1, db, ub, group):
    length, width = tok.shape
    pre = pk.shape[0]
    window = 3 * QB
    pairs, blocks = width // PAIR, length // QB
    hbm = pl.BlockSpec(memory_space=pl.ANY)
    square, wide = jax.ShapeDtypeStruct((length, width), BF16), jax.ShapeDtypeStruct((length, width), F32)
    outs = [(hbm, square)] * 4 + [
        (pl.BlockSpec((1, pairs, window + pre, 2 * QB), lambda i: (i, 0, 0, 0)),
         jax.ShapeDtypeStruct((blocks, pairs, window + pre, 2 * QB), BF16)),
        (hbm, wide), (hbm, wide)]
    up_shape = (width + BIAS_ROWS, up.shape[1])
    outs += [(hbm, jax.ShapeDtypeStruct((group,) + shape, BF16)) for shape in (up_shape, down.shape)]
    chips, part = group // 2, 2 * down.shape[0]
    outs += [(hbm, jax.ShapeDtypeStruct((chips, length, part), BF16)), (hbm, jax.ShapeDtypeStruct((length, 128), F32))]
    count_b = group // (2 * LINE)
    pieces = len(gather_keys(count_b))
    return pl.pallas_call(
        functools.partial(forward_kernel, count_b),
        grid=(blocks,),
        in_specs=[hbm] * 5 + [whole(a) for a in (seg, pk, pv, bo, g1, s1, db, ub)],
        out_specs=[o[0] for o in outs],
        out_shape=[o[1] for o in outs],
        scratch_shapes=[pltpu.VMEM((length, width), t) for t in (BF16, BF16, BF16, BF16, F32, F32)] + [
            pltpu.VMEM((length, 128), F32),
            pltpu.VMEM((length, width), BF16),
            pltpu.VMEM((width, width), BF16),
            pltpu.VMEM(up_shape, BF16),
            pltpu.VMEM(wqkv.shape, BF16),
            pltpu.VMEM((width, length), BF16),
            pltpu.VMEM((width, pre), BF16),
            pltpu.VMEM((length, QB), F32),
            pltpu.VMEM((window, QB), F32),
            pltpu.VMEM((2, window + pre, 2 * QB), F32),
            pltpu.VMEM((width, length), BF16),
            pltpu.VMEM((length, width), BF16),
            pltpu.VMEM((3, up_shape[0], part), BF16),
            pltpu.VMEM((3, part, width), BF16),
            pltpu.VMEM((2, 256, part), F32),
            pltpu.VMEM((2, 256, part), BF16),
            pltpu.VMEM((chips, length, part), BF16),
            pltpu.SemaphoreType.DMA((2, pieces)),
            pltpu.SemaphoreType.DMA((2, pieces)),
            pltpu.SemaphoreType.DMA((3, 2, 2)),
            pltpu.SemaphoreType.DMA((6,)),
            pltpu.SemaphoreType.DMA((chips,)),
            pltpu.SemaphoreType.DMA((7,)),
        ],
        compiler_params=pltpu.CompilerParams(vmem_limit_bytes=VMEM_LIMIT, collective_id=0, has_side_effects=True),
        name="attend_forward",
    )(tok, wqkv, wo, up, down, seg, pk, pv, bo, g1, s1, db, ub)


def ffn_kernel(hat_ref, inv_ref, two_ref, dy_ref, slope_ref, up_hbm, down_hbm, up_own, down_own, wo_ref, g1_ref, g2_ref, s2_ref,
               out_ref, gone_ref, gmix_ref, up, down, hid, low, acc, sems):
    step = pl.program_id(0)
    width = up.shape[0]
    parts, part, _ = down_hbm.shape
    count, _, chunk = slope_ref.shape
    me = lax.axis_index("mp")

    def fetch(d, t, own):
        cols = pl.ds(d * part, part)
        up_src, down_src = (up_own, down_own) if own else (up_hbm.at[d], down_hbm.at[d])
        src, dst = ((up_src.at[pl.ds(0, width)], up.at[:, cols]), (down_src, down.at[cols]))[t]
        return pltpu.make_async_copy(src, dst, sems.at[t, d])

    @pl.when(step == 0)
    def _():
        for h in range(2):
            for t in (1, 0):
                for d in range(h * parts // 2, (h + 1) * parts // 2):

                    @pl.when(me == d)
                    def _():
                        fetch(d, t, True).start()

                    @pl.when(me != d)
                    def _():
                        fetch(d, t, False).start()

    def await_half(t, h):
        @pl.when(step == 0)
        def _():
            for d in range(h * parts // 2, (h + 1) * parts // 2):
                fetch(d, t, False).wait()

    hat2, inv2 = normalize(two_ref[...])
    out_ref[...] = (hat2 * g2_ref[...] + s2_ref[...]).astype(BF16)
    grad_two = norm_back(dy_ref[...].astype(F32), hat2, inv2, g2_ref[...])
    acc[...] = grad_two
    low[...] = grad_two.astype(BF16)

    def cols_of(j):
        return slice(j * chunk, (j + 1) * chunk)

    def back_down(j):
        gh = dot_t(low[...], down[cols_of(j)])
        hid[j % 2] = (gh * slope_ref[j].astype(F32)).astype(BF16)

    def back_up(j):
        acc[...] += dot_t(hid[j % 2], up[:, cols_of(j)])

    await_half(1, 0)
    for j in range(count + 1):
        if j == count // 2:
            await_half(1, 1)
        if j < count:
            back_down(j)
        if j in (1, count // 2 + 1):
            await_half(0, j // (count // 2 + 1))
        if j >= 1:
            back_up(j - 1)

    grad_one = norm_back(acc[...], hat_ref[...], inv_ref[:, 0:1], g1_ref[...])
    gone_ref[...] = grad_one
    gmix_ref[...] = dot_t(grad_one.astype(BF16), wo_ref[...]).astype(BF16)


def feed_forward_backward(hat, inv, two, dy, slope, up, down, up_own, down_own, wo, g1, g2, s2, tb=256):
    rows, width = hat.shape
    parts, ffl, _ = down.shape
    ff = parts * ffl
    chips, _, part = slope.shape
    block = pl.BlockSpec((tb, width), lambda i: (i, 0))
    hbm = pl.BlockSpec(memory_space=pl.ANY)
    return pl.pallas_call(
        ffn_kernel,
        grid=(rows // tb,),
        in_specs=[block, pl.BlockSpec((tb, 128), lambda i: (i, 0))] + [block] * 2 + [pl.BlockSpec((chips, tb, part), lambda i: (0, i, 0))] + [hbm] * 4
        + [whole(a) for a in (wo, g1, g2, s2)],
        out_specs=[block] * 3,
        out_shape=[jax.ShapeDtypeStruct((rows, width), t) for t in (BF16, F32, BF16)],
        scratch_shapes=[
            pltpu.VMEM((width, ff), BF16),
            pltpu.VMEM((ff, width), BF16),
            pltpu.VMEM((2, tb, part), BF16),
            pltpu.VMEM((tb, width), BF16),
            pltpu.VMEM((tb, width), F32),
            pltpu.SemaphoreType.DMA((2, parts)),
        ],
        compiler_params=pltpu.CompilerParams(vmem_limit_bytes=VMEM_LIMIT),
        name="feed_forward_backward",
    )(hat, inv, two, dy, slope, up, down, up_own, down_own, wo, g1, g2, s2)


class Total:
    def __init__(self, count_dp, count_mp, low, slots, parts, result, sems):
        self.low, self.slots, self.parts, self.result = low, slots, parts, result
        self.sems = sems
        self.count_b = count_mp // (2 * LINE)
        self.high_b, self.high_dp = self.count_b // 2, count_dp // 2
        self.count_q = LINE * self.high_b * self.high_dp
        dp, mp = lax.axis_index("dp"), lax.axis_index("mp")
        b = (mp // 2) % self.count_b
        a = mp // (2 * self.count_b)
        self.g = ((dp % 2) * 2 + b % 2) * 2 + mp % 2
        self.q = (a * self.high_b + b // 2) * self.high_dp + dp // 2

    def device(self, g, q):
        a, high = q // (self.high_b * self.high_dp), q % (self.high_b * self.high_dp)
        dp = (high % self.high_dp) * 2 + g // 4
        b = (high // self.high_dp) * 2 + (g // 2) % 2
        return dp, (a * self.count_b + b) * 2 + g % 2

    def near(self, j):
        return self.device((self.g + j) % 8, self.q)

    def far(self, i):
        return self.device(self.g, (self.q + i) % self.count_q)

    def copy(self, phase, j, arriving=False):
        if phase == 0:
            src, dst, to = self.low.at[(self.g + j) % 8], self.slots.at[j], self.near(j)
        elif phase == 1:
            at = (self.q + self.count_q - j) % self.count_q if arriving else self.q
            src, dst, to = self.parts.at[at], self.parts.at[at], self.far(j)
        else:
            at = (self.g + 8 - j) % 8 if arriving else self.g
            src, dst, to = self.result.at[at], self.result.at[at], self.near(j)
        send, recv = self.sems[phase]
        return pltpu.make_async_remote_copy(
            src_ref=src, dst_ref=dst, send_sem=send.at[j], recv_sem=recv.at[j], device_id=to,
            device_id_type=pl.DeviceIdType.MESH)

    def peers(self, phase):
        return range(1, self.count_q if phase == 1 else 8)

    def partners(self):
        return [self.near(j) for j in self.peers(0)] + [self.far(i) for i in self.peers(1)]

    def greet(self):
        barrier = pltpu.get_barrier_semaphore()
        for device in self.partners():
            pl.semaphore_signal(barrier, inc=1, device_id=device, device_id_type=pl.DeviceIdType.MESH)

    def start(self, phase):
        for j in self.peers(phase):
            self.copy(phase, j).start()

    def arrive(self, phase):
        for j in self.peers(phase):
            self.copy(phase, j, True).wait_recv()

    def first(self):
        pl.semaphore_wait(pltpu.get_barrier_semaphore(), len(self.partners()))
        self.start(0)

    def second(self):
        self.arrive(0)
        total = self.low[self.g].astype(F32)
        for j in self.peers(0):
            total = total + self.slots[j].astype(F32)
        self.parts[self.q] = total.astype(BF16)
        self.start(1)

    def third(self):
        self.arrive(1)
        total = self.parts[0].astype(F32)
        for i in range(1, self.count_q):
            total = total + self.parts[i].astype(F32)
        self.result[self.g] = total.astype(BF16)
        self.start(2)

    def last(self):
        self.arrive(2)
        for phase in range(3):
            for j in self.peers(phase):
                self.copy(phase, j).wait_send()


def backward_kernel(counts, p_ref, q_ref, k_ref, v_ref, mix_ref, do_ref, pk_ref, pv_ref, w_hbm, gone_hbm,
                    out_ref, gk_ref, gv_ref, w_ref, gone_ref, kt, dk, dv, gj, delta, gbuf, ds_all, dqt, low, slots, parts, result,
                    send0, recv0, send1, recv1, send2, recv2, late):
    pair = pl.program_id(0)
    loads = [pltpu.make_async_copy(w_hbm, w_ref, late.at[0]), pltpu.make_async_copy(gone_hbm, gone_ref, late.at[1])]

    total = Total(*counts, low, slots, parts, result, ((send0, recv0), (send1, recv1), (send2, recv2)))

    @pl.when(pair == 0)
    def _():
        total.greet()
        for copy in loads:
            copy.start()

    length = q_ref.shape[0]
    pre = pk_ref.shape[0]
    pairs, width = ds_all.shape[0], out_ref.shape[1]
    blocks = length // QB
    depth = p_ref.shape[2]
    window = depth - pre
    ident = eye(QB)
    sub = lax.broadcasted_iota(jnp.int32, (8, PAIR), 0)
    lane = lax.broadcasted_iota(jnp.int32, (8, PAIR), 1)
    pick = jnp.where((sub == 0) == (lane < HEAD_DIM), 1.0, 0.0).astype(BF16)
    dk[...] = jnp.zeros_like(dk)
    dv[...] = jnp.zeros_like(dv)
    kt[pair, :, :length] = dot_t(ident, k_ref[...]).astype(BF16)
    kt[pair, :, length:] = dot_t(ident, pk_ref[...]).astype(BF16)
    prod = do_ref[...].astype(F32) * mix_ref[...].astype(F32)
    high = prod.astype(BF16)
    rest = (prod - high.astype(F32)).astype(BF16)
    delta[...] = dot_t(pick, high) + dot_t(pick, rest)

    def where_of(qb):
        start = min(max(qb * QB - QB, 0), length - window)
        return slice(start, start + window), slice(qb * QB, (qb + 1) * QB)

    def grad_probs(qb):
        win, rows = where_of(qb)
        vals = jnp.concatenate([v_ref[win], pv_ref[...]], axis=0)
        gbuf[qb % 2] = dot_t(vals, split_heads(do_ref[rows]))

    def grad_scores(qb):
        win, rows = where_of(qb)
        d = jnp.concatenate([delta[0:1, rows], delta[1:2, rows]], axis=1)
        ds_all[pair, qb] = (p_ref[qb, 0].astype(F32) * (gbuf[qb % 2] - d)).astype(BF16)

    def grads(qb):
        win, rows = where_of(qb)
        dva = dot(p_ref[qb, 0], split_heads(do_ref[rows]))
        dv[win] += dva[:window]
        dv[length:] += dva[window:]
        dka = dot(ds_all[pair, qb], split_heads(q_ref[rows]))
        dk[win] += dka[:window]
        dk[length:] += dka[window:]

    for i in range(blocks + 2):
        if i < blocks:
            grad_probs(i)
        if 0 <= i - 1 < blocks:
            grad_scores(i - 1)
        if 0 <= i - 2 < blocks:
            grads(i - 2)
    gj[pair, :, 0:PAIR] = dk[:length].astype(BF16)
    gj[pair, :, PAIR:] = dv[:length].astype(BF16)
    cols = pl.ds(pl.multiple_of(pair * PAIR, PAIR), PAIR)
    each = 2 * pre // 8
    for part, ref in enumerate((dk, dv)):
        for i in range(4):
            low[part * 4 + i, :, cols] = ref[length + i * each:length + (i + 1) * each].astype(BF16)

    @pl.when(pair == pl.num_programs(0) - 1)
    def _():
        total.first()

        def query_grads(i, carry):
            rows_of = pl.ds(pl.multiple_of(i * PAIR, PAIR), PAIR)
            for qb in range(blocks):
                win, rows = where_of(qb)
                keys = jnp.concatenate([kt[i, :, win], kt[i, :, length:]], axis=1)
                dqt[rows_of, rows] = own_blocks(dot(keys, ds_all[i, qb]) * HEAD_DIM ** -0.5).astype(BF16)
            return carry

        lax.fori_loop(0, pairs // 2, query_grads, 0)
        total.second()
        lax.fori_loop(pairs // 2, pairs, query_grads, 0)
        total.third()
        for copy in loads:
            copy.wait()
        big = eye(256)
        for r in range(length // 256):
            rr = slice(r * 256, (r + 1) * 256)
            acc = gone_ref[rr] + dot_t(dot_t(big, dqt[:, rr]).astype(BF16), w_ref[:, :width])
            for part in range(2):
                x = jnp.concatenate([gj[i, rr, part * PAIR:(part + 1) * PAIR] for i in range(pairs)], axis=1)
                acc = acc + dot_t(x, w_ref[:, (part + 1) * width:(part + 2) * width])
            out_ref[rr] = acc.astype(BF16)
        total.last()
        for i in range(4):
            gk_ref[i * each:(i + 1) * each] = result[i].astype(F32)
            gv_ref[i * each:(i + 1) * each] = result[4 + i].astype(F32)


def attend_backward(p, q, k, v, mix, do, pk, pv, wqkv, gone, counts):
    length, width = q.shape
    pre = pk.shape[0]
    blocks, pairs, depth, _ = p.shape

    def col(a):
        return pl.BlockSpec((a.shape[0], PAIR), lambda i: (0, i))

    vmem = pl.BlockSpec(memory_space=pltpu.VMEM)
    outs = [(vmem, jax.ShapeDtypeStruct((length, width), BF16))] + [(vmem, jax.ShapeDtypeStruct((pre, width), F32))] * 2
    count_q = counts[0] * counts[1] // 8
    piece = (2 * pre // 8, width)
    return pl.pallas_call(
        functools.partial(backward_kernel, counts),
        grid=(pairs,),
        in_specs=[pl.BlockSpec((blocks, 1, depth, 2 * QB), lambda i: (0, i, 0, 0))]
        + [col(a) for a in (q, k, v, mix, do, pk, pv)] + [pl.BlockSpec(memory_space=pl.ANY)] * 2,
        out_specs=[o[0] for o in outs],
        out_shape=[o[1] for o in outs],
        scratch_shapes=[
            pltpu.VMEM(wqkv.shape, BF16),
            pltpu.VMEM((length, width), F32),
            pltpu.VMEM((pairs, PAIR, length + pre), BF16),
            pltpu.VMEM((length + pre, PAIR), F32),
            pltpu.VMEM((length + pre, PAIR), F32),
            pltpu.VMEM((pairs, length, 2 * PAIR), BF16),
            pltpu.VMEM((8, length), F32),
            pltpu.VMEM((2, depth, 2 * QB), F32),
            pltpu.VMEM((pairs, blocks, depth, 2 * QB), BF16),
            pltpu.VMEM((width, length), BF16),
            pltpu.VMEM((8,) + piece, BF16),
            pltpu.VMEM((8,) + piece, BF16),
            pltpu.VMEM((count_q,) + piece, BF16),
            pltpu.VMEM((8,) + piece, BF16),
        ] + [pltpu.SemaphoreType.DMA((n,)) for n in (8, 8, count_q, count_q, 8, 8, 2)],
        compiler_params=pltpu.CompilerParams(vmem_limit_bytes=BACKWARD_LIMIT, collective_id=1, has_side_effects=True),
        name="attend_backward",
    )(p, q, k, v, mix, do, pk, pv, wqkv, gone)


def hand_over_kernel(*refs):
    n = len(refs) // 2
    for src, dst in zip(refs[:n], refs[n:]):
        dst[...] = src[...]


def hand_over(*arrays):
    steps = 4
    specs = [pl.BlockSpec((a.shape[0] // steps, a.shape[1]), lambda i: (i, 0)) for a in arrays]
    return pl.pallas_call(
        hand_over_kernel,
        grid=(steps,),
        in_specs=specs,
        out_specs=specs,
        out_shape=[jax.ShapeDtypeStruct(a.shape, a.dtype) for a in arrays],
        name="hand_over",
    )(*arrays)


def on_device(counts, tokens, segment_ids, qkv_weight, prefix_keys, prefix_values, out_weight, out_bias, norm1_gain,
              norm1_shift, up_weight, up_bias, down_weight, down_bias, norm2_gain, norm2_shift, out_grad):
    row = lambda a: a.reshape(1, -1)
    q, k, v, mix, probs, hat, two, up_all, down_all, slope, inv = attend_forward(
        tokens[0], qkv_weight, out_weight, up_weight, down_weight, segment_ids, prefix_keys, prefix_values, row(out_bias),
        row(norm1_gain), row(norm1_shift), row(down_bias), row(up_bias), counts[1])
    out, grad_one, grad_mixed = feed_forward_backward(
        hat, inv, two, out_grad[0], slope, up_all, down_all, up_weight, down_weight, out_weight, row(norm1_gain), row(norm2_gain),
        row(norm2_shift))
    grad_tokens, total_k, total_v = hand_over(*attend_backward(
        probs, q, k, v, mix, grad_mixed, prefix_keys, prefix_values, qkv_weight, grad_one, counts))
    return out[None], grad_tokens[None], total_k, total_v


def solution(mesh):
    rows = P(("dp", "mp"), None, None)
    return jax.shard_map(
        functools.partial(on_device, (mesh.shape["dp"], mesh.shape["mp"])),
        mesh=mesh,
        in_specs=(rows, P(("dp", "mp"), None), P(), P(), P(), P(), P(), P(), P(), P(None, "mp"), P("mp"), P("mp", None),
                  P(), P(), P(), rows),
        out_specs=(rows, rows, P(), P()),
        check_vma=False,
    )
```

```python
import functools

import jax
import jax.numpy as jnp
from jax import lax
from jax.experimental import pallas as pl
from jax.experimental.pallas import tpu as pltpu
from jax.sharding import PartitionSpec as P

EPSILON = 1e-05
ROOT_HALF = 0.7071067811865476
INV_ROOT_TWOPI = 0.3989422804014327
MASK_FILL = -1e30
HEAD_DIM = 64
PAIR = 2 * HEAD_DIM
QB = 128
F32 = jnp.float32
BF16 = jnp.bfloat16
VMEM_LIMIT = 62 * 1024 * 1024
BACKWARD_LIMIT = 56 * 1024 * 1024
BIAS_ROWS = 32
QKV_SLOT = (1, 1)
GATHER_SLOTS = (
    (16, 0, 0, True), (16, 0, 0, False),
    (2, 1, 0, True), (2, 1, 0, False),
    (4, 0, 1, True),
    (6, 1, 1, True), (6, 0, 1, False),
    (7, 0, 2, True),
    (8, 1, 1, False),
    (9, 1, 2, True), (9, 0, 2, False),
    (11, 0, 3, True), (11, 1, 2, False),
    (12, 1, 3, True), (12, 0, 3, False),
    (13, 1, 3, False),
    (14, 0, 4, True), (14, 1, 4, True),
    (15, 0, 4, False), (15, 1, 4, False),
)


def dot(a, b):
    return lax.dot_general(a, b, (((1,), (0,)), ((), ())), preferred_element_type=F32)


def dot_t(a, b):
    return lax.dot_general(a, b, (((1,), (1,)), ((), ())), preferred_element_type=F32)


def eye(n):
    r = lax.broadcasted_iota(jnp.int32, (n, n), 0)
    c = lax.broadcasted_iota(jnp.int32, (n, n), 1)
    return jnp.where(r == c, 1.0, 0.0).astype(BF16)


def split_heads(x):
    lane = lax.broadcasted_iota(jnp.int32, x.shape, 1)
    zero = jnp.zeros_like(x)
    return jnp.concatenate([jnp.where(lane < HEAD_DIM, x, zero), jnp.where(lane < HEAD_DIM, zero, x)], axis=0)


def own_blocks(x):
    return jnp.concatenate([x[:HEAD_DIM, :QB], x[HEAD_DIM:, QB:]], axis=0)


def normalize(x):
    scale = 1.0 / x.shape[-1]
    cen = x - jnp.sum(x, -1, keepdims=True) * scale
    inv = lax.rsqrt(jnp.sum(cen * cen, -1, keepdims=True) * scale + EPSILON)
    return cen * inv, inv


def norm_back(grad, hat, inv, gain):
    scale = 1.0 / grad.shape[-1]
    sc = grad * gain
    mean1 = jnp.sum(sc, -1, keepdims=True) * scale
    mean2 = jnp.sum(sc * hat, -1, keepdims=True) * scale
    return (sc - mean1 - hat * mean2) * inv


def whole(a):
    return pl.BlockSpec(a.shape, lambda i: (0,) * a.ndim, pipeline_mode=pl.Buffered(1))


def kept(shape, dtype):
    spec = pl.BlockSpec(shape, lambda i: (0,) * len(shape), pipeline_mode=pl.Buffered(1))
    return spec, jax.ShapeDtypeStruct(shape, dtype)


LINE = 4


def flip(x, bits):
    bit = 1
    while bit <= bits:
        if bits & bit:
            x = x + bit - 2 * bit * ((x // bit) % 2)
        bit *= 2
    return x


def guarded(condition, body):
    if condition is None:
        body()
    else:
        pl.when(condition)(body)


def gather_keys(count_b):
    others = range(1, count_b)
    keys = [("z", side, d, 0) for side in (1, -1) for d in (1, 2, 3)]
    keys += [("z", side, d, 1) for side in (1, -1) for d in (1, 2)]
    for s in others:
        keys += [("x", s, d, 0) for d in (0, 1, -1, 2, 3)] + [("x", s, 3, 1)]
        keys += [("y", s, d, 0) for d in (0, 1, -1, 2)]
    keys.append(("y", 0, 3, 0))
    keys.append(("core", 0, 0, None))
    for s in range(count_b):
        keys += [("core", s, d, part) for d in (0, 1, -1, 2, 3) for part in (0, 1) if (s, d) != (0, 0)]
    return {key: i for i, key in enumerate(keys)}


def gather_events(count_b):
    others = range(1, count_b)
    sides = (1, -1)
    return [
        [("x", s, 0, 0) for s in others] + [("z", side, 1, 0) for side in sides],
        [("z", side, 2, 0) for side in sides] + [("x", s, d, 0) for s in others for d in sides] + [("y", s, 0, 0) for s in others],
        [("z", side, 3, 0) for side in sides] + [("x", s, 2, 0) for s in others] + [("y", s, d, 0) for s in others for d in sides],
        [("z", side, 1, 1) for side in sides] + [("y", 0, 3, 0)] + [("x", s, 3, 0) for s in others],
        [("z", side, 2, 1) for side in sides] + [("y", s, 2, 0) for s in others] + [("x", s, 3, 1) for s in others],
    ]


class Gather:
    def __init__(self, count_b, inputs, alls, sems):
        self.count_b = count_b
        self.inputs, self.alls = inputs, alls
        self.send, self.recv = sems
        self.dp = lax.axis_index("dp")
        self.mp = lax.axis_index("mp")
        self.core = self.mp % 2
        self.b = (self.mp // 2) % self.count_b
        self.a = self.mp // (2 * self.count_b)
        self.half = self.dp % 2
        self.keys = gather_keys(count_b)

    def index(self, a, s, other=False):
        core = 1 - self.core if other else self.core
        return (a * self.count_b + flip(self.b, s)) * 2 + core

    def at(self, d):
        if d in (2, 3):
            return self.a + d - 2 * d * ((self.a + d) // LINE)
        return self.a + d

    def inside(self, d):
        if d == 1:
            return self.a < LINE - 1
        if d == -1:
            return self.a > 0
        if d == 3:
            return self.a % 3 == 0
        return None

    def gets(self, key):
        kind, s, d, part = key
        if kind != "z":
            return self.inside(d)
        return self.a + d < LINE if s == 1 else self.a >= d

    def sends(self, key):
        kind, s, d, part = key
        if kind != "z":
            return self.inside(d)
        low, high = (1, LINE - d) if s == 1 else (d - 1, LINE - 2)
        return (self.a >= low) & (self.a <= high)

    def copy(self, t, key, arriving):
        kind, s, d, part = key
        own = d == 0 and not arriving
        if kind == "z":
            own = d == 1 and not arriving
            target = (self.dp, self.index(self.a - s, 0))
            chunk = self.index(self.a + s * d, 0) if arriving else self.index(self.a + s * (d - 1), 0)
        elif kind == "x":
            target = (self.dp, self.index(self.a, s))
            chunk = self.index(self.at(d), s if arriving else 0)
        elif kind == "y":
            target = (flip(self.dp, 1), self.mp)
            chunk = self.index(self.at(d), s)
            own = False
        else:
            target = (self.dp, self.index(self.a, 0, True))
            chunk = self.index(self.at(d), s, arriving)
            own = own and s == 0
        ref = self.alls[t]
        rows = ref.shape[1]
        if part is None:
            span = pl.ds(0, rows)
        else:
            which = 1 - part if kind == "y" and arriving else part
            which = self.half if which == 0 else 1 - self.half
            span = pl.ds(pl.multiple_of(which * (rows // 2), 16), rows // 2)
        src = self.inputs[t].at[span] if own else ref.at[chunk, span]
        number = self.keys[key]
        return pltpu.make_async_remote_copy(
            src_ref=src, dst_ref=ref.at[chunk, span], send_sem=self.send.at[t, number], recv_sem=self.recv.at[t, number],
            device_id=target, device_id_type=pl.DeviceIdType.MESH)

    def start(self, t, *key):
        guarded(self.sends(key), lambda: self.copy(t, key, False).start())

    def arrive(self, t, key):
        self.copy(t, key, True).wait_recv()

    def greet(self):
        barrier = pltpu.get_barrier_semaphore()
        partners = [(self.inside(d), (self.dp, self.index(self.a + d, 0))) for d in (1, -1)]
        partners += [(None, (self.dp, self.index(self.a, s))) for s in range(1, self.count_b)]
        partners += [(None, (self.dp, self.index(self.a, 0, True))), (None, (flip(self.dp, 1), self.mp))]
        for condition, device in partners:
            guarded(condition, lambda: pl.semaphore_signal(
                barrier, inc=1, device_id=device, device_id_type=pl.DeviceIdType.MESH))
        ends = 1 - (self.a % 3 + 1) // 2
        pl.semaphore_wait(barrier, len(partners) - ends)

    def open(self, t):
        for side in (1, -1):
            self.start(t, "z", side, 1, 0)
        for s in range(1, self.count_b):
            self.start(t, "x", s, 0, 0)
        self.start(t, "core", 0, 0, None)

    def pass_on(self, t, key):
        kind, s, d, part = key

        def body():
            self.arrive(t, key)
            if kind == "z":
                if d < (3 if part == 0 else 2):
                    self.start(t, "z", s, d + 1, part)
                at = s if d == 1 else d
                if part == 0:
                    for other in range(1, self.count_b):
                        self.start(t, "x", other, at, 0)
                    if d == 3:
                        self.start(t, "y", 0, 3, 0)
                self.start(t, "core", 0, at, part)
            elif kind == "x":
                if d != 3:
                    self.start(t, "y", s, d, 0)
                self.start(t, "core", s, d, part)
            else:
                if d == 3:
                    for other in range(1, self.count_b):
                        self.start(t, "x", other, 3, 1)
                self.start(t, "core", s, d, 1)

        guarded(self.gets(key), body)

    def level(self, t, n, along):
        for key in gather_events(self.count_b)[n]:
            if (key[0] == "z") == along:
                self.pass_on(t, key)
        if along and n < LINE - 1:
            for side in (1, -1):
                sent = LINE - 1 - self.a if side == 1 else self.a
                pl.when(sent == n)(lambda: self.start(t, "z", side, 1, 1))

    def from_core(self, n, along):
        keys = []
        for kind, s, d, part in gather_events(self.count_b)[n]:
            if (kind == "z") == along:
                if kind == "z":
                    key = ("core", 0, s if d == 1 else d, part)
                else:
                    key = ("core", s, d, 1 if kind == "y" else part)
                if key not in keys:
                    keys.append(key)
        for t in range(2):
            for key in keys:
                guarded(self.gets(key), lambda: self.arrive(t, key))

    def chip(self, o):
        n = self.count_b - 1
        end = self.a % 3 == 0
        one, two, three = 1 + n, 1 + 2 * n, 4 + 2 * n
        rank = jnp.where(o < one, 0, jnp.where(o <= two, 1, jnp.where(o == two + 1, jnp.where(end, 3, 2), jnp.where(
            o == two + 2, jnp.where(end, 2, 3), jnp.where(o < three + n, 2, 3)))))
        s = jnp.where(o < one, o, jnp.where(o < two, o - one + 1, jnp.where(o < three, 0, jnp.where(
            o < three + n, o - three + 1, o - three - n + 1))))
        a = jnp.where(rank == 0, self.a, jnp.where(rank == 1, 1 + self.a % 2, jnp.where(
            rank == 2, (2 + 3 * self.a) % 5, 3 - 3 * (self.a // 2))))
        return a * self.count_b + (self.b + s) % self.count_b

    def close(self, t):
        for key in self.keys:
            guarded(self.sends(key), lambda: self.copy(t, key, False).wait_send())


def forward_kernel(count_b, tok_hbm, wqkv_hbm, wo_hbm, up_hbm, down_in, seg_ref, pk_ref, pv_ref, bo_ref, g1_ref, s1_ref, db_ref, ub_ref,
                   q_hbm, k_hbm, v_hbm, mix_hbm, p_out, hat_hbm, two_hbm, up_all, down_all, slope_out, inv_hbm,
                   q_out, k_out, v_out, mix_out, hat_v, two, inv_v, tok_ref, wo_ref, up_in, wqkv_ref, vt, pvt, segc, bias, sbuf, mixt, low, up_v, down_v, pre, hid, slope, send, recv, wsem, qsem, osem, xsem, tsem):
    qb = pl.program_id(0)

    def copy_out(n):
        src = (q_out, k_out, v_out, mix_out, hat_v, two, inv_v)[n]
        return pltpu.make_async_copy(src, (q_hbm, k_hbm, v_hbm, mix_hbm, hat_hbm, two_hbm, inv_hbm)[n], xsem.at[n])

    gather = Gather(count_b, (up_in, down_in), (up_all, down_all), (send, recv))

    def pass_on(now):
        for slot, t, n, along in GATHER_SLOTS:
            if slot == now:
                gather.level(t, n, along)

    length, width = tok_ref.shape
    window = bias.shape[0]
    pairs = width // PAIR

    @pl.when(qb == 0)
    def _():
        def weights(part):
            cols = pl.ds(part * width, width)
            return pltpu.make_async_copy(wqkv_hbm.at[:, cols], wqkv_ref.at[:, cols], qsem.at[part])

        whole_in = [pltpu.make_async_copy(src, dst, qsem.at[3 + n]) for n, (src, dst) in enumerate((
            (up_hbm, up_in.at[pl.ds(0, width)]), (tok_hbm, tok_ref), (wo_hbm, wo_ref)))]
        whole_in[0].start()
        whole_in[1].start()
        for part in range(3):
            weights(part).start()
        whole_in[2].start()
        up_in[width:] = jnp.broadcast_to(ub_ref[...].astype(F32), (BIAS_ROWS, ub_ref.shape[1])).astype(BF16)
        gather.greet()
        whole_in[0].wait()
        gather.open(0)
        gather.open(1)
        tile = 256
        whole_in[1].wait()
        for part, ref in enumerate((q_out, k_out, v_out)):
            weights(part).wait()
            for j in range(width // tile):
                x = dot(tok_ref[...], wqkv_ref[:, part * width + j * tile:part * width + (j + 1) * tile]).astype(BF16)
                if part == 0:
                    x = x * jnp.asarray(HEAD_DIM ** -0.5, BF16)
                ref[:, j * tile:(j + 1) * tile] = x
                if (part, j) == QKV_SLOT:
                    pass_on(16)
            copy_out(part).start()
        whole_in[2].wait()
        big = eye(256)
        for j in range(width // 256):
            cols = slice(j * 256, (j + 1) * 256)
            vt[cols, :] = dot_t(big, v_out[:, cols]).astype(BF16)
            pvt[cols, :] = dot_t(big, pv_ref[:, cols]).astype(BF16)
        pass_on(0)
        ident = eye(QB)
        seg = jnp.broadcast_to(seg_ref[...].astype(F32), (QB, length)).astype(BF16)
        for j in range(length // QB):
            segc[j * QB:(j + 1) * QB, :] = dot_t(ident, seg[:, j * QB:(j + 1) * QB])

    for slot in range(1, length // QB):

        @pl.when(qb == slot)
        def _():
            pass_on(slot)

    start = pl.multiple_of(jnp.clip(qb * QB - QB, 0, length - window), QB)
    win = pl.ds(start, window)
    rows = pl.ds(pl.multiple_of(qb * QB, QB), QB)
    segq = seg_ref[:, rows].astype(F32)
    bias[...] = jnp.where(segc[win, :] == segq, 0.0, MASK_FILL)

    def score(pair):
        cols = slice(pair * PAIR, (pair + 1) * PAIR)
        keys = jnp.concatenate([k_out[win, cols], pk_ref[:, cols]], axis=0)
        sbuf[pair % 2] = dot_t(keys, split_heads(q_out[rows, cols]))

    def soft(pair):
        both = jnp.concatenate([bias[...], bias[...]], axis=1)
        sw = sbuf[pair % 2, :window] + both
        sp = sbuf[pair % 2, window:]
        top = jnp.maximum(jnp.max(sw, 0, keepdims=True), jnp.max(sp, 0, keepdims=True))
        ew = jnp.exp(sw - top)
        ep = jnp.exp(sp - top)
        inv = 1.0 / (jnp.sum(ew, 0, keepdims=True) + jnp.sum(ep, 0, keepdims=True))
        p_out[0, pair, :window] = (ew * inv).astype(BF16)
        p_out[0, pair, window:] = (ep * inv).astype(BF16)

    def mixing(pair):
        cols = slice(pair * PAIR, (pair + 1) * PAIR)
        vals = jnp.concatenate([vt[cols, win], pvt[cols, :]], axis=1)
        mixt[cols, rows] = own_blocks(dot(vals, p_out[0, pair])).astype(BF16)

    for i in range(pairs + 2):
        if i < pairs:
            score(i)
        if 0 <= i - 1 < pairs:
            soft(i - 1)
        if 0 <= i - 2 < pairs:
            mixing(i - 2)

    @pl.when(qb == pl.num_programs(0) - 1)
    def _():
        pass_on(8)
        big = eye(256)
        for r in range(length // 256):
            rr = slice(r * 256, (r + 1) * 256)
            mix_out[rr] = dot_t(big, mixt[:, rr]).astype(BF16)
        copy_out(3).start()
        for r in range(length // 256):
            rr = slice(r * 256, (r + 1) * 256)
            res = tok_ref[rr].astype(F32) + dot(mix_out[rr], wo_ref[...]) + bo_ref[...]
            hat, inv = normalize(res)
            hat_v[rr] = hat
            inv_v[rr] = jnp.broadcast_to(inv, (256, 128))
            first = hat * g1_ref[...] + s1_ref[...]
            low[rr] = first.astype(BF16)
            two[rr] = first + db_ref[...]
        copy_out(4).start()
        copy_out(6).start()
        pass_on(9)

        chips = LINE * count_b
        ffl = down_in.shape[0]
        per = length // 256

        def loads(o):
            chip = gather.chip(o)
            out = []
            for c in range(2):
                core = gather.core if c else 1 - gather.core
                cols = pl.ds(pl.multiple_of(core * ffl, 128), ffl)
                own = isinstance(o, int) and o == 0 and c == 1
                for t, to in ((0, up_v.at[o % 3, :, cols]), (1, down_v.at[o % 3, cols])):
                    src = (up_in, down_in)[t] if own else (up_all, down_all)[t].at[2 * chip + core]
                    out.append(pltpu.make_async_copy(src, to, wsem.at[o % 3, t, c]))
            return out

        def load(o):
            for copy in loads(o):
                copy.start()

        def loaded(o):
            for copy in loads(o):
                copy.wait()

        def rows_of(b):
            return slice(b * 256, (b + 1) * 256)

        def up(o, b):
            pre[b % 2] = dot(low[rows_of(b)], up_v[o % 3, :width, :])

        def act(o, b):
            u = pre[b % 2] + up_v[o % 3, width:width + 1, :].astype(F32)
            half = 0.5 * lax.erf(u * ROOT_HALF) + 0.5
            hid[b % 2] = (u * half).astype(BF16)
            slope[o, rows_of(b)] = (half + u * (jnp.exp(-0.5 * u * u) * INV_ROOT_TWOPI)).astype(BF16)

        def down(o, b):
            two[rows_of(b)] += dot(hid[b % 2], down_v[o % 3])

        def earlier(o, b, n):
            return (o, b - n) if b >= n else (o - 1, b - n + per)

        def chip_steps(o, ahead):
            loaded(o)
            ahead()
            for b in range(per):
                up(o, b)
                if b >= 1 or not (isinstance(o, int) and o == 0):
                    act(*earlier(o, b, 1))
                if b >= 2 or not (isinstance(o, int) and o == 0):
                    down(*earlier(o, b, 2))

        def keep(o):
            return pltpu.make_async_copy(slope.at[o], slope_out.at[gather.chip(o)], osem.at[o])

        def more():
            pass_on(10)
            for n in range(2):
                for along in (True, False):
                    gather.from_core(n, along)

        for t in range(2):
            gather.arrive(t, ("core", 0, 0, None))
        load(0)

        def first_ahead():
            more()
            load(1)

        chip_steps(0, first_ahead)
        others = count_b - 1
        needs = ((others, 11, 2, (True, False)), (2 * others, 12, 3, (True,)), (2 * others + 1, 13, 3, (False,)),
                 (2 * others + 2, 14, 4, (True,)), (2 * others + 3, 15, 4, (False,)))

        def chip_step(o, carry):
            def ahead():
                for at, slot, n, kinds in needs:

                    @pl.when(o == at)
                    def _():
                        pass_on(slot)
                        for along in kinds:
                            gather.from_core(n, along)

                @pl.when(o < chips - 1)
                def _():
                    load(o + 1)

            chip_steps(o, ahead)
            keep(o - 1).start()
            return carry

        lax.fori_loop(1, chips, chip_step, 0)
        def rows_out(b):
            return pltpu.make_async_copy(two.at[rows_of(b)], two_hbm.at[rows_of(b)], tsem.at[b])

        for b in range(per - 2):
            rows_out(b).start()
        act(chips - 1, per - 1)
        down(chips - 1, per - 2)
        rows_out(per - 2).start()
        down(chips - 1, per - 1)
        rows_out(per - 1).start()
        keep(chips - 1).start()
        for t in range(2):
            gather.close(t)
        for o in range(chips):
            keep(o).wait()
        for n in (0, 1, 2, 3, 4, 6):
            copy_out(n).wait()
        for b in range(per):
            rows_out(b).wait()


def attend_forward(tok, wqkv, wo, up, down, seg, pk, pv, bo, g1, s1, db, ub, group):
    length, width = tok.shape
    pre = pk.shape[0]
    window = 3 * QB
    pairs, blocks = width // PAIR, length // QB
    hbm = pl.BlockSpec(memory_space=pl.ANY)
    square, wide = jax.ShapeDtypeStruct((length, width), BF16), jax.ShapeDtypeStruct((length, width), F32)
    outs = [(hbm, square)] * 4 + [
        (pl.BlockSpec((1, pairs, window + pre, 2 * QB), lambda i: (i, 0, 0, 0)),
         jax.ShapeDtypeStruct((blocks, pairs, window + pre, 2 * QB), BF16)),
        (hbm, wide), (hbm, wide)]
    up_shape = (width + BIAS_ROWS, up.shape[1])
    outs += [(hbm, jax.ShapeDtypeStruct((group,) + shape, BF16)) for shape in (up_shape, down.shape)]
    chips, part = group // 2, 2 * down.shape[0]
    outs += [(hbm, jax.ShapeDtypeStruct((chips, length, part), BF16)), (hbm, jax.ShapeDtypeStruct((length, 128), F32))]
    count_b = group // (2 * LINE)
    pieces = len(gather_keys(count_b))
    return pl.pallas_call(
        functools.partial(forward_kernel, count_b),
        grid=(blocks,),
        in_specs=[hbm] * 5 + [whole(a) for a in (seg, pk, pv, bo, g1, s1, db, ub)],
        out_specs=[o[0] for o in outs],
        out_shape=[o[1] for o in outs],
        scratch_shapes=[pltpu.VMEM((length, width), t) for t in (BF16, BF16, BF16, BF16, F32, F32)] + [
            pltpu.VMEM((length, 128), F32),
            pltpu.VMEM((length, width), BF16),
            pltpu.VMEM((width, width), BF16),
            pltpu.VMEM(up_shape, BF16),
            pltpu.VMEM(wqkv.shape, BF16),
            pltpu.VMEM((width, length), BF16),
            pltpu.VMEM((width, pre), BF16),
            pltpu.VMEM((length, QB), F32),
            pltpu.VMEM((window, QB), F32),
            pltpu.VMEM((2, window + pre, 2 * QB), F32),
            pltpu.VMEM((width, length), BF16),
            pltpu.VMEM((length, width), BF16),
            pltpu.VMEM((3, up_shape[0], part), BF16),
            pltpu.VMEM((3, part, width), BF16),
            pltpu.VMEM((2, 256, part), F32),
            pltpu.VMEM((2, 256, part), BF16),
            pltpu.VMEM((chips, length, part), BF16),
            pltpu.SemaphoreType.DMA((2, pieces)),
            pltpu.SemaphoreType.DMA((2, pieces)),
            pltpu.SemaphoreType.DMA((3, 2, 2)),
            pltpu.SemaphoreType.DMA((6,)),
            pltpu.SemaphoreType.DMA((chips,)),
            pltpu.SemaphoreType.DMA((7,)),
            pltpu.SemaphoreType.DMA((length // 256,)),
        ],
        compiler_params=pltpu.CompilerParams(vmem_limit_bytes=VMEM_LIMIT, collective_id=0, has_side_effects=True),
        name="attend_forward",
    )(tok, wqkv, wo, up, down, seg, pk, pv, bo, g1, s1, db, ub)


def ffn_kernel(hat_ref, inv_ref, two_ref, dy_ref, slope_ref, up_hbm, down_hbm, up_own, down_own, wo_ref, g1_ref, g2_ref, s2_ref,
               out_ref, gone_ref, gmix_ref, up, down, hid, low, acc, sems):
    step = pl.program_id(0)
    width = up.shape[0]
    parts, part, _ = down_hbm.shape
    count, _, chunk = slope_ref.shape
    me = lax.axis_index("mp")

    def fetch(d, t, own):
        cols = pl.ds(d * part, part)
        up_src, down_src = (up_own, down_own) if own else (up_hbm.at[d], down_hbm.at[d])
        src, dst = ((up_src.at[pl.ds(0, width)], up.at[:, cols]), (down_src, down.at[cols]))[t]
        return pltpu.make_async_copy(src, dst, sems.at[t, d])

    @pl.when(step == 0)
    def _():
        for h in range(2):
            for t in (1, 0):
                for d in range(h * parts // 2, (h + 1) * parts // 2):

                    @pl.when(me == d)
                    def _():
                        fetch(d, t, True).start()

                    @pl.when(me != d)
                    def _():
                        fetch(d, t, False).start()

    def await_half(t, h):
        @pl.when(step == 0)
        def _():
            for d in range(h * parts // 2, (h + 1) * parts // 2):
                fetch(d, t, False).wait()

    hat2, inv2 = normalize(two_ref[...])
    out_ref[...] = (hat2 * g2_ref[...] + s2_ref[...]).astype(BF16)
    grad_two = norm_back(dy_ref[...].astype(F32), hat2, inv2, g2_ref[...])
    acc[...] = grad_two
    low[...] = grad_two.astype(BF16)

    def cols_of(j):
        return slice(j * chunk, (j + 1) * chunk)

    def back_down(j):
        gh = dot_t(low[...], down[cols_of(j)])
        hid[j % 2] = (gh * slope_ref[j].astype(F32)).astype(BF16)

    def back_up(j):
        acc[...] += dot_t(hid[j % 2], up[:, cols_of(j)])

    await_half(1, 0)
    for j in range(count + 1):
        if j == count // 2:
            await_half(1, 1)
        if j < count:
            back_down(j)
        if j in (1, count // 2 + 1):
            await_half(0, j // (count // 2 + 1))
        if j >= 1:
            back_up(j - 1)

    grad_one = norm_back(acc[...], hat_ref[...], inv_ref[:, 0:1], g1_ref[...])
    gone_ref[...] = grad_one
    gmix_ref[...] = dot_t(grad_one.astype(BF16), wo_ref[...]).astype(BF16)


def feed_forward_backward(hat, inv, two, dy, slope, up, down, up_own, down_own, wo, g1, g2, s2, tb=256):
    rows, width = hat.shape
    parts, ffl, _ = down.shape
    ff = parts * ffl
    chips, _, part = slope.shape
    block = pl.BlockSpec((tb, width), lambda i: (i, 0))
    hbm = pl.BlockSpec(memory_space=pl.ANY)
    return pl.pallas_call(
        ffn_kernel,
        grid=(rows // tb,),
        in_specs=[block, pl.BlockSpec((tb, 128), lambda i: (i, 0))] + [block] * 2 + [pl.BlockSpec((chips, tb, part), lambda i: (0, i, 0))] + [hbm] * 4
        + [whole(a) for a in (wo, g1, g2, s2)],
        out_specs=[block] * 3,
        out_shape=[jax.ShapeDtypeStruct((rows, width), t) for t in (BF16, F32, BF16)],
        scratch_shapes=[
            pltpu.VMEM((width, ff), BF16),
            pltpu.VMEM((ff, width), BF16),
            pltpu.VMEM((2, tb, part), BF16),
            pltpu.VMEM((tb, width), BF16),
            pltpu.VMEM((tb, width), F32),
            pltpu.SemaphoreType.DMA((2, parts)),
        ],
        compiler_params=pltpu.CompilerParams(vmem_limit_bytes=VMEM_LIMIT),
        name="feed_forward_backward",
    )(hat, inv, two, dy, slope, up, down, up_own, down_own, wo, g1, g2, s2)


class Total:
    def __init__(self, count_dp, count_mp, low, slots, parts, result, sems):
        self.low, self.slots, self.parts, self.result = low, slots, parts, result
        self.sems = sems
        self.count_b = count_mp // (2 * LINE)
        self.high_b, self.high_dp = self.count_b // 2, count_dp // 2
        self.count_q = LINE * self.high_b * self.high_dp
        dp, mp = lax.axis_index("dp"), lax.axis_index("mp")
        b = (mp // 2) % self.count_b
        a = mp // (2 * self.count_b)
        self.g = ((dp % 2) * 2 + b % 2) * 2 + mp % 2
        self.q = (a * self.high_b + b // 2) * self.high_dp + dp // 2

    def device(self, g, q):
        a, high = q // (self.high_b * self.high_dp), q % (self.high_b * self.high_dp)
        dp = (high % self.high_dp) * 2 + g // 4
        b = (high // self.high_dp) * 2 + (g // 2) % 2
        return dp, (a * self.count_b + b) * 2 + g % 2

    def near(self, j):
        return self.device((self.g + j) % 8, self.q)

    def far(self, i):
        return self.device(self.g, (self.q + i) % self.count_q)

    def copy(self, phase, j, arriving=False):
        if phase == 0:
            src, dst, to = self.low.at[(self.g + j) % 8], self.slots.at[j], self.near(j)
        elif phase == 1:
            at = (self.q + self.count_q - j) % self.count_q if arriving else self.q
            src, dst, to = self.parts.at[at], self.parts.at[at], self.far(j)
        else:
            at = (self.g + 8 - j) % 8 if arriving else self.g
            src, dst, to = self.result.at[at], self.result.at[at], self.near(j)
        send, recv = self.sems[phase]
        return pltpu.make_async_remote_copy(
            src_ref=src, dst_ref=dst, send_sem=send.at[j], recv_sem=recv.at[j], device_id=to,
            device_id_type=pl.DeviceIdType.MESH)

    def peers(self, phase):
        return range(1, self.count_q if phase == 1 else 8)

    def partners(self):
        return [self.near(j) for j in self.peers(0)] + [self.far(i) for i in self.peers(1)]

    def greet(self):
        barrier = pltpu.get_barrier_semaphore()
        for device in self.partners():
            pl.semaphore_signal(barrier, inc=1, device_id=device, device_id_type=pl.DeviceIdType.MESH)

    def start(self, phase):
        for j in self.peers(phase):
            self.copy(phase, j).start()

    def arrive(self, phase):
        for j in self.peers(phase):
            self.copy(phase, j, True).wait_recv()

    def first(self):
        pl.semaphore_wait(pltpu.get_barrier_semaphore(), len(self.partners()))
        self.start(0)

    def second(self):
        self.arrive(0)
        total = self.low[self.g].astype(F32)
        for j in self.peers(0):
            total = total + self.slots[j].astype(F32)
        self.parts[self.q] = total.astype(BF16)
        self.start(1)

    def third(self):
        self.arrive(1)
        total = self.parts[0].astype(F32)
        for i in range(1, self.count_q):
            total = total + self.parts[i].astype(F32)
        self.result[self.g] = total.astype(BF16)
        self.start(2)

    def last(self):
        self.arrive(2)
        for phase in range(3):
            for j in self.peers(phase):
                self.copy(phase, j).wait_send()


def backward_kernel(counts, p_ref, q_ref, k_ref, v_ref, mix_ref, do_ref, pk_ref, pv_ref, w_hbm, gone_hbm,
                    out_ref, gk_ref, gv_ref, w_ref, gone_ref, kt, dk, dv, gj, delta, gbuf, ds_all, dqt, low, slots, parts, result,
                    send0, recv0, send1, recv1, send2, recv2, late):
    pair = pl.program_id(0)
    loads = [pltpu.make_async_copy(w_hbm, w_ref, late.at[0]), pltpu.make_async_copy(gone_hbm, gone_ref, late.at[1])]

    total = Total(*counts, low, slots, parts, result, ((send0, recv0), (send1, recv1), (send2, recv2)))

    @pl.when(pair == 0)
    def _():
        total.greet()
        for copy in loads:
            copy.start()

    length = q_ref.shape[0]
    pre = pk_ref.shape[0]
    pairs, width = ds_all.shape[0], out_ref.shape[1]
    blocks = length // QB
    depth = p_ref.shape[2]
    window = depth - pre
    ident = eye(QB)
    sub = lax.broadcasted_iota(jnp.int32, (8, PAIR), 0)
    lane = lax.broadcasted_iota(jnp.int32, (8, PAIR), 1)
    pick = jnp.where((sub == 0) == (lane < HEAD_DIM), 1.0, 0.0).astype(BF16)
    dk[...] = jnp.zeros_like(dk)
    dv[...] = jnp.zeros_like(dv)
    kt[pair, :, :length] = dot_t(ident, k_ref[...]).astype(BF16)
    kt[pair, :, length:] = dot_t(ident, pk_ref[...]).astype(BF16)
    prod = do_ref[...].astype(F32) * mix_ref[...].astype(F32)
    high = prod.astype(BF16)
    rest = (prod - high.astype(F32)).astype(BF16)
    delta[...] = dot_t(pick, high) + dot_t(pick, rest)

    def where_of(qb):
        start = min(max(qb * QB - QB, 0), length - window)
        return slice(start, start + window), slice(qb * QB, (qb + 1) * QB)

    def grad_probs(qb):
        win, rows = where_of(qb)
        vals = jnp.concatenate([v_ref[win], pv_ref[...]], axis=0)
        gbuf[qb % 2] = dot_t(vals, split_heads(do_ref[rows]))

    def grad_scores(qb):
        win, rows = where_of(qb)
        d = jnp.concatenate([delta[0:1, rows], delta[1:2, rows]], axis=1)
        ds_all[pair, qb] = (p_ref[qb, 0].astype(F32) * (gbuf[qb % 2] - d)).astype(BF16)

    def grads(qb):
        win, rows = where_of(qb)
        dva = dot(p_ref[qb, 0], split_heads(do_ref[rows]))
        dv[win] += dva[:window]
        dv[length:] += dva[window:]
        dka = dot(ds_all[pair, qb], split_heads(q_ref[rows]))
        dk[win] += dka[:window]
        dk[length:] += dka[window:]

    for i in range(blocks + 2):
        if i < blocks:
            grad_probs(i)
        if 0 <= i - 1 < blocks:
            grad_scores(i - 1)
        if 0 <= i - 2 < blocks:
            grads(i - 2)
    gj[pair, :, 0:PAIR] = dk[:length].astype(BF16)
    gj[pair, :, PAIR:] = dv[:length].astype(BF16)
    cols = pl.ds(pl.multiple_of(pair * PAIR, PAIR), PAIR)
    each = 2 * pre // 8
    for part, ref in enumerate((dk, dv)):
        for i in range(4):
            low[part * 4 + i, :, cols] = ref[length + i * each:length + (i + 1) * each].astype(BF16)

    @pl.when(pair == pl.num_programs(0) - 1)
    def _():
        total.first()

        def query_grads(i, carry):
            rows_of = pl.ds(pl.multiple_of(i * PAIR, PAIR), PAIR)
            for qb in range(blocks):
                win, rows = where_of(qb)
                keys = jnp.concatenate([kt[i, :, win], kt[i, :, length:]], axis=1)
                dqt[rows_of, rows] = own_blocks(dot(keys, ds_all[i, qb]) * HEAD_DIM ** -0.5).astype(BF16)
            return carry

        lax.fori_loop(0, pairs // 2, query_grads, 0)
        total.second()
        lax.fori_loop(pairs // 2, pairs, query_grads, 0)
        total.third()
        for copy in loads:
            copy.wait()
        big = eye(256)
        for r in range(length // 256):
            rr = slice(r * 256, (r + 1) * 256)
            acc = gone_ref[rr] + dot_t(dot_t(big, dqt[:, rr]).astype(BF16), w_ref[:, :width])
            for part in range(2):
                x = jnp.concatenate([gj[i, rr, part * PAIR:(part + 1) * PAIR] for i in range(pairs)], axis=1)
                acc = acc + dot_t(x, w_ref[:, (part + 1) * width:(part + 2) * width])
            out_ref[rr] = acc.astype(BF16)
        total.last()
        for i in range(4):
            gk_ref[i * each:(i + 1) * each] = result[i].astype(F32)
            gv_ref[i * each:(i + 1) * each] = result[4 + i].astype(F32)


def attend_backward(p, q, k, v, mix, do, pk, pv, wqkv, gone, counts):
    length, width = q.shape
    pre = pk.shape[0]
    blocks, pairs, depth, _ = p.shape

    def col(a):
        return pl.BlockSpec((a.shape[0], PAIR), lambda i: (0, i))

    vmem = pl.BlockSpec(memory_space=pltpu.VMEM)
    outs = [(vmem, jax.ShapeDtypeStruct((length, width), BF16))] + [(vmem, jax.ShapeDtypeStruct((pre, width), F32))] * 2
    count_q = counts[0] * counts[1] // 8
    piece = (2 * pre // 8, width)
    return pl.pallas_call(
        functools.partial(backward_kernel, counts),
        grid=(pairs,),
        in_specs=[pl.BlockSpec((blocks, 1, depth, 2 * QB), lambda i: (0, i, 0, 0))]
        + [col(a) for a in (q, k, v, mix, do, pk, pv)] + [pl.BlockSpec(memory_space=pl.ANY)] * 2,
        out_specs=[o[0] for o in outs],
        out_shape=[o[1] for o in outs],
        scratch_shapes=[
            pltpu.VMEM(wqkv.shape, BF16),
            pltpu.VMEM((length, width), F32),
            pltpu.VMEM((pairs, PAIR, length + pre), BF16),
            pltpu.VMEM((length + pre, PAIR), F32),
            pltpu.VMEM((length + pre, PAIR), F32),
            pltpu.VMEM((pairs, length, 2 * PAIR), BF16),
            pltpu.VMEM((8, length), F32),
            pltpu.VMEM((2, depth, 2 * QB), F32),
            pltpu.VMEM((pairs, blocks, depth, 2 * QB), BF16),
            pltpu.VMEM((width, length), BF16),
            pltpu.VMEM((8,) + piece, BF16),
            pltpu.VMEM((8,) + piece, BF16),
            pltpu.VMEM((count_q,) + piece, BF16),
            pltpu.VMEM((8,) + piece, BF16),
        ] + [pltpu.SemaphoreType.DMA((n,)) for n in (8, 8, count_q, count_q, 8, 8, 2)],
        compiler_params=pltpu.CompilerParams(vmem_limit_bytes=BACKWARD_LIMIT, collective_id=1, has_side_effects=True),
        name="attend_backward",
    )(p, q, k, v, mix, do, pk, pv, wqkv, gone)


def hand_over_kernel(*refs):
    n = len(refs) // 2
    for src, dst in zip(refs[:n], refs[n:]):
        dst[...] = src[...]


def hand_over(*arrays):
    steps = 4
    specs = [pl.BlockSpec((a.shape[0] // steps, a.shape[1]), lambda i: (i, 0)) for a in arrays]
    return pl.pallas_call(
        hand_over_kernel,
        grid=(steps,),
        in_specs=specs,
        out_specs=specs,
        out_shape=[jax.ShapeDtypeStruct(a.shape, a.dtype) for a in arrays],
        name="hand_over",
    )(*arrays)


def on_device(counts, tokens, segment_ids, qkv_weight, prefix_keys, prefix_values, out_weight, out_bias, norm1_gain,
              norm1_shift, up_weight, up_bias, down_weight, down_bias, norm2_gain, norm2_shift, out_grad):
    row = lambda a: a.reshape(1, -1)
    q, k, v, mix, probs, hat, two, up_all, down_all, slope, inv = attend_forward(
        tokens[0], qkv_weight, out_weight, up_weight, down_weight, segment_ids, prefix_keys, prefix_values, row(out_bias),
        row(norm1_gain), row(norm1_shift), row(down_bias), row(up_bias), counts[1])
    out, grad_one, grad_mixed = feed_forward_backward(
        hat, inv, two, out_grad[0], slope, up_all, down_all, up_weight, down_weight, out_weight, row(norm1_gain), row(norm2_gain),
        row(norm2_shift))
    grad_tokens, total_k, total_v = hand_over(*attend_backward(
        probs, q, k, v, mix, grad_mixed, prefix_keys, prefix_values, qkv_weight, grad_one, counts))
    return out[None], grad_tokens[None], total_k, total_v


def solution(mesh):
    rows = P(("dp", "mp"), None, None)
    return jax.shard_map(
        functools.partial(on_device, (mesh.shape["dp"], mesh.shape["mp"])),
        mesh=mesh,
        in_specs=(rows, P(("dp", "mp"), None), P(), P(), P(), P(), P(), P(), P(), P(None, "mp"), P("mp"), P("mp", None),
                  P(), P(), P(), rows),
        out_specs=(rows, rows, P(), P()),
        check_vma=False,
    )
```
